32 devices in a mesh: parts: 2 (over y), row: 8 (over z, core), col: 2 (over x), ch: 1.
Axes of the slice: x: 2, y: 2, z: 4, core: 2. Of those that a mesh axis runs over, the one named last changes fastest.
Arguments:
- z_trunk: bfloat16 [128, 64, 128], P(('parts', 'row'), ('col', 'ch')), parts along dimension 0, may hold values from -6 to 6
- single: bfloat16 [128, 384], P('parts'), parts along dimension 0, may hold values from -6 to 6
- atom_coords: float32 [3, 512], P(None, ('parts', 'row', 'col', 'ch')), parts along dimension 1, may hold values from -48 to 48
- atom_single: bfloat16 [512, 128], P(('parts', 'row', 'col', 'ch')), parts along dimension 0, may hold values from -6 to 6
- rep_atom: int32 [128], P('parts'), parts along dimension 0, may hold values from 0 to 255
- atom_token: int32 [512], P(('parts', 'row', 'col', 'ch')), parts along dimension 0, may hold values from 0 to 63
- token_mask: int32 [128], P('parts'), parts along dimension 0, may hold values from 0 to 1, as said below
- chain_id: int32 [128], P('parts'), parts along dimension 0, may hold values from 0 to 5, never falling along the last dimension, each value on 1 to 32 neighbouring positions
- w_left: bfloat16 [384, 128], replicated, may hold values from -0.3125 to 0.3125
- w_right: bfloat16 [384, 128], replicated, may hold values from -0.3125 to 0.3125
- w_dist: bfloat16 [39, 128], replicated, may hold values from -4 to 4
- tri_in: bfloat16 [128, 640], replicated, may hold values from -0.5 to 0.5
- tri_out: bfloat16 [128, 128], replicated, may hold values from -0.5 to 0.5
- pae_w: bfloat16 [128, 64], replicated, may hold values from -30 to 30
- pool_w: bfloat16 [128, 384], replicated, may hold values from -0.5 to 0.5
- plddt_w: bfloat16 [384, 50], replicated, may hold values from -30 to 30
- atom_w: bfloat16 [128, 50], replicated, may hold values from -0.5 to 0.5
Outputs:
- aligned_error: float32 [128, 64], P(('parts', 'row'), ('col', 'ch')), parts along dimension 0
- interface_score: float32 [128], P(('parts', 'row')), parts along dimension 0
- atom_confidence: float32 [512], P(('parts', 'row', 'col', 'ch')), parts along dimension 0
The draws below stay inside these ranges and needn't reach their ends.
There are 2 independent parts, one for each index of `parts`. The reference program is written for one: setup_inputs(seed, part) draws one part's arguments, and reference() takes and returns one part's arrays. A program takes and returns all parts, laid end to end along the dimension named above; an argument that names none is the same for every part. Nothing has to cross between parts.
Inputs may be any that keep to these rules, and one draw needn't show every extreme that they name: `token_mask`: the real tokens form a prefix of 32 tokens or more. `chain_id`: never falls from one token to the next.
All inputs are finite; a program needn't handle non-finite values.
Results may differ from the reference program's by a relative error of at most 0.013.
Values may be sent and summed in bfloat16 or wider, within the bound.
No kernel may reach another device: no remote copies, remote signals or barrier semaphores. Data moves between devices by JAX's collectives and lax.ppermute only.
A program may use at most 64 MiB of HBM per device.

```python
import math
import jax
import jax.numpy as jnp
import numpy as np
from jax import lax

CZ = 128
CS = 384
CA = 128
DBINS = 39
BINS_PAE = 64
BINS_PL = 50
CHAINS = 6
N = 64
ATOMS = 256


def drawn_weights(key, row_count, col_count):
    return jax.random.normal(jax.random.fold_in(key, 11), (row_count, col_count), jnp.float32) / math.sqrt(row_count)


def draw_pae_w(key, part):
    weights = drawn_weights(key, CZ, BINS_PAE)
    return jnp.clip(weights, -30.0, 30.0).astype(jnp.bfloat16)


def draw_plddt_w(key, part):
    weights = drawn_weights(key, CS, BINS_PL)
    return jnp.clip(weights, -30.0, 30.0).astype(jnp.bfloat16)


def draw_token_mask(key, part):
    valid_count = jax.random.randint(jax.random.fold_in(key, 21), (), N // 2, N + 1)
    return (jnp.arange(N) < valid_count).astype(jnp.int32)


def with_ends(drawn, rng, smallest, largest):
    extent = drawn.shape
    index_at = [jax.random.randint(jax.random.fold_in(rng, axis), (), 0, extent[axis]) for axis in range(len(extent))]
    drawn = drawn.at[tuple(index_at)].set(smallest)
    longest = extent.index(max(extent))
    index_at[longest] = (index_at[longest] + 1) % extent[longest]
    return drawn.at[tuple(index_at)].set(largest)


def block_levels(key, dims, split, low, high):
    loudness, own = 1.0, jax.random.fold_in(key, 6)
    for dim, parts in split:
        heights = jnp.exp(jax.random.uniform(jax.random.fold_in(own, dim), (parts,), jnp.float32, low / len(split), high / len(split)))
        loudness = loudness * jnp.repeat(heights, dims[dim] // parts).reshape([-1 if axis == dim else 1 for axis in range(len(dims))])
    return loudness


def length_profile(number_of, total, most, lean):
    weights = [(1 << 20) // math.isqrt(standing ** lean) + 1 for standing in range(2, number_of + 1)]
    rest, given = total - most - (number_of - 1), [1] * (number_of - 1)
    while rest > 0:
        candidates = [i for i in range(number_of - 1) if given[i] < most]
        mass, left = sum([weights[i] for i in candidates]), rest
        for i in candidates:
            extra = min(most - given[i], max(1, left * weights[i] // mass), rest)
            given[i] = given[i] + extra
            rest = rest - extra
    return np.array([most] + given)


def uneven(rng, count, total, bound, slope):
    if count == 2:
        one = jax.random.randint(rng, (), max(1, total - bound), min(bound, total - 1) + 1)
        return jnp.stack([one, total - one])
    lengths = jnp.asarray(length_profile(count, total, bound, slope), jnp.int32)
    couples = (count - 1) // 2
    source_of, sink = lengths[1:1 + 2 * couples:2], lengths[2:2 + 2 * couples:2]
    room = jnp.minimum(source_of - 1, bound - sink)
    shifted = jax.random.randint(jax.random.fold_in(rng, 1), (couples,), 0, 1 << 20) % (room + 1)
    lengths = lengths.at[1:1 + 2 * couples:2].set(source_of - shifted).at[2:2 + 2 * couples:2].set(sink + shifted)
    return lengths[jax.random.permutation(jax.random.fold_in(rng, 2), count)]


def gaussian(own_key, dims, scale, bound, pieces=(), held_as=jnp.bfloat16):
    loudness = block_levels(own_key, dims, pieces, -0.22, 0.18) if pieces else 1.0
    array = jax.random.normal(own_key, dims, jnp.float32) * scale * loudness
    return jnp.minimum(jnp.maximum(array, -bound), bound).astype(held_as)


def setup_inputs(seed: int = 0, part: int = 0) -> dict:
    seeds = jax.random.split(jax.random.key(seed), 18)
    part_keys = jax.random.split(jax.random.fold_in(seeds[17], part), 18)
    z_trunk = gaussian(part_keys[0], (N, N, CZ), 1.0, 6.0, ((0, 8), (1, 2)))
    single = gaussian(part_keys[1], (N, CS), 1.0, 6.0)
    atom_coords = gaussian(part_keys[2], (3, ATOMS), 8.0, 48.0, ((1, 16),), jnp.float32)
    atom_single = gaussian(part_keys[3], (ATOMS, CA), 1.0, 6.0, ((0, 16),))
    rep_atom = with_ends(jax.random.randint(part_keys[4], (N,), 0, ATOMS), jax.random.fold_in(part_keys[4], 1), 0, ATOMS - 1).astype(jnp.int32)
    atom_token = with_ends(jax.random.randint(part_keys[5], (ATOMS,), 0, N), jax.random.fold_in(part_keys[5], 1), 0, N - 1).astype(jnp.int32)
    token_mask = draw_token_mask(jax.random.fold_in(jax.random.fold_in(seeds[17], part), 71), part)
    chain_id = jnp.searchsorted(jnp.cumsum(uneven(part_keys[7], CHAINS, N, N // 2, 2)), jnp.arange(N), side="right").astype(jnp.int32)
    w_left = gaussian(seeds[8], (CS, CZ), CS ** -0.5, 0.3125)
    w_right = gaussian(seeds[9], (CS, CZ), CS ** -0.5, 0.3125)
    w_dist = gaussian(seeds[10], (DBINS, CZ), 2 ** -0.5, 4.0)
    tri_in = gaussian(seeds[11], (CZ, 5 * CZ), CZ ** -0.5, 0.5)
    tri_out = gaussian(seeds[12], (CZ, CZ), CZ ** -0.5, 0.5)
    pae_w = draw_pae_w(jax.random.fold_in(seeds[17], 71), part)
    pool_w = gaussian(seeds[14], (CZ, CS), CZ ** -0.5, 0.5)
    plddt_w = draw_plddt_w(jax.random.fold_in(seeds[17], 71), part)
    atom_w = gaussian(seeds[16], (CA, BINS_PL), CA ** -0.5, 0.5)
    return {"z_trunk": z_trunk, "single": single, "atom_coords": atom_coords, "atom_single": atom_single, "rep_atom": rep_atom, "atom_token": atom_token, "token_mask": token_mask, "chain_id": chain_id, "w_left": w_left, "w_right": w_right, "w_dist": w_dist, "tri_in": tri_in, "tri_out": tri_out, "pae_w": pae_w, "pool_w": pool_w, "plddt_w": plddt_w, "atom_w": atom_w}


EPSILON = 1e-05

def layer_norm(values):
    center = values - lax.optimization_barrier(jnp.mean(values, axis=-1, keepdims=True))
    spread = lax.optimization_barrier(jnp.mean(center * center, axis=-1, keepdims=True))
    return center * lax.rsqrt(spread + EPSILON)

def distance_basis(distance, count):
    step_size = 18.0 / (count - 1)
    centers = 3.375 + step_size * jnp.arange(count, dtype=jnp.float32)
    scaled = (distance[..., None] - centers) / step_size
    return jnp.exp(-scaled * scaled)

def bin_average(logits, centers):
    probability = jax.nn.softmax(logits, axis=-1)
    return lax.optimization_barrier(jnp.sum(probability * centers, axis=-1))

def reference(z_trunk, single, atom_coords, atom_single, rep_atom, atom_token, token_mask, chain_id, w_left, w_right, w_dist, tri_in, tri_out, pae_w, pool_w, plddt_w, atom_w):
    coords = jnp.take(atom_coords, rep_atom, axis=1)
    offset = coords[:, :, None] - coords[:, None, :]
    distance = jnp.sqrt(lax.optimization_barrier(jnp.sum(offset * offset, axis=0)))
    radial_basis = distance_basis(distance, DBINS).astype(jnp.bfloat16)
    embedded = jnp.dot(radial_basis.reshape(-1, DBINS), w_dist, preferred_element_type=jnp.float32).reshape(N, N, CZ)
    from_rows = jnp.dot(single, w_left, preferred_element_type=jnp.float32)
    from_cols = jnp.dot(single, w_right, preferred_element_type=jnp.float32)
    pair_rep = z_trunk.astype(jnp.float32) + from_rows[:, None, :] + from_cols[None, :, :] + embedded
    mask_float = token_mask.astype(jnp.float32)
    pair_mask = mask_float[:, None] * mask_float[None, :]
    normed = layer_norm(pair_rep).astype(jnp.bfloat16)
    projected = jnp.dot(normed.reshape(-1, CZ), tri_in, preferred_element_type=jnp.float32).reshape(N, N, 5 * CZ)
    left_side = (jax.nn.sigmoid(projected[..., 0:CZ]) * projected[..., CZ:2 * CZ] * pair_mask[..., None]).astype(jnp.bfloat16)
    right_side = (jax.nn.sigmoid(projected[..., 2 * CZ:3 * CZ]) * projected[..., 3 * CZ:4 * CZ] * pair_mask[..., None]).astype(jnp.bfloat16)
    gating = jax.nn.sigmoid(projected[..., 4 * CZ:5 * CZ])
    product_sum = jnp.einsum('ikc,jkc->ijc', left_side.astype(jnp.float32), right_side.astype(jnp.float32))
    normed_outer = layer_norm(product_sum).astype(jnp.bfloat16)
    updated = pair_rep + gating * jnp.dot(normed_outer.reshape(-1, CZ), tri_out, preferred_element_type=jnp.float32).reshape(N, N, CZ)
    pae_logits = jnp.dot(updated.astype(jnp.bfloat16).reshape(-1, CZ), pae_w, preferred_element_type=jnp.float32).reshape(N, N, BINS_PAE)
    pae_centers = 0.5 * (jnp.arange(BINS_PAE, dtype=jnp.float32) + 0.5)
    probability = jax.nn.softmax(pae_logits, axis=-1)
    aligned_error = lax.optimization_barrier(jnp.sum(probability * pae_centers, axis=-1))
    tm_scale = 1.24 * (max(N, 19) - 15) ** (1.0 / 3.0) - 1.8
    tm_values = 1.0 / (1.0 + (pae_centers / tm_scale) ** 2)
    tm_pair = lax.optimization_barrier(jnp.sum(probability * tm_values, axis=-1))
    interface = pair_mask * (chain_id[:, None] != chain_id[None, :]).astype(jnp.float32)
    numerator = lax.optimization_barrier(jnp.sum(interface * tm_pair, axis=1))
    count_total = lax.optimization_barrier(jnp.sum(interface, axis=1))
    interface_score = numerator / jnp.maximum(count_total, 1.0)
    pooled = lax.optimization_barrier(jnp.sum(mask_float[None, :, None] * updated, axis=1)) / jnp.sum(mask_float)
    single_new = single.astype(jnp.float32) + jnp.dot(pooled.astype(jnp.bfloat16), pool_w, preferred_element_type=jnp.float32)
    single_norm = layer_norm(single_new).astype(jnp.bfloat16)
    token_logits = jnp.dot(single_norm, plddt_w, preferred_element_type=jnp.float32)
    atom_logits = jnp.take(token_logits, atom_token, axis=0) + jnp.dot(atom_single, atom_w, preferred_element_type=jnp.float32)
    plddt_centers = (jnp.arange(BINS_PL, dtype=jnp.float32) + 0.5) / BINS_PL
    atom_confidence = bin_average(atom_logits, plddt_centers)
    return (aligned_error, interface_score, atom_confidence)
```

```python
import jax
import jax.numpy as jnp
from jax import lax
from jax.experimental import pallas as pl
from jax.experimental.pallas import tpu as pltpu
from jax.sharding import PartitionSpec as P

EPSILON = 1e-05


def layer_norm(values):
    center = values - jnp.mean(values, axis=-1, keepdims=True)
    spread = jnp.mean(center * center, axis=-1, keepdims=True)
    return center * lax.rsqrt(spread + EPSILON)


def distance_basis(distance, count):
    step_size = 18.0 / (count - 1)
    centers = 3.375 + step_size * jnp.arange(count, dtype=jnp.float32)
    scaled = (distance[..., None] - centers) / step_size
    return jnp.exp(-scaled * scaled)


def bin_average(logits, centers):
    probability = jax.nn.softmax(logits, axis=-1)
    return jnp.sum(probability * centers, axis=-1)


def per_device(
    z_trunk,
    single,
    atom_coords,
    atom_single,
    rep_atom,
    atom_token,
    token_mask,
    chain_id,
    w_left,
    w_right,
    w_dist,
    tri_in,
    tri_out,
    pae_w,
    pool_w,
    plddt_w,
    atom_w,
):
    tile_rows, tile_cols, pair_width = z_trunk.shape
    tokens = single.shape[0]
    col_index = lax.axis_index("col") * lax.axis_size("ch") + lax.axis_index("ch")
    row_start = lax.axis_index("row") * tile_rows
    col_start = col_index * tile_cols
    wanted = jnp.concatenate(
        [
            lax.dynamic_slice_in_dim(rep_atom, row_start, tile_rows),
            lax.dynamic_slice_in_dim(rep_atom, col_start, tile_cols),
        ]
    )
    shard_piece = lax.all_gather(atom_coords, ("row", "col", "ch"), axis=1, tiled=True)
    places = lax.iota(jnp.int32, shard_piece.shape[1])
    selector = (places[:, None] == wanted[None, :]).astype(jnp.float32)
    coords = jnp.dot(
        shard_piece, selector, precision=lax.Precision.HIGHEST, preferred_element_type=jnp.float32
    )
    offset = coords[:, :tile_rows, None] - coords[:, None, tile_rows:]
    distance = jnp.sqrt(jnp.sum(offset * offset, axis=0))
    basis_count = w_dist.shape[0]
    radial_basis = distance_basis(distance, basis_count).astype(jnp.bfloat16)
    embedded = jnp.dot(
        radial_basis.reshape(-1, basis_count), w_dist, preferred_element_type=jnp.float32
    ).reshape(tile_rows, tile_cols, pair_width)
    row_single = lax.dynamic_slice_in_dim(single, row_start, tile_rows)
    col_single = lax.dynamic_slice_in_dim(single, col_start, tile_cols)
    from_rows = jnp.dot(row_single, w_left, preferred_element_type=jnp.float32)
    from_cols = jnp.dot(col_single, w_right, preferred_element_type=jnp.float32)
    pair_rep = (
        z_trunk.astype(jnp.float32) + from_rows[:, None, :] + from_cols[None, :, :] + embedded
    )
    mask_float = token_mask.astype(jnp.float32)
    row_mask = lax.dynamic_slice_in_dim(mask_float, row_start, tile_rows)
    col_mask = lax.dynamic_slice_in_dim(mask_float, col_start, tile_cols)
    pair_mask = row_mask[:, None] * col_mask[None, :]
    normed = layer_norm(pair_rep).astype(jnp.bfloat16)
    projected = jnp.dot(
        normed.reshape(-1, pair_width), tri_in, preferred_element_type=jnp.float32
    ).reshape(tile_rows, tile_cols, 5 * pair_width)
    left_side = (
        jax.nn.sigmoid(projected[..., 0:pair_width])
        * projected[..., pair_width : 2 * pair_width]
        * pair_mask[..., None]
    ).astype(jnp.bfloat16)
    right_side = (
        jax.nn.sigmoid(projected[..., 2 * pair_width : 3 * pair_width])
        * projected[..., 3 * pair_width : 4 * pair_width]
        * pair_mask[..., None]
    ).astype(jnp.bfloat16)
    gating = jax.nn.sigmoid(projected[..., 4 * pair_width : 5 * pair_width])
    partial_terms = jnp.einsum(
        "ikc,jkc->ijc",
        left_side,
        lax.all_gather(right_side, "row", axis=0, tiled=True),
        preferred_element_type=jnp.float32,
    )
    product_sum = lax.psum_scatter(partial_terms, ("col", "ch"), scatter_dimension=1, tiled=True)
    normed_outer = layer_norm(product_sum).astype(jnp.bfloat16)
    updated = pair_rep + gating * jnp.dot(
        normed_outer.reshape(-1, pair_width), tri_out, preferred_element_type=jnp.float32
    ).reshape(tile_rows, tile_cols, pair_width)
    bins_pae = pae_w.shape[1]
    pae_logits = jnp.dot(
        updated.astype(jnp.bfloat16).reshape(-1, pair_width),
        pae_w,
        preferred_element_type=jnp.float32,
    ).reshape(tile_rows, tile_cols, bins_pae)
    pae_centers = 0.5 * (jnp.arange(bins_pae, dtype=jnp.float32) + 0.5)
    probability = jax.nn.softmax(pae_logits, axis=-1)
    aligned_error = jnp.sum(probability * pae_centers, axis=-1)
    tm_scale = 1.24 * (max(tokens, 19) - 15) ** (1.0 / 3.0) - 1.8
    tm_values = 1.0 / (1.0 + (pae_centers / tm_scale) ** 2)
    tm_pair = jnp.sum(probability * tm_values, axis=-1)
    row_chain = lax.dynamic_slice_in_dim(chain_id, row_start, tile_rows)
    col_chain = lax.dynamic_slice_in_dim(chain_id, col_start, tile_cols)
    interface = pair_mask * (row_chain[:, None] != col_chain[None, :]).astype(jnp.float32)
    numerator_part = jnp.sum(interface * tm_pair, axis=1)
    count_part = jnp.sum(interface, axis=1)
    pooled_part = jnp.sum(col_mask[None, :, None] * updated, axis=1)
    numerator, count_total, pooled = lax.psum(
        (numerator_part, count_part, pooled_part), ("col", "ch")
    )
    interface_score = numerator / jnp.maximum(count_total, 1.0)
    pooled = pooled / jnp.sum(mask_float)
    single_new = row_single.astype(jnp.float32) + jnp.dot(
        pooled.astype(jnp.bfloat16), pool_w, preferred_element_type=jnp.float32
    )
    single_norm = layer_norm(single_new).astype(jnp.bfloat16)
    bins_plddt = plddt_w.shape[1]
    shard_piece = lax.all_gather(single_norm, "row", axis=0, tiled=True)
    places = lax.iota(jnp.int32, shard_piece.shape[0])
    selector = (atom_token[:, None] == places[None, :]).astype(jnp.bfloat16)
    picked = jnp.dot(selector, shard_piece, preferred_element_type=jnp.float32)
    atom_logits = jnp.dot(picked.astype(jnp.bfloat16), plddt_w, preferred_element_type=jnp.float32)
    atom_logits = atom_logits + jnp.dot(atom_single, atom_w, preferred_element_type=jnp.float32)
    plddt_centers = (jnp.arange(bins_plddt, dtype=jnp.float32) + 0.5) / bins_plddt
    atom_confidence = bin_average(atom_logits, plddt_centers)
    return (aligned_error, interface_score, atom_confidence)


WHOLE_PAIR_BYTES = 4 * 1024 * 1024
VMEM = pl.BlockSpec(memory_space=pltpu.VMEM)
SMEM = pl.BlockSpec(memory_space=pltpu.SMEM)


def sigmoid(values):
    return 1.0 / (1.0 + jnp.exp(-values))


def place_of():
    row = lax.axis_index("row")
    return lax.div(row, 2), lax.rem(row, 2), lax.axis_index("col")


def token_count(mask_ref):
    return jnp.sum(mask_ref[...].astype(jnp.float32), axis=1, keepdims=True)


def pack_kernel(z_ref, mine_ref, other_ref, out_ref):
    rows, cols, width = z_ref.shape
    atoms = mine_ref.shape[1]
    out_ref[0 : rows * cols, :] = z_ref[...].reshape(rows * cols, width)
    half = lax.rem(lax.axis_index("row"), 2)
    for place, ref in ((half, mine_ref), (1 - half, other_ref)):
        value = ref[...]
        high = value.astype(jnp.bfloat16).astype(jnp.float32)
        middle = (value - high).astype(jnp.bfloat16).astype(jnp.float32)
        low = value - high - middle
        filler = jnp.zeros((width - 9, atoms), jnp.float32)
        stacked = jnp.concatenate([high, middle, low, filler], axis=0)
        start = pl.multiple_of(rows * cols + place * atoms, 16)
        out_ref[pl.ds(start, atoms), :] = stacked.T.astype(jnp.bfloat16)


def edge_kernel(slots, col_count, *refs):
    packs = refs[: len(slots)]
    single_ref, rep_ref, mask_ref, w_left_ref, w_right_ref, w_dist_ref, tri_in_ref = refs[
        len(slots) : len(slots) + 7
    ]
    pair_ref, gating_ref, left_ref, right_ref = refs[len(slots) + 7 : len(slots) + 11]
    xyz_ref, rows_ref, cols_ref, dist_ref = refs[len(slots) + 11 :]
    _, tile_rows, _, tile_cols, width = pair_ref.shape
    tokens = single_ref.shape[0]
    pairs = tile_rows * tile_cols
    atoms = (packs[0].shape[0] - pairs) // 2
    basis_count = w_dist_ref.shape[0]
    chip, half, col = place_of()
    single = single_ref[...]
    rows_ref[...] = jnp.dot(single, w_left_ref[...], preferred_element_type=jnp.float32)
    cols_ref[...] = jnp.dot(single, w_right_ref[...], preferred_element_type=jnp.float32)
    dist_ref[...] = jnp.zeros_like(dist_ref)
    dist_ref[0:basis_count, :] = w_dist_ref[...].astype(jnp.float32)
    w_dist = dist_ref[...].astype(jnp.bfloat16)
    rep = rep_ref[...]
    order = lax.broadcasted_iota(jnp.int32, (2 * atoms, tokens), 0)
    picked = jnp.zeros((tokens, width), jnp.float32)
    for pack, (chip_step, col_step) in zip(packs, slots):
        device = 2 * (chip ^ chip_step) * col_count + (col ^ col_step)
        number = jnp.where(
            order < atoms, order + device * atoms, order - atoms + (device + col_count) * atoms
        )
        chosen = (number == rep).astype(jnp.float32).astype(jnp.bfloat16)
        picked = picked + lax.dot_general(
            chosen, pack[pairs:, :], (((0,), (0,)), ((), ())), preferred_element_type=jnp.float32
        )
    for axis in range(3):
        whole = picked[:, axis : axis + 1] + picked[:, axis + 3 : axis + 4]
        whole = whole + picked[:, axis + 6 : axis + 7]
        xyz_ref[axis] = jnp.broadcast_to(whole, (tokens, width))
    count = token_count(mask_ref)
    step_size = 18.0 / (basis_count - 1)
    centers = 3.375 + step_size * lax.broadcasted_iota(jnp.int32, (1, 1, width), 2).astype(
        jnp.float32
    )
    row_order = lax.broadcasted_iota(jnp.int32, (tile_rows, tile_cols, width), 0)
    col_order = lax.broadcasted_iota(jnp.int32, (tile_rows, tile_cols, width), 1)
    limit = count.astype(jnp.int32).reshape(1, 1, 1)
    tri_in = tri_in_ref[...]
    for pack, (chip_step, col_step) in zip(packs, slots):
        at_chip = chip ^ chip_step
        at_col = col ^ col_step
        row_start = pl.multiple_of((2 * at_chip + half) * tile_rows, 8)
        col_start = pl.multiple_of(at_col * tile_cols, 8)
        row_slice = pl.ds(row_start, tile_rows)
        col_slice = pl.ds(col_start, tile_cols)
        square = jnp.zeros((tile_rows, tile_cols, width), jnp.float32)
        for axis in range(3):
            gap = xyz_ref[axis, row_slice, :][:, None, :] - xyz_ref[axis, col_slice, :][None]
            square = square + gap * gap
        scaled = (jnp.sqrt(square) - centers) * (1.0 / step_size)
        basis = jnp.exp(-scaled * scaled).astype(jnp.bfloat16)
        pair = (
            pack[0:pairs, :].astype(jnp.float32).reshape(tile_rows, tile_cols, width)
            + rows_ref[row_slice, :][:, None, :]
            + cols_ref[col_slice, :][None]
        )
        pair = pair.reshape(pairs, width) + jnp.dot(
            basis.reshape(pairs, width), w_dist, preferred_element_type=jnp.float32
        )
        tile = (tile_rows, tile_cols, width)
        pair_ref[at_chip, :, at_col] = pair.reshape(tile)
        normed = layer_norm(pair).astype(jnp.bfloat16)
        projected = jnp.dot(normed, tri_in, preferred_element_type=jnp.float32)
        real = jnp.where(
            (row_order + row_start < limit) & (col_order + col_start < limit), 1.0, 0.0
        )
        left = sigmoid(projected[:, 0:width]) * projected[:, width : 2 * width]
        left = (left.reshape(tile) * real).astype(jnp.bfloat16)
        left_ref[at_chip, :, at_col] = left.astype(jnp.float32)
        right = sigmoid(projected[:, 2 * width : 3 * width]) * projected[:, 3 * width : 4 * width]
        right = right.reshape(tile) * real
        right_ref[at_col, :, at_chip] = jnp.swapaxes(right, 0, 1).astype(jnp.bfloat16)
        gating_ref[at_chip, :, at_col] = sigmoid(projected[:, 4 * width :]).reshape(tile)


def triangle_kernel(
    tm_scale,
    left_ref,
    mine_ref,
    other_ref,
    pair_ref,
    gating_ref,
    tri_out_ref,
    pae_w_ref,
    mask_ref,
    chain_ref,
    chain_smem,
    aligned_ref,
    interface_ref,
    pooled_ref,
    right_ref,
    updated_ref,
):
    chips, tile_rows, col_count, tile_cols, width = pair_ref.shape
    tokens = col_count * tile_cols
    chip, half, col = place_of()
    shape = (tokens, chips, tile_rows, width)
    right_ref[:, :, half] = mine_ref[...].reshape(shape).astype(jnp.float32)
    right_ref[:, :, 1 - half] = other_ref[...].reshape(shape).astype(jnp.float32)
    count = token_count(mask_ref)
    token_order = lax.broadcasted_iota(jnp.int32, (tokens, width), 0)
    real = jnp.where(token_order < count.astype(jnp.int32), 1.0, 0.0)
    tri_out = tri_out_ref[...]
    block = 4
    blocks = tile_rows // block

    def rows_of(step, carry):
        at_chip = lax.div(step, blocks)
        first = lax.rem(step, blocks) * block

        def add_token(token, sums):
            key = right_ref[token].reshape(tokens, width)
            key_col = lax.div(token, tile_cols)
            key_place = lax.rem(token, tile_cols)
            return tuple(
                sums[i] + left_ref[at_chip, first + i, key_col, pl.ds(key_place, 1), :] * key
                for i in range(block)
            )

        zero = jnp.zeros((tokens, width), jnp.float32)
        sums = lax.fori_loop(0, tokens, add_token, (zero,) * block, unroll=8)
        outer = jnp.concatenate(sums, axis=0)
        change = jnp.dot(
            layer_norm(outer).astype(jnp.bfloat16), tri_out, preferred_element_type=jnp.float32
        )
        for i in range(block):
            gating = gating_ref[at_chip, first + i].reshape(tokens, width)
            updated = pair_ref[at_chip, first + i].reshape(tokens, width) + gating * (
                change[i * tokens : (i + 1) * tokens]
            )
            updated_ref[at_chip, first + i] = updated.astype(jnp.bfloat16)
            pooled_ref[pl.ds(at_chip * tile_rows + first + i, 1), :] = jnp.sum(
                updated * real, axis=0, keepdims=True
            )
        return carry

    lax.fori_loop(0, chips * blocks, rows_of, 0)
    bins = pae_w_ref.shape[1]
    logits = lax.dot_general(
        pae_w_ref[...],
        updated_ref[chip].reshape(tile_rows * tokens, width),
        (((0,), (1,)), ((), ())),
        preferred_element_type=jnp.float32,
    )
    centers = 0.5 * (lax.broadcasted_iota(jnp.int32, (bins, 1), 0).astype(jnp.float32) + 0.5)
    ratio = centers / tm_scale
    weight = jnp.exp(logits - jnp.max(logits, axis=0, keepdims=True))
    total = jnp.sum(weight, axis=0, keepdims=True)
    error = jnp.sum(weight * centers, axis=0, keepdims=True) / total
    tm_pair = jnp.sum(weight * (1.0 / (1.0 + ratio * ratio)), axis=0, keepdims=True) / total
    chains = chain_ref[...]
    keys = lax.broadcasted_iota(jnp.int32, (1, tokens), 1)
    limit = count.astype(jnp.int32)
    places = lax.broadcasted_iota(jnp.int32, (1, tile_rows), 1)
    scores = jnp.zeros((1, tile_rows), jnp.float32)
    query = (2 * chip + half) * tile_rows
    for i in range(tile_rows):
        span = error[:, i * tokens : (i + 1) * tokens]
        mine = span[:, 0:tile_cols]
        for other in range(1, col_count):
            mine = jnp.where(
                col == other, span[:, other * tile_cols : (other + 1) * tile_cols], mine
            )
        aligned_ref[i : i + 1, :] = mine
        face = (keys < limit) & (query + i < limit) & (chains != chain_smem[query + i])
        face = jnp.where(face, 1.0, 0.0)
        number = jnp.sum(face, axis=1, keepdims=True)
        score = jnp.sum(face * tm_pair[:, i * tokens : (i + 1) * tokens], axis=1, keepdims=True)
        scores = jnp.where(places == i, score / jnp.maximum(number, 1.0), scores)
    interface_ref[...] = scores


def atom_kernel(
    mine_ref,
    other_ref,
    single_ref,
    mask_ref,
    pool_w_ref,
    plddt_w_ref,
    atom_token_ref,
    atom_single_ref,
    atom_w_ref,
    out_ref,
    pooled_ref,
):
    chips, _, tile_rows, width = pooled_ref.shape
    tokens = single_ref.shape[0]
    half = lax.rem(lax.axis_index("row"), 2)
    pooled_ref[:, half] = mine_ref[...].reshape(chips, tile_rows, width)
    pooled_ref[:, 1 - half] = other_ref[...].reshape(chips, tile_rows, width)
    pooled = pooled_ref[...].reshape(tokens, width) / token_count(mask_ref)
    single_new = single_ref[...].astype(jnp.float32) + jnp.dot(
        pooled.astype(jnp.bfloat16), pool_w_ref[...], preferred_element_type=jnp.float32
    )
    single_norm = layer_norm(single_new).astype(jnp.bfloat16)
    atoms = atom_token_ref.shape[1]
    order = lax.broadcasted_iota(jnp.int32, (tokens, atoms), 0)
    chosen = (order == atom_token_ref[...]).astype(jnp.float32).astype(jnp.bfloat16)
    picked = lax.dot_general(
        chosen, single_norm, (((0,), (0,)), ((), ())), preferred_element_type=jnp.float32
    ).astype(jnp.bfloat16)
    turned = (((0,), (1,)), ((), ()))
    logits = lax.dot_general(
        plddt_w_ref[...], picked, turned, preferred_element_type=jnp.float32
    ) + lax.dot_general(
        atom_w_ref[...], atom_single_ref[...], turned, preferred_element_type=jnp.float32
    )
    bins = logits.shape[0]
    centers = (lax.broadcasted_iota(jnp.int32, (bins, 1), 0).astype(jnp.float32) + 0.5) / bins
    weight = jnp.exp(logits - jnp.max(logits, axis=0, keepdims=True))
    total = jnp.sum(weight, axis=0, keepdims=True)
    out_ref[...] = jnp.sum(weight * centers, axis=0, keepdims=True) / total


def direct(
    z_trunk,
    single,
    atom_coords,
    atom_single,
    rep_atom,
    atom_token,
    token_mask,
    chain_id,
    w_left,
    w_right,
    w_dist,
    tri_in,
    tri_out,
    pae_w,
    pool_w,
    plddt_w,
    atom_w,
):
    tile_rows, tile_cols, width = z_trunk.shape
    tokens = single.shape[0]
    if tokens * tokens * width * 4 > WHOLE_PAIR_BYTES:
        return per_device(
            z_trunk, single, atom_coords, atom_single, rep_atom, atom_token, token_mask, chain_id,
            w_left, w_right, w_dist, tri_in, tri_out, pae_w, pool_w, plddt_w, atom_w,
        )
    row_count = lax.axis_size("row")
    col_count = lax.axis_size("col")
    chips = row_count // 2
    atoms = atom_coords.shape[1]
    float32 = jnp.float32

    def across(values, axis, count, step):
        return lax.ppermute(values, axis, [(i, i ^ step) for i in range(count)])

    def partner(values):
        return across(values, "row", row_count, 1)

    packed = pl.pallas_call(
        pack_kernel,
        out_shape=jax.ShapeDtypeStruct((tile_rows * tile_cols + 2 * atoms, width), jnp.bfloat16),
        in_specs=[VMEM] * 3,
        out_specs=VMEM,
        name="pack",
    )(z_trunk, atom_coords, partner(atom_coords))
    slots = [(i, j) for i in range(chips) for j in range(col_count)]
    along = [packed] + [across(packed, "row", row_count, 2 * i) for i in range(1, chips)]
    packs = [along[i] if j == 0 else across(along[i], "col", col_count, j) for i, j in slots]
    mask_row = token_mask.reshape(1, tokens)
    tiles = jax.ShapeDtypeStruct((chips, tile_rows, col_count, tile_cols, width), float32)
    turned = jax.ShapeDtypeStruct((col_count, tile_cols, chips, tile_rows, width), jnp.bfloat16)
    pair, gating, left, right = pl.pallas_call(
        lambda *refs: edge_kernel(slots, col_count, *refs),
        out_shape=(tiles, tiles, tiles, turned),
        in_specs=[VMEM] * (len(slots) + 7),
        out_specs=(VMEM,) * 4,
        scratch_shapes=[
            pltpu.VMEM((3, tokens, width), float32),
            pltpu.VMEM((tokens, width), float32),
            pltpu.VMEM((tokens, width), float32),
            pltpu.VMEM((width, width), float32),
        ],
        name="edges",
    )(*packs, single, rep_atom.reshape(1, tokens), mask_row, w_left, w_right, w_dist, tri_in)
    tm_scale = 1.24 * (max(tokens, 19) - 15) ** (1.0 / 3.0) - 1.8
    aligned_error, interface_score, pooled = pl.pallas_call(
        lambda *refs: triangle_kernel(tm_scale, *refs),
        out_shape=(
            jax.ShapeDtypeStruct((tile_rows, tile_cols), float32),
            jax.ShapeDtypeStruct((1, tile_rows), float32),
            jax.ShapeDtypeStruct((chips * tile_rows, width), float32),
        ),
        in_specs=[VMEM] * 9 + [SMEM],
        out_specs=(VMEM,) * 3,
        scratch_shapes=[
            pltpu.VMEM((tokens, chips, 2, tile_rows, width), float32),
            pltpu.VMEM((chips, tile_rows, tokens, width), jnp.bfloat16),
        ],
        name="triangle",
    )(
        left, right, partner(right), pair, gating, tri_out, pae_w, mask_row,
        chain_id.reshape(1, tokens), chain_id,
    )
    atom_confidence = pl.pallas_call(
        atom_kernel,
        out_shape=jax.ShapeDtypeStruct((1, atoms), float32),
        in_specs=[VMEM] * 9,
        out_specs=VMEM,
        scratch_shapes=[pltpu.VMEM((chips, 2, tile_rows, width), float32)],
        name="atoms",
    )(
        pooled, partner(pooled), single, mask_row, pool_w, plddt_w,
        atom_token.reshape(1, atoms), atom_single, atom_w,
    )
    return (aligned_error, interface_score.reshape(tile_rows), atom_confidence.reshape(atoms))


def gathers_whole(mesh):
    row_count, col_count = mesh.shape["row"], mesh.shape["col"]
    power = all(count & (count - 1) == 0 for count in (row_count, col_count))
    return power and row_count > 1 and mesh.shape["ch"] == 1


def solution(mesh):
    placed = (
        P(("parts", "row"), ("col", "ch"), None),
        P("parts", None),
        P(None, ("parts", "row", "col", "ch")),
        P(("parts", "row", "col", "ch"), None),
        P("parts"),
        P(("parts", "row", "col", "ch")),
        P("parts"),
        P("parts"),
        P(),
        P(),
        P(),
        P(),
        P(),
        P(),
        P(),
        P(),
        P(),
    )
    return jax.shard_map(
        direct if gathers_whole(mesh) else per_device,
        mesh=mesh,
        in_specs=placed,
        out_specs=(
            P(("parts", "row"), ("col", "ch")),
            P(("parts", "row")),
            P(("parts", "row", "col", "ch")),
        ),
        check_vma=False,
    )
```

```python
import jax
import jax.numpy as jnp
from jax import lax
from jax.experimental import pallas as pl
from jax.experimental.pallas import tpu as pltpu
from jax.sharding import PartitionSpec as P

EPSILON = 1e-05


def layer_norm(values):
    center = values - jnp.mean(values, axis=-1, keepdims=True)
    spread = jnp.mean(center * center, axis=-1, keepdims=True)
    return center * lax.rsqrt(spread + EPSILON)


def distance_basis(distance, count):
    step_size = 18.0 / (count - 1)
    centers = 3.375 + step_size * jnp.arange(count, dtype=jnp.float32)
    scaled = (distance[..., None] - centers) / step_size
    return jnp.exp(-scaled * scaled)


def bin_average(logits, centers):
    probability = jax.nn.softmax(logits, axis=-1)
    return jnp.sum(probability * centers, axis=-1)


def per_device(
    z_trunk,
    single,
    atom_coords,
    atom_single,
    rep_atom,
    atom_token,
    token_mask,
    chain_id,
    w_left,
    w_right,
    w_dist,
    tri_in,
    tri_out,
    pae_w,
    pool_w,
    plddt_w,
    atom_w,
):
    tile_rows, tile_cols, pair_width = z_trunk.shape
    tokens = single.shape[0]
    col_index = lax.axis_index("col") * lax.axis_size("ch") + lax.axis_index("ch")
    row_start = lax.axis_index("row") * tile_rows
    col_start = col_index * tile_cols
    wanted = jnp.concatenate(
        [
            lax.dynamic_slice_in_dim(rep_atom, row_start, tile_rows),
            lax.dynamic_slice_in_dim(rep_atom, col_start, tile_cols),
        ]
    )
    shard_piece = lax.all_gather(atom_coords, ("row", "col", "ch"), axis=1, tiled=True)
    places = lax.iota(jnp.int32, shard_piece.shape[1])
    selector = (places[:, None] == wanted[None, :]).astype(jnp.float32)
    coords = jnp.dot(
        shard_piece, selector, precision=lax.Precision.HIGHEST, preferred_element_type=jnp.float32
    )
    offset = coords[:, :tile_rows, None] - coords[:, None, tile_rows:]
    distance = jnp.sqrt(jnp.sum(offset * offset, axis=0))
    basis_count = w_dist.shape[0]
    radial_basis = distance_basis(distance, basis_count).astype(jnp.bfloat16)
    embedded = jnp.dot(
        radial_basis.reshape(-1, basis_count), w_dist, preferred_element_type=jnp.float32
    ).reshape(tile_rows, tile_cols, pair_width)
    row_single = lax.dynamic_slice_in_dim(single, row_start, tile_rows)
    col_single = lax.dynamic_slice_in_dim(single, col_start, tile_cols)
    from_rows = jnp.dot(row_single, w_left, preferred_element_type=jnp.float32)
    from_cols = jnp.dot(col_single, w_right, preferred_element_type=jnp.float32)
    pair_rep = (
        z_trunk.astype(jnp.float32) + from_rows[:, None, :] + from_cols[None, :, :] + embedded
    )
    mask_float = token_mask.astype(jnp.float32)
    row_mask = lax.dynamic_slice_in_dim(mask_float, row_start, tile_rows)
    col_mask = lax.dynamic_slice_in_dim(mask_float, col_start, tile_cols)
    pair_mask = row_mask[:, None] * col_mask[None, :]
    normed = layer_norm(pair_rep).astype(jnp.bfloat16)
    projected = jnp.dot(
        normed.reshape(-1, pair_width), tri_in, preferred_element_type=jnp.float32
    ).reshape(tile_rows, tile_cols, 5 * pair_width)
    left_side = (
        jax.nn.sigmoid(projected[..., 0:pair_width])
        * projected[..., pair_width : 2 * pair_width]
        * pair_mask[..., None]
    ).astype(jnp.bfloat16)
    right_side = (
        jax.nn.sigmoid(projected[..., 2 * pair_width : 3 * pair_width])
        * projected[..., 3 * pair_width : 4 * pair_width]
        * pair_mask[..., None]
    ).astype(jnp.bfloat16)
    gating = jax.nn.sigmoid(projected[..., 4 * pair_width : 5 * pair_width])
    partial_terms = jnp.einsum(
        "ikc,jkc->ijc",
        left_side,
        lax.all_gather(right_side, "row", axis=0, tiled=True),
        preferred_element_type=jnp.float32,
    )
    product_sum = lax.psum_scatter(partial_terms, ("col", "ch"), scatter_dimension=1, tiled=True)
    normed_outer = layer_norm(product_sum).astype(jnp.bfloat16)
    updated = pair_rep + gating * jnp.dot(
        normed_outer.reshape(-1, pair_width), tri_out, preferred_element_type=jnp.float32
    ).reshape(tile_rows, tile_cols, pair_width)
    bins_pae = pae_w.shape[1]
    pae_logits = jnp.dot(
        updated.astype(jnp.bfloat16).reshape(-1, pair_width),
        pae_w,
        preferred_element_type=jnp.float32,
    ).reshape(tile_rows, tile_cols, bins_pae)
    pae_centers = 0.5 * (jnp.arange(bins_pae, dtype=jnp.float32) + 0.5)
    probability = jax.nn.softmax(pae_logits, axis=-1)
    aligned_error = jnp.sum(probability * pae_centers, axis=-1)
    tm_scale = 1.24 * (max(tokens, 19) - 15) ** (1.0 / 3.0) - 1.8
    tm_values = 1.0 / (1.0 + (pae_centers / tm_scale) ** 2)
    tm_pair = jnp.sum(probability * tm_values, axis=-1)
    row_chain = lax.dynamic_slice_in_dim(chain_id, row_start, tile_rows)
    col_chain = lax.dynamic_slice_in_dim(chain_id, col_start, tile_cols)
    interface = pair_mask * (row_chain[:, None] != col_chain[None, :]).astype(jnp.float32)
    numerator_part = jnp.sum(interface * tm_pair, axis=1)
    count_part = jnp.sum(interface, axis=1)
    pooled_part = jnp.sum(col_mask[None, :, None] * updated, axis=1)
    numerator, count_total, pooled = lax.psum(
        (numerator_part, count_part, pooled_part), ("col", "ch")
    )
    interface_score = numerator / jnp.maximum(count_total, 1.0)
    pooled = pooled / jnp.sum(mask_float)
    single_new = row_single.astype(jnp.float32) + jnp.dot(
        pooled.astype(jnp.bfloat16), pool_w, preferred_element_type=jnp.float32
    )
    single_norm = layer_norm(single_new).astype(jnp.bfloat16)
    bins_plddt = plddt_w.shape[1]
    shard_piece = lax.all_gather(single_norm, "row", axis=0, tiled=True)
    places = lax.iota(jnp.int32, shard_piece.shape[0])
    selector = (atom_token[:, None] == places[None, :]).astype(jnp.bfloat16)
    picked = jnp.dot(selector, shard_piece, preferred_element_type=jnp.float32)
    atom_logits = jnp.dot(picked.astype(jnp.bfloat16), plddt_w, preferred_element_type=jnp.float32)
    atom_logits = atom_logits + jnp.dot(atom_single, atom_w, preferred_element_type=jnp.float32)
    plddt_centers = (jnp.arange(bins_plddt, dtype=jnp.float32) + 0.5) / bins_plddt
    atom_confidence = bin_average(atom_logits, plddt_centers)
    return (aligned_error, interface_score, atom_confidence)


WHOLE_PAIR_BYTES = 4 * 1024 * 1024
SCOPED_BYTES = 16 * 1024 * 1024
VMEM = pl.BlockSpec(memory_space=pltpu.VMEM)


HBM = pl.BlockSpec(memory_space=pltpu.HBM)


def run(kernel, name, out_shapes, arguments, held=None, scratch=(), aliases=None):
    held = len(arguments) if held is None else held
    spaces = [pltpu.VMEM] * held + [pltpu.HBM] * (len(arguments) - held)
    return pl.pallas_call(
        kernel,
        out_shape=out_shapes,
        in_specs=[VMEM] * held + [HBM] * (len(arguments) - held),
        out_specs=(VMEM,) * len(out_shapes) if isinstance(out_shapes, tuple) else VMEM,
        scratch_shapes=list(scratch),
        input_output_aliases=aliases or {},
        compiler_params=pltpu.CompilerParams(vmem_limit_bytes=SCOPED_BYTES),
        name=name,
    )(*map(pltpu.with_memory_space_constraint, arguments, spaces))


def bring(sources, targets, arrived):
    copies = [
        pltpu.make_async_copy(source, target, arrived.at[place])
        for place, (source, target) in enumerate(zip(sources, targets))
    ]
    for copy in copies:
        copy.start()
    for copy in copies:
        copy.wait()


def sigmoid(values):
    return 1.0 / (1.0 + jnp.exp(-values))


def place_of():
    row = lax.axis_index("row")
    return lax.div(row, 2), lax.rem(row, 2), lax.axis_index("col")


def token_count(mask_ref):
    return jnp.sum(mask_ref[...].astype(jnp.float32), axis=1, keepdims=True)


def real_pairs(mask_ref, row_start, col_start, shape):
    limit = token_count(mask_ref).astype(jnp.int32).reshape(1, 1, 1)
    rows = lax.broadcasted_iota(jnp.int32, shape, 0) + row_start
    cols = lax.broadcasted_iota(jnp.int32, shape, 1) + col_start
    return jnp.where((rows < limit) & (cols < limit), 1.0, 0.0)


def fetch_kernel(z_ref, coords_ref, out_ref, coords_out_ref, arrived):
    pairs = z_ref.shape[0]
    bring((z_ref, coords_ref), (out_ref.at[0:pairs, :], coords_out_ref), arrived)
    out_ref[pairs:, :] = jnp.zeros_like(out_ref[pairs:, :])


def pack_kernel(packed_ref, mine_ref, other_ref, out_ref):
    del packed_ref
    width = out_ref.shape[1]
    atoms = mine_ref.shape[1]
    first = lax.rem(lax.axis_index("row"), 2) == 0
    mine, other = mine_ref[...], other_ref[...]
    value = jnp.concatenate(
        [jnp.where(first, mine, other), jnp.where(first, other, mine)], axis=1
    )
    high = value.astype(jnp.bfloat16).astype(jnp.float32)
    middle = (value - high).astype(jnp.bfloat16).astype(jnp.float32)
    low = value - high - middle
    stacked = jnp.concatenate([high, middle, low, jnp.zeros((7, 2 * atoms), jnp.float32)], axis=0)
    filler = jnp.zeros((16, width - 2 * atoms), jnp.float32)
    out_ref[out_ref.shape[0] - 16 :, :] = jnp.concatenate([stacked, filler], axis=1).astype(
        jnp.bfloat16
    )


def prepare_kernel(copied, *refs):
    raw = refs[1:6]
    sources = refs[6 : 6 + copied]
    rows_ref, cols_ref, dist_ref, atom_part_ref = refs[6 + copied : 10 + copied]
    targets = refs[10 + copied : 10 + 2 * copied]
    w_left_ref, w_right_ref, w_dist_ref, atom_single_ref, atom_w_ref, arrived = refs[
        10 + 2 * copied :
    ]
    landing = (w_left_ref, w_right_ref, w_dist_ref, atom_single_ref, atom_w_ref)
    bring((*raw, *sources), (*landing, *targets), arrived)
    single = targets[0][...]
    rows_ref[...] = jnp.dot(single, w_left_ref[...], preferred_element_type=jnp.float32)
    cols_ref[...] = jnp.dot(single, w_right_ref[...], preferred_element_type=jnp.float32)
    dist_ref[...] = jnp.zeros_like(dist_ref)
    dist_ref[0 : w_dist_ref.shape[0], :] = w_dist_ref[...].astype(jnp.float32)
    atom_part_ref[...] = lax.dot_general(
        atom_w_ref[...],
        atom_single_ref[...],
        (((1,), (1,)), ((), ())),
        preferred_element_type=jnp.float32,
    )


def edge_kernel(slots, col_count, atoms, basis_count, *refs):
    packs = refs[: len(slots)]
    rows_ref, cols_ref, dist_ref, rep_ref, mask_ref, tri_in_ref = refs[len(slots) : len(slots) + 6]
    pair_ref, normed_ref, right_ref, xyz_ref = refs[len(slots) + 6 :]
    _, tile_rows, _, tile_cols, width = pair_ref.shape
    tokens = rows_ref.shape[0]
    pairs = tile_rows * tile_cols
    chip, half, col = place_of()
    w_dist = dist_ref[...].astype(jnp.bfloat16)
    rep = rep_ref[...]
    order = lax.broadcasted_iota(jnp.int32, (width, tokens), 0)
    picked = jnp.zeros((tokens, 16), jnp.float32)
    for pack, (chip_step, col_step) in zip(packs, slots):
        device = 2 * (chip ^ chip_step) * col_count + (col ^ col_step)
        number = jnp.where(
            order < atoms, order + device * atoms, order - atoms + (device + col_count) * atoms
        )
        chosen = (number == rep).astype(jnp.float32).astype(jnp.bfloat16)
        picked = picked + lax.dot_general(
            chosen, pack[pairs:, :], (((0,), (1,)), ((), ())), preferred_element_type=jnp.float32
        )
    for axis in range(3):
        whole = picked[:, axis : axis + 1] + picked[:, axis + 3 : axis + 4]
        whole = whole + picked[:, axis + 6 : axis + 7]
        xyz_ref[axis] = jnp.broadcast_to(whole, (tokens, width))
    step_size = 18.0 / (basis_count - 1)
    centers = 3.375 + step_size * lax.broadcasted_iota(jnp.int32, (1, 1, width), 2).astype(
        jnp.float32
    )
    tile = (tile_rows, tile_cols, width)
    tri_in = tri_in_ref[:, 2 * width : 4 * width]
    for pack, (chip_step, col_step) in zip(packs, slots):
        at_chip = chip ^ chip_step
        at_col = col ^ col_step
        row_start = pl.multiple_of((2 * at_chip + half) * tile_rows, 8)
        col_start = pl.multiple_of(at_col * tile_cols, 8)
        row_slice = pl.ds(row_start, tile_rows)
        col_slice = pl.ds(col_start, tile_cols)
        square = jnp.zeros(tile, jnp.float32)
        for axis in range(3):
            gap = xyz_ref[axis, row_slice, :][:, None, :] - xyz_ref[axis, col_slice, :][None]
            square = square + gap * gap
        scaled = (jnp.sqrt(square) - centers) * (1.0 / step_size)
        basis = jnp.exp(-scaled * scaled).astype(jnp.bfloat16)
        pair = (
            pack[0:pairs, :].astype(jnp.float32).reshape(tile)
            + rows_ref[row_slice, :][:, None, :]
            + cols_ref[col_slice, :][None]
        )
        pair = pair.reshape(pairs, width) + jnp.dot(
            basis.reshape(pairs, width), w_dist, preferred_element_type=jnp.float32
        )
        pair_ref[at_chip, :, at_col] = pair.reshape(tile)
        normed = layer_norm(pair).astype(jnp.bfloat16)
        normed_ref[at_chip, :, at_col] = normed.reshape(tile)
        projected = jnp.dot(normed, tri_in, preferred_element_type=jnp.float32)
        right = sigmoid(projected[:, 0:width]) * projected[:, width : 2 * width]
        right = right.reshape(tile) * real_pairs(mask_ref, row_start, col_start, tile)
        right_ref[at_col, :, at_chip] = jnp.swapaxes(right, 0, 1).astype(jnp.bfloat16)


def left_kernel(normed_ref, tri_in_ref, mask_ref, left_ref, gating_ref):
    chips, tile_rows, col_count, tile_cols, width = normed_ref.shape
    _, half, _ = place_of()
    pairs = tile_rows * tile_cols
    tile = (tile_rows, tile_cols, width)
    tri_in = jnp.concatenate([tri_in_ref[:, 0 : 2 * width], tri_in_ref[:, 4 * width :]], axis=1)
    for at_chip in range(chips):
        for at_col in range(col_count):
            normed = normed_ref[at_chip, :, at_col].reshape(pairs, width)
            projected = jnp.dot(normed, tri_in, preferred_element_type=jnp.float32)
            left = sigmoid(projected[:, 0:width]) * projected[:, width : 2 * width]
            real = real_pairs(
                mask_ref, (2 * at_chip + half) * tile_rows, at_col * tile_cols, tile
            )
            left = (left.reshape(tile) * real).astype(jnp.bfloat16)
            left_ref[at_chip, :, at_col] = left.astype(jnp.float32)
            gating_ref[at_chip, :, at_col] = sigmoid(projected[:, 2 * width :]).reshape(tile)


def triangle_kernel(
    left_ref,
    mine_ref,
    other_ref,
    pair_ref,
    gating_ref,
    tri_out_ref,
    mask_ref,
    pooled_ref,
    own_ref,
    right_ref,
    updated_ref,
):
    chips, tile_rows, col_count, tile_cols, width = pair_ref.shape
    tokens = col_count * tile_cols
    chip, half, _ = place_of()
    shape = (tokens, chips, tile_rows, width)
    right_ref[:, :, half] = mine_ref[...].reshape(shape).astype(jnp.float32)
    right_ref[:, :, 1 - half] = other_ref[...].reshape(shape).astype(jnp.float32)
    token_order = lax.broadcasted_iota(jnp.int32, (tokens, width), 0)
    real = jnp.where(token_order < token_count(mask_ref).astype(jnp.int32), 1.0, 0.0)
    tri_out = tri_out_ref[...]
    block = 4
    blocks = tile_rows // block

    def rows_of(step, carry):
        at_chip = lax.div(step, blocks)
        first = lax.rem(step, blocks) * block

        def add_token(token, sums):
            key = right_ref[token].reshape(tokens, width)
            key_col = lax.div(token, tile_cols)
            key_place = lax.rem(token, tile_cols)
            return tuple(
                sums[i] + left_ref[at_chip, first + i, key_col, pl.ds(key_place, 1), :] * key
                for i in range(block)
            )

        zero = jnp.zeros((tokens, width), jnp.float32)
        sums = lax.fori_loop(0, tokens, add_token, (zero,) * block, unroll=8)
        outer = jnp.concatenate(sums, axis=0)
        change = jnp.dot(
            layer_norm(outer).astype(jnp.bfloat16), tri_out, preferred_element_type=jnp.float32
        )
        for i in range(block):
            gating = gating_ref[at_chip, first + i].reshape(tokens, width)
            updated = pair_ref[at_chip, first + i].reshape(tokens, width) + gating * (
                change[i * tokens : (i + 1) * tokens]
            )
            updated_ref[at_chip, first + i] = updated.astype(jnp.bfloat16)
            pooled_ref[pl.ds(at_chip * tile_rows + first + i, 1), :] = jnp.sum(
                updated * real, axis=0, keepdims=True
            )
        return carry

    lax.fori_loop(0, chips * blocks, rows_of, 0)
    own_ref[...] = updated_ref[chip].reshape(tile_rows * tokens, width)


def score_kernel(
    tm_scale, col_count, own_ref, pae_w_ref, mask_ref, chain_ref, aligned_ref, interface_ref
):
    tile_rows, tile_cols = aligned_ref.shape
    tokens = chain_ref.shape[1]
    chip, half, col = place_of()
    bins = pae_w_ref.shape[0]
    logits = lax.dot_general(
        pae_w_ref[...],
        own_ref[...],
        (((1,), (1,)), ((), ())),
        preferred_element_type=jnp.float32,
    )
    centers = 0.5 * (lax.broadcasted_iota(jnp.int32, (bins, 1), 0).astype(jnp.float32) + 0.5)
    ratio = centers / tm_scale
    weight = jnp.exp(logits - jnp.max(logits, axis=0, keepdims=True))
    total = jnp.sum(weight, axis=0, keepdims=True)
    error = jnp.sum(weight * centers, axis=0, keepdims=True) / total
    tm_pair = jnp.sum(weight * (1.0 / (1.0 + ratio * ratio)), axis=0, keepdims=True) / total
    chains = chain_ref[...]
    keys = lax.broadcasted_iota(jnp.int32, (1, tokens), 1)
    limit = token_count(mask_ref).astype(jnp.int32)
    places = lax.broadcasted_iota(jnp.int32, (1, tile_rows), 1)
    scores = jnp.zeros((1, tile_rows), jnp.float32)
    query = (2 * chip + half) * tile_rows
    for i in range(tile_rows):
        span = error[:, i * tokens : (i + 1) * tokens]
        mine = span[:, 0:tile_cols]
        for other in range(1, col_count):
            mine = jnp.where(
                col == other, span[:, other * tile_cols : (other + 1) * tile_cols], mine
            )
        aligned_ref[i : i + 1, :] = mine
        own_chain = jnp.sum(
            jnp.where(keys == query + i, chains, 0).astype(jnp.float32), axis=1, keepdims=True
        ).astype(jnp.int32)
        face = (keys < limit) & (query + i < limit) & (chains != own_chain)
        face = jnp.where(face, 1.0, 0.0)
        number = jnp.sum(face, axis=1, keepdims=True)
        score = jnp.sum(face * tm_pair[:, i * tokens : (i + 1) * tokens], axis=1, keepdims=True)
        scores = jnp.where(places == i, score / jnp.maximum(number, 1.0), scores)
    interface_ref[...] = scores


def atom_kernel(
    mine_ref,
    other_ref,
    single_ref,
    mask_ref,
    pool_w_ref,
    plddt_w_ref,
    atom_token_ref,
    atom_part_ref,
    out_ref,
    pooled_ref,
):
    chips, _, tile_rows, width = pooled_ref.shape
    tokens = single_ref.shape[0]
    half = lax.rem(lax.axis_index("row"), 2)
    pooled_ref[:, half] = mine_ref[...].reshape(chips, tile_rows, width)
    pooled_ref[:, 1 - half] = other_ref[...].reshape(chips, tile_rows, width)
    pooled = pooled_ref[...].reshape(tokens, width) / token_count(mask_ref)
    single_new = single_ref[...].astype(jnp.float32) + jnp.dot(
        pooled.astype(jnp.bfloat16), pool_w_ref[...], preferred_element_type=jnp.float32
    )
    single_norm = layer_norm(single_new).astype(jnp.bfloat16)
    atoms = atom_token_ref.shape[1]
    order = lax.broadcasted_iota(jnp.int32, (tokens, atoms), 0)
    chosen = (order == atom_token_ref[...]).astype(jnp.float32).astype(jnp.bfloat16)
    picked = lax.dot_general(
        chosen, single_norm, (((0,), (0,)), ((), ())), preferred_element_type=jnp.float32
    ).astype(jnp.bfloat16)
    logits = (
        lax.dot_general(
            plddt_w_ref[...], picked, (((1,), (1,)), ((), ())), preferred_element_type=jnp.float32
        )
        + atom_part_ref[...]
    )
    bins = logits.shape[0]
    centers = (lax.broadcasted_iota(jnp.int32, (bins, 1), 0).astype(jnp.float32) + 0.5) / bins
    weight = jnp.exp(logits - jnp.max(logits, axis=0, keepdims=True))
    total = jnp.sum(weight, axis=0, keepdims=True)
    out_ref[...] = jnp.sum(weight * centers, axis=0, keepdims=True) / total


def direct(
    z_trunk,
    single,
    atom_coords,
    atom_single,
    rep_atom,
    atom_token,
    token_mask,
    chain_id,
    w_left,
    w_right,
    w_dist,
    tri_in,
    tri_out,
    pae_w,
    pool_w,
    plddt_w,
    atom_w,
):
    tile_rows, tile_cols, width = z_trunk.shape
    tokens = single.shape[0]
    atoms = atom_coords.shape[1]
    if tokens * tokens * width * 4 > WHOLE_PAIR_BYTES or 2 * atoms > width:
        return per_device(
            z_trunk, single, atom_coords, atom_single, rep_atom, atom_token, token_mask, chain_id,
            w_left, w_right, w_dist, tri_in, tri_out, pae_w, pool_w, plddt_w, atom_w,
        )
    row_count = lax.axis_size("row")
    col_count = lax.axis_size("col")
    chips = row_count // 2
    float32, bfloat16 = jnp.float32, jnp.bfloat16

    def across(values, axis, count, step):
        return lax.ppermute(values, axis, [(i, i ^ step) for i in range(count)])

    def partner(values):
        return across(values, "row", row_count, 1)

    block = pltpu.VMEM((tile_rows * tile_cols + 16, width), bfloat16)
    fetched, coords = run(
        fetch_kernel,
        "fetch",
        (block, pltpu.VMEM((3, atoms), float32)),
        (z_trunk.reshape(tile_rows * tile_cols, width), atom_coords),
        0,
        scratch=(pltpu.SemaphoreType.DMA((2,)),),
    )
    packed = run(
        pack_kernel, "pack", block, (fetched, coords, partner(atom_coords)), aliases={0: 0}
    )
    slots = [(i, j) for i in range(chips) for j in range(col_count)]
    along = [packed] + [across(packed, "row", row_count, 2 * i) for i in range(1, chips)]
    packs = [along[i] if j == 0 else across(along[i], "col", col_count, j) for i, j in slots]
    raw = (w_left, w_right, w_dist, atom_single, atom_w.T)
    kept = (
        single, tri_in, tri_out, pae_w.T, pool_w, plddt_w.T, rep_atom.reshape(1, tokens),
        token_mask.reshape(1, tokens), chain_id.reshape(1, tokens), atom_token.reshape(1, atoms),
    )
    rows, cols, dist, atom_part, *kept = run(
        lambda *refs: prepare_kernel(len(kept), *refs),
        "prepare",
        (
            pltpu.VMEM((tokens, width), float32),
            pltpu.VMEM((tokens, width), float32),
            pltpu.VMEM((width, width), float32),
            pltpu.VMEM((plddt_w.shape[1], atoms), float32),
            *[pltpu.VMEM(value.shape, value.dtype) for value in kept],
        ),
        (packed, *raw, *kept),
        1,
        scratch=(
            *[pltpu.VMEM(value.shape, value.dtype) for value in raw],
            pltpu.SemaphoreType.DMA((len(raw) + len(kept),)),
        ),
    )
    single, tri_in, tri_out, pae_w, pool_w, plddt_w, rep, mask, chain, atom_token = kept
    full = (chips, tile_rows, col_count, tile_cols, width)
    pair, normed, right = run(
        lambda *refs: edge_kernel(slots, col_count, atoms, w_dist.shape[0], *refs),
        "edges",
        (
            pltpu.VMEM(full, float32),
            pltpu.VMEM(full, bfloat16),
            pltpu.VMEM((col_count, tile_cols, chips, tile_rows, width), bfloat16),
        ),
        (*packs, rows, cols, dist, rep, mask, tri_in),
        scratch=(pltpu.VMEM((3, tokens, width), float32),),
    )
    left, gating = run(
        left_kernel,
        "left",
        (pltpu.VMEM(full, float32), pltpu.VMEM(full, float32)),
        (normed, tri_in, mask),
    )
    pooled, own = run(
        triangle_kernel,
        "triangle",
        (
            pltpu.VMEM((chips * tile_rows, width), float32),
            pltpu.VMEM((tile_rows * tokens, width), bfloat16),
        ),
        (left, right, partner(right), pair, gating, tri_out, mask),
        scratch=(
            pltpu.VMEM((tokens, chips, 2, tile_rows, width), float32),
            pltpu.VMEM((chips, tile_rows, tokens, width), bfloat16),
        ),
    )
    tm_scale = 1.24 * (max(tokens, 19) - 15) ** (1.0 / 3.0) - 1.8
    aligned_error, interface_score = run(
        lambda *refs: score_kernel(tm_scale, col_count, *refs),
        "scores",
        (
            jax.ShapeDtypeStruct((tile_rows, tile_cols), float32),
            jax.ShapeDtypeStruct((1, tile_rows), float32),
        ),
        (own, pae_w, mask, chain),
    )
    atom_confidence = run(
        atom_kernel,
        "atoms",
        jax.ShapeDtypeStruct((1, atoms), float32),
        (pooled, partner(pooled), single, mask, pool_w, plddt_w, atom_token, atom_part),
        scratch=(pltpu.VMEM((chips, 2, tile_rows, width), float32),),
    )
    return (aligned_error, interface_score.reshape(tile_rows), atom_confidence.reshape(atoms))


def gathers_whole(mesh):
    row_count, col_count = mesh.shape["row"], mesh.shape["col"]
    power = all(count & (count - 1) == 0 for count in (row_count, col_count))
    return power and row_count > 1 and mesh.shape["ch"] == 1


def solution(mesh):
    placed = (
        P(("parts", "row"), ("col", "ch"), None),
        P("parts", None),
        P(None, ("parts", "row", "col", "ch")),
        P(("parts", "row", "col", "ch"), None),
        P("parts"),
        P(("parts", "row", "col", "ch")),
        P("parts"),
        P("parts"),
        P(),
        P(),
        P(),
        P(),
        P(),
        P(),
        P(),
        P(),
        P(),
    )
    return jax.shard_map(
        direct if gathers_whole(mesh) else per_device,
        mesh=mesh,
        in_specs=placed,
        out_specs=(
            P(("parts", "row"), ("col", "ch")),
            P(("parts", "row")),
            P(("parts", "row", "col", "ch")),
        ),
        check_vma=False,
    )
```

```python
import jax
import jax.numpy as jnp
from jax import lax
from jax.experimental import pallas as pl
from jax.experimental.pallas import tpu as pltpu
from jax.sharding import PartitionSpec as P

EPSILON = 1e-05


def layer_norm(values):
    center = values - jnp.mean(values, axis=-1, keepdims=True)
    spread = jnp.mean(center * center, axis=-1, keepdims=True)
    return center * lax.rsqrt(spread + EPSILON)


def distance_basis(distance, count):
    step_size = 18.0 / (count - 1)
    centers = 3.375 + step_size * jnp.arange(count, dtype=jnp.float32)
    scaled = (distance[..., None] - centers) / step_size
    return jnp.exp(-scaled * scaled)


def bin_average(logits, centers):
    probability = jax.nn.softmax(logits, axis=-1)
    return jnp.sum(probability * centers, axis=-1)


def per_device(
    z_trunk,
    single,
    atom_coords,
    atom_single,
    rep_atom,
    atom_token,
    token_mask,
    chain_id,
    w_left,
    w_right,
    w_dist,
    tri_in,
    tri_out,
    pae_w,
    pool_w,
    plddt_w,
    atom_w,
):
    tile_rows, tile_cols, pair_width = z_trunk.shape
    tokens = single.shape[0]
    col_index = lax.axis_index("col") * lax.axis_size("ch") + lax.axis_index("ch")
    row_start = lax.axis_index("row") * tile_rows
    col_start = col_index * tile_cols
    wanted = jnp.concatenate(
        [
            lax.dynamic_slice_in_dim(rep_atom, row_start, tile_rows),
            lax.dynamic_slice_in_dim(rep_atom, col_start, tile_cols),
        ]
    )
    shard_piece = lax.all_gather(atom_coords, ("row", "col", "ch"), axis=1, tiled=True)
    places = lax.iota(jnp.int32, shard_piece.shape[1])
    selector = (places[:, None] == wanted[None, :]).astype(jnp.float32)
    coords = jnp.dot(
        shard_piece, selector, precision=lax.Precision.HIGHEST, preferred_element_type=jnp.float32
    )
    offset = coords[:, :tile_rows, None] - coords[:, None, tile_rows:]
    distance = jnp.sqrt(jnp.sum(offset * offset, axis=0))
    basis_count = w_dist.shape[0]
    radial_basis = distance_basis(distance, basis_count).astype(jnp.bfloat16)
    embedded = jnp.dot(
        radial_basis.reshape(-1, basis_count), w_dist, preferred_element_type=jnp.float32
    ).reshape(tile_rows, tile_cols, pair_width)
    row_single = lax.dynamic_slice_in_dim(single, row_start, tile_rows)
    col_single = lax.dynamic_slice_in_dim(single, col_start, tile_cols)
    from_rows = jnp.dot(row_single, w_left, preferred_element_type=jnp.float32)
    from_cols = jnp.dot(col_single, w_right, preferred_element_type=jnp.float32)
    pair_rep = (
        z_trunk.astype(jnp.float32) + from_rows[:, None, :] + from_cols[None, :, :] + embedded
    )
    mask_float = token_mask.astype(jnp.float32)
    row_mask = lax.dynamic_slice_in_dim(mask_float, row_start, tile_rows)
    col_mask = lax.dynamic_slice_in_dim(mask_float, col_start, tile_cols)
    pair_mask = row_mask[:, None] * col_mask[None, :]
    normed = layer_norm(pair_rep).astype(jnp.bfloat16)
    projected = jnp.dot(
        normed.reshape(-1, pair_width), tri_in, preferred_element_type=jnp.float32
    ).reshape(tile_rows, tile_cols, 5 * pair_width)
    left_side = (
        jax.nn.sigmoid(projected[..., 0:pair_width])
        * projected[..., pair_width : 2 * pair_width]
        * pair_mask[..., None]
    ).astype(jnp.bfloat16)
    right_side = (
        jax.nn.sigmoid(projected[..., 2 * pair_width : 3 * pair_width])
        * projected[..., 3 * pair_width : 4 * pair_width]
        * pair_mask[..., None]
    ).astype(jnp.bfloat16)
    gating = jax.nn.sigmoid(projected[..., 4 * pair_width : 5 * pair_width])
    partial_terms = jnp.einsum(
        "ikc,jkc->ijc",
        left_side,
        lax.all_gather(right_side, "row", axis=0, tiled=True),
        preferred_element_type=jnp.float32,
    )
    product_sum = lax.psum_scatter(partial_terms, ("col", "ch"), scatter_dimension=1, tiled=True)
    normed_outer = layer_norm(product_sum).astype(jnp.bfloat16)
    updated = pair_rep + gating * jnp.dot(
        normed_outer.reshape(-1, pair_width), tri_out, preferred_element_type=jnp.float32
    ).reshape(tile_rows, tile_cols, pair_width)
    bins_pae = pae_w.shape[1]
    pae_logits = jnp.dot(
        updated.astype(jnp.bfloat16).reshape(-1, pair_width),
        pae_w,
        preferred_element_type=jnp.float32,
    ).reshape(tile_rows, tile_cols, bins_pae)
    pae_centers = 0.5 * (jnp.arange(bins_pae, dtype=jnp.float32) + 0.5)
    probability = jax.nn.softmax(pae_logits, axis=-1)
    aligned_error = jnp.sum(probability * pae_centers, axis=-1)
    tm_scale = 1.24 * (max(tokens, 19) - 15) ** (1.0 / 3.0) - 1.8
    tm_values = 1.0 / (1.0 + (pae_centers / tm_scale) ** 2)
    tm_pair = jnp.sum(probability * tm_values, axis=-1)
    row_chain = lax.dynamic_slice_in_dim(chain_id, row_start, tile_rows)
    col_chain = lax.dynamic_slice_in_dim(chain_id, col_start, tile_cols)
    interface = pair_mask * (row_chain[:, None] != col_chain[None, :]).astype(jnp.float32)
    numerator_part = jnp.sum(interface * tm_pair, axis=1)
    count_part = jnp.sum(interface, axis=1)
    pooled_part = jnp.sum(col_mask[None, :, None] * updated, axis=1)
    numerator, count_total, pooled = lax.psum(
        (numerator_part, count_part, pooled_part), ("col", "ch")
    )
    interface_score = numerator / jnp.maximum(count_total, 1.0)
    pooled = pooled / jnp.sum(mask_float)
    single_new = row_single.astype(jnp.float32) + jnp.dot(
        pooled.astype(jnp.bfloat16), pool_w, preferred_element_type=jnp.float32
    )
    single_norm = layer_norm(single_new).astype(jnp.bfloat16)
    bins_plddt = plddt_w.shape[1]
    shard_piece = lax.all_gather(single_norm, "row", axis=0, tiled=True)
    places = lax.iota(jnp.int32, shard_piece.shape[0])
    selector = (atom_token[:, None] == places[None, :]).astype(jnp.bfloat16)
    picked = jnp.dot(selector, shard_piece, preferred_element_type=jnp.float32)
    atom_logits = jnp.dot(picked.astype(jnp.bfloat16), plddt_w, preferred_element_type=jnp.float32)
    atom_logits = atom_logits + jnp.dot(atom_single, atom_w, preferred_element_type=jnp.float32)
    plddt_centers = (jnp.arange(bins_plddt, dtype=jnp.float32) + 0.5) / bins_plddt
    atom_confidence = bin_average(atom_logits, plddt_centers)
    return (aligned_error, interface_score, atom_confidence)


WHOLE_PAIR_BYTES = 4 * 1024 * 1024
SPREAD = 1
SCOPED_BYTES = 16 * 1024 * 1024
VMEM = pl.BlockSpec(memory_space=pltpu.VMEM)


HBM = pl.BlockSpec(memory_space=pltpu.HBM)


def run(kernel, name, out_shapes, arguments, held=None, scratch=(), aliases=None):
    held = len(arguments) if held is None else held
    spaces = [pltpu.VMEM] * held + [pltpu.HBM] * (len(arguments) - held)
    return pl.pallas_call(
        kernel,
        out_shape=out_shapes,
        in_specs=[VMEM] * held + [HBM] * (len(arguments) - held),
        out_specs=(VMEM,) * len(out_shapes) if isinstance(out_shapes, tuple) else VMEM,
        scratch_shapes=list(scratch),
        input_output_aliases=aliases or {},
        compiler_params=pltpu.CompilerParams(vmem_limit_bytes=SCOPED_BYTES),
        name=name,
    )(*map(pltpu.with_memory_space_constraint, arguments, spaces))


def bring(sources, targets, arrived):
    copies = [
        pltpu.make_async_copy(source, target, arrived.at[place])
        for place, (source, target) in enumerate(zip(sources, targets))
    ]
    for copy in copies:
        copy.start()
    for copy in copies:
        copy.wait()


def sigmoid(values):
    return 0.5 * jnp.tanh(0.5 * values) + 0.5


def gated(gates, values, half_mask):
    return (jnp.tanh(0.5 * gates) + 1.0) * values * half_mask


def place_of():
    row = lax.axis_index("row")
    return lax.div(row, 2), lax.rem(row, 2), lax.axis_index("col")


def token_count(mask_ref):
    return jnp.sum(mask_ref[...].astype(jnp.float32), axis=1, keepdims=True)


def half_mask(limit, row_start, col_start, shape):
    rows, cols, width = shape
    places = lax.broadcasted_iota(jnp.int32, (cols, width), 0) + col_start
    keys = jnp.where(places < limit, 0.5, 0.0)
    return jnp.stack([jnp.where(row_start + i < limit, keys, 0.0) for i in range(rows)])


def fetch_kernel(z_ref, coords_ref, out_ref, coords_out_ref, arrived):
    pairs = z_ref.shape[0]
    bring((z_ref, coords_ref), (out_ref.at[0:pairs, :], coords_out_ref), arrived)
    out_ref[pairs:, :] = jnp.zeros_like(out_ref[pairs:, :])


def pack_kernel(packed_ref, mine_ref, other_ref, out_ref):
    del packed_ref
    width = out_ref.shape[1]
    atoms = mine_ref.shape[1]
    first = lax.rem(lax.axis_index("row"), 2) == 0
    mine, other = mine_ref[...], other_ref[...]
    value = jnp.concatenate(
        [jnp.where(first, mine, other), jnp.where(first, other, mine)], axis=1
    )
    high = value.astype(jnp.bfloat16).astype(jnp.float32)
    middle = (value - high).astype(jnp.bfloat16).astype(jnp.float32)
    low = value - high - middle
    stacked = jnp.concatenate([high, middle, low, jnp.zeros((7, 2 * atoms), jnp.float32)], axis=0)
    filler = jnp.zeros((16, width - 2 * atoms), jnp.float32)
    out_ref[out_ref.shape[0] - 16 :, :] = jnp.concatenate([stacked, filler], axis=1).astype(
        jnp.bfloat16
    )


def prepare_kernel(copied, *refs):
    raw = refs[1:6]
    sources = refs[6 : 6 + copied]
    rows_ref, cols_ref, dist_ref, atom_part_ref = refs[6 + copied : 10 + copied]
    targets = refs[10 + copied : 10 + 2 * copied]
    w_left_ref, w_right_ref, w_dist_ref, atom_single_ref, atom_w_ref, arrived = refs[
        10 + 2 * copied :
    ]
    landing = (w_left_ref, w_right_ref, w_dist_ref, atom_single_ref, atom_w_ref)
    bring((*raw, *sources), (*landing, *targets), arrived)
    single = targets[0][...]
    rows_ref[...] = jnp.dot(single, w_left_ref[...], preferred_element_type=jnp.float32)
    cols_ref[...] = jnp.dot(single, w_right_ref[...], preferred_element_type=jnp.float32)
    dist_ref[...] = jnp.zeros_like(dist_ref)
    dist_ref[0 : w_dist_ref.shape[0], :] = w_dist_ref[...].astype(jnp.float32)
    atom_part_ref[...] = lax.dot_general(
        atom_w_ref[...],
        atom_single_ref[...],
        (((1,), (1,)), ((), ())),
        preferred_element_type=jnp.float32,
    )


def edge_kernel(slots, col_count, atoms, basis_count, *refs):
    packs = refs[: len(slots)]
    rows_ref, cols_ref, dist_ref, rep_ref, mask_ref, tri_in_ref = refs[len(slots) : len(slots) + 6]
    pair_ref, normed_ref, right_ref, distance_ref = refs[len(slots) + 6 :]
    _, tile_rows, _, tile_cols, width = pair_ref.shape
    tokens = rows_ref.shape[0]
    pairs = tile_rows * tile_cols
    chip, half, col = place_of()
    w_dist = dist_ref[...].astype(jnp.bfloat16)
    rep = rep_ref[...]
    order = lax.broadcasted_iota(jnp.int32, (width, tokens), 0)
    picked = jnp.zeros((tokens, 16), jnp.float32)
    across = jnp.zeros((16, tokens), jnp.float32)
    for pack, (chip_step, col_step) in zip(packs, slots):
        device = 2 * (chip ^ chip_step) * col_count + (col ^ col_step)
        number = jnp.where(
            order < atoms, order + device * atoms, order - atoms + (device + col_count) * atoms
        )
        chosen = (number == rep).astype(jnp.float32).astype(jnp.bfloat16)
        pieces = pack[pairs:, :]
        picked = picked + lax.dot_general(
            chosen, pieces, (((0,), (1,)), ((), ())), preferred_element_type=jnp.float32
        )
        across = across + jnp.dot(pieces, chosen, preferred_element_type=jnp.float32)
    square = jnp.zeros((tokens, width), jnp.float32)
    for axis in range(3):
        down = picked[:, axis : axis + 1] + picked[:, axis + 3 : axis + 4]
        down = down + picked[:, axis + 6 : axis + 7]
        along = across[axis : axis + 1] + across[axis + 3 : axis + 4] + across[axis + 6 : axis + 7]
        along = jnp.concatenate([along, jnp.zeros((1, width - tokens), jnp.float32)], axis=1)
        gap = down - along
        square = square + gap * gap
    distance = jnp.sqrt(square)
    for chip_step in range(pair_ref.shape[0]):
        first = (2 * (chip ^ chip_step) + half) * tile_rows
        distance_ref[chip_step] = pltpu.roll(distance, lax.rem(width - first, width), 1)
    step_size = 18.0 / (basis_count - 1)
    centers = 3.375 + step_size * lax.broadcasted_iota(jnp.int32, (1, 1, width), 2).astype(
        jnp.float32
    )
    limit = token_count(mask_ref).astype(jnp.int32)
    tile = (tile_rows, tile_cols, width)
    tri_in = tri_in_ref[:, 2 * width : 4 * width]
    for pack, (chip_step, col_step) in zip(packs, slots):
        at_chip = chip ^ chip_step
        at_col = col ^ col_step
        row_start = pl.multiple_of((2 * at_chip + half) * tile_rows, 8)
        col_start = pl.multiple_of(at_col * tile_cols, 8)
        row_slice = pl.ds(row_start, tile_rows)
        col_slice = pl.ds(col_start, tile_cols)
        near = distance_ref[chip_step, col_slice, :]
        spread = jnp.stack(
            [jnp.broadcast_to(near[:, i : i + 1], (tile_cols, width)) for i in range(tile_rows)]
        )
        scaled = (spread - centers) * (1.0 / step_size)
        basis = jnp.exp(-scaled * scaled).astype(jnp.bfloat16)
        pair = (
            pack[0:pairs, :].astype(jnp.float32).reshape(tile)
            + rows_ref[row_slice, :][:, None, :]
            + cols_ref[col_slice, :][None]
        )
        pair = pair.reshape(pairs, width) + jnp.dot(
            basis.reshape(pairs, width), w_dist, preferred_element_type=jnp.float32
        )
        pair_ref[at_chip, :, at_col] = pair.reshape(tile)
        normed = layer_norm(pair).astype(jnp.bfloat16)
        normed_ref[at_chip, :, at_col] = normed.reshape(tile)
        projected = jnp.dot(normed, tri_in, preferred_element_type=jnp.float32)
        right = gated(
            projected[:, 0:width].reshape(tile),
            projected[:, width : 2 * width].reshape(tile),
            half_mask(limit, row_start, col_start, tile),
        )
        right_ref[at_col, :, at_chip] = jnp.swapaxes(right, 0, 1).astype(jnp.bfloat16)


def left_kernel(normed_ref, tri_in_ref, mask_ref, turned_ref, gating_ref, left_ref):
    chips, tile_rows, col_count, tile_cols, width = normed_ref.shape
    tokens = col_count * tile_cols
    _, half, _ = place_of()
    step = turned_ref.shape[0] // (chips * tile_rows)
    limit = token_count(mask_ref).astype(jnp.int32)
    pairs = tile_rows * tile_cols
    tile = (tile_rows, tile_cols, width)
    tri_in = jnp.concatenate([tri_in_ref[:, 0 : 2 * width], tri_in_ref[:, 4 * width :]], axis=1)
    for at_chip in range(chips):
        for at_col in range(col_count):
            normed = normed_ref[at_chip, :, at_col].reshape(pairs, width)
            projected = jnp.dot(normed, tri_in, preferred_element_type=jnp.float32)
            left_ref[:, at_col * tile_cols : (at_col + 1) * tile_cols, :] = gated(
                projected[:, 0:width].reshape(tile),
                projected[:, width : 2 * width].reshape(tile),
                half_mask(limit, (2 * at_chip + half) * tile_rows, at_col * tile_cols, tile),
            )
            gating_ref[at_chip, :, at_col] = sigmoid(projected[:, 2 * width :]).reshape(tile)
        for i in range(tile_rows):
            turned_ref[pl.ds((at_chip * tile_rows + i) * step, width), :] = left_ref[i].T


def triangle_kernel(
    left_ref,
    mine_ref,
    other_ref,
    pair_ref,
    gating_ref,
    tri_out_ref,
    mask_ref,
    pooled_ref,
    own_ref,
    right_ref,
    keys_ref,
    outer_ref,
    updated_ref,
):
    chips, tile_rows, col_count, tile_cols, width = pair_ref.shape
    tokens = col_count * tile_cols
    queries = chips * tile_rows
    step = keys_ref.shape[0] // tokens
    chip, half, _ = place_of()
    shape = (tokens, chips, tile_rows, width)
    right_ref[:, :, half] = mine_ref[...].reshape(shape).astype(jnp.float32)
    right_ref[:, :, 1 - half] = other_ref[...].reshape(shape).astype(jnp.float32)

    def turn(token, carry):
        start = token * step
        keys_ref[pl.ds(start, width), :] = right_ref[token].reshape(tokens, width).T
        return carry

    lax.fori_loop(0, tokens, turn, 0, unroll=tokens)

    def multiply(channel, carry):
        query = left_ref[pl.ds(channel, queries, stride=step), :].astype(jnp.bfloat16)
        key = keys_ref[pl.ds(channel, tokens, stride=step), :].astype(jnp.bfloat16)
        outer_ref[pl.ds(channel, queries, stride=step), :] = jnp.dot(
            query, key, preferred_element_type=jnp.float32
        )
        return carry

    lax.fori_loop(0, width, multiply, 0, unroll=width)
    token_order = lax.broadcasted_iota(jnp.int32, (tokens, width), 0)
    real = jnp.where(token_order < token_count(mask_ref).astype(jnp.int32), 1.0, 0.0)
    tri_out = tri_out_ref[...]
    block = tile_rows
    blocks = tile_rows // block

    def rows_of(group, carry):
        at_chip = lax.div(group, blocks)
        first = lax.rem(group, blocks) * block
        outer = jnp.concatenate(
            [
                outer_ref[pl.ds((group * block + i) * step, width), :].T
                for i in range(block)
            ],
            axis=0,
        )
        change = jnp.dot(
            layer_norm(outer).astype(jnp.bfloat16), tri_out, preferred_element_type=jnp.float32
        )
        for i in range(block):
            gating = gating_ref[at_chip, first + i].reshape(tokens, width)
            updated = pair_ref[at_chip, first + i].reshape(tokens, width) + gating * (
                change[i * tokens : (i + 1) * tokens]
            )
            updated_ref[at_chip, first + i] = updated.astype(jnp.bfloat16)
            pooled_ref[pl.ds(at_chip * tile_rows + first + i, 1), :] = jnp.sum(
                updated * real, axis=0, keepdims=True
            )
        return carry

    lax.fori_loop(0, chips * blocks, rows_of, 0, unroll=2)
    own_ref[...] = updated_ref[chip].reshape(tile_rows * tokens, width)


def score_kernel(
    tm_scale, col_count, own_ref, pae_w_ref, mask_ref, chain_ref, aligned_ref, interface_ref
):
    tile_rows, tile_cols = aligned_ref.shape
    tokens = chain_ref.shape[1]
    chip, half, col = place_of()
    bins = pae_w_ref.shape[0]
    logits = lax.dot_general(
        pae_w_ref[...],
        own_ref[...],
        (((1,), (1,)), ((), ())),
        preferred_element_type=jnp.float32,
    )
    centers = 0.5 * (lax.broadcasted_iota(jnp.int32, (bins, 1), 0).astype(jnp.float32) + 0.5)
    ratio = centers / tm_scale
    weight = jnp.exp(logits - jnp.max(logits, axis=0, keepdims=True))
    total = jnp.sum(weight, axis=0, keepdims=True)
    error = jnp.sum(weight * centers, axis=0, keepdims=True) / total
    tm_pair = jnp.sum(weight * (1.0 / (1.0 + ratio * ratio)), axis=0, keepdims=True) / total
    chains = chain_ref[...]
    keys = lax.broadcasted_iota(jnp.int32, (1, tokens), 1)
    limit = token_count(mask_ref).astype(jnp.int32)
    places = lax.broadcasted_iota(jnp.int32, (1, tile_rows), 1)
    scores = jnp.zeros((1, tile_rows), jnp.float32)
    query = (2 * chip + half) * tile_rows
    for i in range(tile_rows):
        span = error[:, i * tokens : (i + 1) * tokens]
        mine = span[:, 0:tile_cols]
        for other in range(1, col_count):
            mine = jnp.where(
                col == other, span[:, other * tile_cols : (other + 1) * tile_cols], mine
            )
        aligned_ref[i : i + 1, :] = mine
        own_chain = jnp.sum(
            jnp.where(keys == query + i, chains, 0).astype(jnp.float32), axis=1, keepdims=True
        ).astype(jnp.int32)
        face = (keys < limit) & (query + i < limit) & (chains != own_chain)
        face = jnp.where(face, 1.0, 0.0)
        number = jnp.sum(face, axis=1, keepdims=True)
        score = jnp.sum(face * tm_pair[:, i * tokens : (i + 1) * tokens], axis=1, keepdims=True)
        scores = jnp.where(places == i, score / jnp.maximum(number, 1.0), scores)
    interface_ref[...] = scores


def atom_kernel(
    mine_ref,
    other_ref,
    single_ref,
    mask_ref,
    pool_w_ref,
    plddt_w_ref,
    atom_token_ref,
    atom_part_ref,
    out_ref,
    pooled_ref,
):
    chips, _, tile_rows, width = pooled_ref.shape
    tokens = single_ref.shape[0]
    half = lax.rem(lax.axis_index("row"), 2)
    pooled_ref[:, half] = mine_ref[...].reshape(chips, tile_rows, width)
    pooled_ref[:, 1 - half] = other_ref[...].reshape(chips, tile_rows, width)
    pooled = pooled_ref[...].reshape(tokens, width) / token_count(mask_ref)
    atoms = atom_token_ref.shape[1]
    order = lax.broadcasted_iota(jnp.int32, (tokens, atoms), 0)
    chosen = (order == atom_token_ref[...]).astype(jnp.float32).astype(jnp.bfloat16)
    turned = (((0,), (0,)), ((), ()))
    pooled = lax.dot_general(
        chosen, pooled.astype(jnp.bfloat16), turned, preferred_element_type=jnp.float32
    )
    picked = lax.dot_general(chosen, single_ref[...], turned, preferred_element_type=jnp.float32)
    picked = layer_norm(
        picked
        + jnp.dot(
            pooled.astype(jnp.bfloat16), pool_w_ref[...], preferred_element_type=jnp.float32
        )
    ).astype(jnp.bfloat16)
    logits = (
        lax.dot_general(
            plddt_w_ref[...], picked, (((1,), (1,)), ((), ())), preferred_element_type=jnp.float32
        )
        + atom_part_ref[...]
    )
    bins = logits.shape[0]
    centers = (lax.broadcasted_iota(jnp.int32, (bins, 1), 0).astype(jnp.float32) + 0.5) / bins
    weight = jnp.exp(logits - jnp.max(logits, axis=0, keepdims=True))
    total = jnp.sum(weight, axis=0, keepdims=True)
    out_ref[...] = jnp.sum(weight * centers, axis=0, keepdims=True) / total


def direct(
    z_trunk,
    single,
    atom_coords,
    atom_single,
    rep_atom,
    atom_token,
    token_mask,
    chain_id,
    w_left,
    w_right,
    w_dist,
    tri_in,
    tri_out,
    pae_w,
    pool_w,
    plddt_w,
    atom_w,
):
    tile_rows, tile_cols, width = z_trunk.shape
    tokens = single.shape[0]
    atoms = atom_coords.shape[1]
    if tokens * tokens * width * 4 > WHOLE_PAIR_BYTES or 2 * atoms > width:
        return per_device(
            z_trunk, single, atom_coords, atom_single, rep_atom, atom_token, token_mask, chain_id,
            w_left, w_right, w_dist, tri_in, tri_out, pae_w, pool_w, plddt_w, atom_w,
        )
    row_count = lax.axis_size("row")
    col_count = lax.axis_size("col")
    chips = row_count // 2
    float32, bfloat16 = jnp.float32, jnp.bfloat16

    def across(values, axis, count, step):
        return lax.ppermute(values, axis, [(i, i ^ step) for i in range(count)])

    def partner(values):
        return across(values, "row", row_count, 1)

    block = pltpu.VMEM((tile_rows * tile_cols + 16, width), bfloat16)
    fetched, coords = run(
        fetch_kernel,
        "fetch",
        (block, pltpu.VMEM((3, atoms), float32)),
        (z_trunk.reshape(tile_rows * tile_cols, width), atom_coords),
        0,
        scratch=(pltpu.SemaphoreType.DMA((2,)),),
    )
    packed = run(
        pack_kernel, "pack", block, (fetched, coords, partner(atom_coords)), aliases={0: 0}
    )
    slots = [(i, j) for i in range(chips) for j in range(col_count)]
    along = [packed] + [across(packed, "row", row_count, 2 * i) for i in range(1, chips)]
    beside = [packed] + [across(packed, "col", col_count, j) for j in range(1, col_count)]

    def pack_of(i, j):
        if i == 0 or j == 0:
            return beside[j] if i == 0 else along[i]
        if i < chips - 1:
            return across(beside[j], "row", row_count, 2 * i)
        return across(along[i], "col", col_count, j)

    packs = [pack_of(i, j) for i, j in slots]
    raw = (w_left, w_right, w_dist, atom_single, atom_w.T)
    kept = (
        single, tri_in, tri_out, pae_w.T, pool_w, plddt_w.T, rep_atom.reshape(1, tokens),
        token_mask.reshape(1, tokens), chain_id.reshape(1, tokens), atom_token.reshape(1, atoms),
    )
    rows, cols, dist, atom_part, *kept = run(
        lambda *refs: prepare_kernel(len(kept), *refs),
        "prepare",
        (
            pltpu.VMEM((tokens, width), float32),
            pltpu.VMEM((tokens, width), float32),
            pltpu.VMEM((width, width), float32),
            pltpu.VMEM((plddt_w.shape[1], atoms), float32),
            *[pltpu.VMEM(value.shape, value.dtype) for value in kept],
        ),
        (packed, *raw, *kept),
        1,
        scratch=(
            *[pltpu.VMEM(value.shape, value.dtype) for value in raw],
            pltpu.SemaphoreType.DMA((len(raw) + len(kept),)),
        ),
    )
    single, tri_in, tri_out, pae_w, pool_w, plddt_w, rep, mask, chain, atom_token = kept
    full = (chips, tile_rows, col_count, tile_cols, width)
    pair, normed, right = run(
        lambda *refs: edge_kernel(slots, col_count, atoms, w_dist.shape[0], *refs),
        "edges",
        (
            pltpu.VMEM(full, float32),
            pltpu.VMEM(full, bfloat16),
            pltpu.VMEM((col_count, tile_cols, chips, tile_rows, width), bfloat16),
        ),
        (*packs, rows, cols, dist, rep, mask, tri_in),
        scratch=(pltpu.VMEM((chips, tokens, width), float32),),
    )
    step = width + SPREAD
    left, gating = run(
        left_kernel,
        "left",
        (pltpu.VMEM((chips * tile_rows * step, tokens), float32), pltpu.VMEM(full, float32)),
        (normed, tri_in, mask),
        scratch=(pltpu.VMEM((tile_rows, tokens, width), float32),),
    )
    pooled, own = run(
        triangle_kernel,
        "triangle",
        (
            pltpu.VMEM((chips * tile_rows, width), float32),
            pltpu.VMEM((tile_rows * tokens, width), bfloat16),
        ),
        (left, right, partner(right), pair, gating, tri_out, mask),
        scratch=(
            pltpu.VMEM((tokens, chips, 2, tile_rows, width), float32),
            pltpu.VMEM((tokens * step, tokens), float32),
            pltpu.VMEM((chips * tile_rows * step, tokens), float32),
            pltpu.VMEM((chips, tile_rows, tokens, width), bfloat16),
        ),
    )
    tm_scale = 1.24 * (max(tokens, 19) - 15) ** (1.0 / 3.0) - 1.8
    aligned_error, interface_score = run(
        lambda *refs: score_kernel(tm_scale, col_count, *refs),
        "scores",
        (
            jax.ShapeDtypeStruct((tile_rows, tile_cols), float32),
            jax.ShapeDtypeStruct((1, tile_rows), float32),
        ),
        (own, pae_w, mask, chain),
    )
    atom_confidence = run(
        atom_kernel,
        "atoms",
        jax.ShapeDtypeStruct((1, atoms), float32),
        (pooled, partner(pooled), single, mask, pool_w, plddt_w, atom_token, atom_part),
        scratch=(pltpu.VMEM((chips, 2, tile_rows, width), float32),),
    )
    return (aligned_error, interface_score.reshape(tile_rows), atom_confidence.reshape(atoms))


def gathers_whole(mesh):
    row_count, col_count = mesh.shape["row"], mesh.shape["col"]
    power = all(count & (count - 1) == 0 for count in (row_count, col_count))
    return power and row_count > 1 and mesh.shape["ch"] == 1


def solution(mesh):
    placed = (
        P(("parts", "row"), ("col", "ch"), None),
        P("parts", None),
        P(None, ("parts", "row", "col", "ch")),
        P(("parts", "row", "col", "ch"), None),
        P("parts"),
        P(("parts", "row", "col", "ch")),
        P("parts"),
        P("parts"),
        P(),
        P(),
        P(),
        P(),
        P(),
        P(),
        P(),
        P(),
        P(),
    )
    return jax.shard_map(
        direct if gathers_whole(mesh) else per_device,
        mesh=mesh,
        in_specs=placed,
        out_specs=(
            P(("parts", "row"), ("col", "ch")),
            P(("parts", "row")),
            P(("parts", "row", "col", "ch")),
        ),
        check_vma=False,
    )
```

```python
import jax
import jax.numpy as jnp
from jax import lax
from jax.experimental import pallas as pl
from jax.experimental.pallas import tpu as pltpu
from jax.sharding import PartitionSpec as P

EPSILON = 1e-05


def layer_norm(values):
    center = values - jnp.mean(values, axis=-1, keepdims=True)
    spread = jnp.mean(center * center, axis=-1, keepdims=True)
    return center * lax.rsqrt(spread + EPSILON)


def distance_basis(distance, count):
    step_size = 18.0 / (count - 1)
    centers = 3.375 + step_size * jnp.arange(count, dtype=jnp.float32)
    scaled = (distance[..., None] - centers) / step_size
    return jnp.exp(-scaled * scaled)


def bin_average(logits, centers):
    probability = jax.nn.softmax(logits, axis=-1)
    return jnp.sum(probability * centers, axis=-1)


def per_device(
    z_trunk,
    single,
    atom_coords,
    atom_single,
    rep_atom,
    atom_token,
    token_mask,
    chain_id,
    w_left,
    w_right,
    w_dist,
    tri_in,
    tri_out,
    pae_w,
    pool_w,
    plddt_w,
    atom_w,
):
    tile_rows, tile_cols, pair_width = z_trunk.shape
    tokens = single.shape[0]
    col_index = lax.axis_index("col") * lax.axis_size("ch") + lax.axis_index("ch")
    row_start = lax.axis_index("row") * tile_rows
    col_start = col_index * tile_cols
    wanted = jnp.concatenate(
        [
            lax.dynamic_slice_in_dim(rep_atom, row_start, tile_rows),
            lax.dynamic_slice_in_dim(rep_atom, col_start, tile_cols),
        ]
    )
    shard_piece = lax.all_gather(atom_coords, ("row", "col", "ch"), axis=1, tiled=True)
    places = lax.iota(jnp.int32, shard_piece.shape[1])
    selector = (places[:, None] == wanted[None, :]).astype(jnp.float32)
    coords = jnp.dot(
        shard_piece, selector, precision=lax.Precision.HIGHEST, preferred_element_type=jnp.float32
    )
    offset = coords[:, :tile_rows, None] - coords[:, None, tile_rows:]
    distance = jnp.sqrt(jnp.sum(offset * offset, axis=0))
    basis_count = w_dist.shape[0]
    radial_basis = distance_basis(distance, basis_count).astype(jnp.bfloat16)
    embedded = jnp.dot(
        radial_basis.reshape(-1, basis_count), w_dist, preferred_element_type=jnp.float32
    ).reshape(tile_rows, tile_cols, pair_width)
    row_single = lax.dynamic_slice_in_dim(single, row_start, tile_rows)
    col_single = lax.dynamic_slice_in_dim(single, col_start, tile_cols)
    from_rows = jnp.dot(row_single, w_left, preferred_element_type=jnp.float32)
    from_cols = jnp.dot(col_single, w_right, preferred_element_type=jnp.float32)
    pair_rep = (
        z_trunk.astype(jnp.float32) + from_rows[:, None, :] + from_cols[None, :, :] + embedded
    )
    mask_float = token_mask.astype(jnp.float32)
    row_mask = lax.dynamic_slice_in_dim(mask_float, row_start, tile_rows)
    col_mask = lax.dynamic_slice_in_dim(mask_float, col_start, tile_cols)
    pair_mask = row_mask[:, None] * col_mask[None, :]
    normed = layer_norm(pair_rep).astype(jnp.bfloat16)
    projected = jnp.dot(
        normed.reshape(-1, pair_width), tri_in, preferred_element_type=jnp.float32
    ).reshape(tile_rows, tile_cols, 5 * pair_width)
    left_side = (
        jax.nn.sigmoid(projected[..., 0:pair_width])
        * projected[..., pair_width : 2 * pair_width]
        * pair_mask[..., None]
    ).astype(jnp.bfloat16)
    right_side = (
        jax.nn.sigmoid(projected[..., 2 * pair_width : 3 * pair_width])
        * projected[..., 3 * pair_width : 4 * pair_width]
        * pair_mask[..., None]
    ).astype(jnp.bfloat16)
    gating = jax.nn.sigmoid(projected[..., 4 * pair_width : 5 * pair_width])
    partial_terms = jnp.einsum(
        "ikc,jkc->ijc",
        left_side,
        lax.all_gather(right_side, "row", axis=0, tiled=True),
        preferred_element_type=jnp.float32,
    )
    product_sum = lax.psum_scatter(partial_terms, ("col", "ch"), scatter_dimension=1, tiled=True)
    normed_outer = layer_norm(product_sum).astype(jnp.bfloat16)
    updated = pair_rep + gating * jnp.dot(
        normed_outer.reshape(-1, pair_width), tri_out, preferred_element_type=jnp.float32
    ).reshape(tile_rows, tile_cols, pair_width)
    bins_pae = pae_w.shape[1]
    pae_logits = jnp.dot(
        updated.astype(jnp.bfloat16).reshape(-1, pair_width),
        pae_w,
        preferred_element_type=jnp.float32,
    ).reshape(tile_rows, tile_cols, bins_pae)
    pae_centers = 0.5 * (jnp.arange(bins_pae, dtype=jnp.float32) + 0.5)
    probability = jax.nn.softmax(pae_logits, axis=-1)
    aligned_error = jnp.sum(probability * pae_centers, axis=-1)
    tm_scale = 1.24 * (max(tokens, 19) - 15) ** (1.0 / 3.0) - 1.8
    tm_values = 1.0 / (1.0 + (pae_centers / tm_scale) ** 2)
    tm_pair = jnp.sum(probability * tm_values, axis=-1)
    row_chain = lax.dynamic_slice_in_dim(chain_id, row_start, tile_rows)
    col_chain = lax.dynamic_slice_in_dim(chain_id, col_start, tile_cols)
    interface = pair_mask * (row_chain[:, None] != col_chain[None, :]).astype(jnp.float32)
    numerator_part = jnp.sum(interface * tm_pair, axis=1)
    count_part = jnp.sum(interface, axis=1)
    pooled_part = jnp.sum(col_mask[None, :, None] * updated, axis=1)
    numerator, count_total, pooled = lax.psum(
        (numerator_part, count_part, pooled_part), ("col", "ch")
    )
    interface_score = numerator / jnp.maximum(count_total, 1.0)
    pooled = pooled / jnp.sum(mask_float)
    single_new = row_single.astype(jnp.float32) + jnp.dot(
        pooled.astype(jnp.bfloat16), pool_w, preferred_element_type=jnp.float32
    )
    single_norm = layer_norm(single_new).astype(jnp.bfloat16)
    bins_plddt = plddt_w.shape[1]
    shard_piece = lax.all_gather(single_norm, "row", axis=0, tiled=True)
    places = lax.iota(jnp.int32, shard_piece.shape[0])
    selector = (atom_token[:, None] == places[None, :]).astype(jnp.bfloat16)
    picked = jnp.dot(selector, shard_piece, preferred_element_type=jnp.float32)
    atom_logits = jnp.dot(picked.astype(jnp.bfloat16), plddt_w, preferred_element_type=jnp.float32)
    atom_logits = atom_logits + jnp.dot(atom_single, atom_w, preferred_element_type=jnp.float32)
    plddt_centers = (jnp.arange(bins_plddt, dtype=jnp.float32) + 0.5) / bins_plddt
    atom_confidence = bin_average(atom_logits, plddt_centers)
    return (aligned_error, interface_score, atom_confidence)


WHOLE_PAIR_BYTES = 4 * 1024 * 1024
SPREAD = 1
SCOPED_BYTES = 16 * 1024 * 1024
VMEM = pl.BlockSpec(memory_space=pltpu.VMEM)


HBM = pl.BlockSpec(memory_space=pltpu.HBM)


def run(kernel, name, out_shapes, arguments, held=None, scratch=(), aliases=None):
    held = len(arguments) if held is None else held
    spaces = [pltpu.VMEM] * held + [pltpu.HBM] * (len(arguments) - held)
    return pl.pallas_call(
        kernel,
        out_shape=out_shapes,
        in_specs=[VMEM] * held + [HBM] * (len(arguments) - held),
        out_specs=(VMEM,) * len(out_shapes) if isinstance(out_shapes, tuple) else VMEM,
        scratch_shapes=list(scratch),
        input_output_aliases=aliases or {},
        compiler_params=pltpu.CompilerParams(vmem_limit_bytes=SCOPED_BYTES),
        name=name,
    )(*map(pltpu.with_memory_space_constraint, arguments, spaces))


def bring(sources, targets, arrived):
    copies = [
        pltpu.make_async_copy(source, target, arrived.at[place])
        for place, (source, target) in enumerate(zip(sources, targets))
    ]
    for copy in copies:
        copy.start()
    for copy in copies:
        copy.wait()


def sigmoid(values):
    return 0.5 * jnp.tanh(0.5 * values) + 0.5


def gated(gates, values, half_mask):
    return (jnp.tanh(0.5 * gates) + 1.0) * values * half_mask


def place_of():
    row = lax.axis_index("row")
    return lax.div(row, 2), lax.rem(row, 2), lax.axis_index("col")


def token_count(mask_ref):
    return jnp.sum(mask_ref[...].astype(jnp.float32), axis=1, keepdims=True)


def half_mask(limit, row_start, col_start, shape):
    rows, cols, width = shape
    places = lax.broadcasted_iota(jnp.int32, (cols, width), 0) + col_start
    keys = jnp.where(places < limit, 0.5, 0.0)
    return jnp.stack([jnp.where(row_start + i < limit, keys, 0.0) for i in range(rows)])


def spread_keys(target, at_chip, at_col, half, tile):
    rows, cols, _ = tile.shape
    for group in range(cols // rows):
        chip = at_col * (cols // (2 * rows)) + group // 2
        target[at_chip, :, (group % 2) ^ half, chip] = tile[:, group * rows : (group + 1) * rows]


def fetch_kernel(z_ref, coords_ref, out_ref, coords_out_ref, arrived):
    pairs = z_ref.shape[0]
    bring((z_ref, coords_ref), (out_ref.at[0:pairs, :], coords_out_ref), arrived)
    out_ref[pairs:, :] = jnp.zeros_like(out_ref[pairs:, :])


def pack_kernel(packed_ref, mine_ref, other_ref, out_ref):
    del packed_ref
    width = out_ref.shape[1]
    atoms = mine_ref.shape[1]
    first = lax.rem(lax.axis_index("row"), 2) == 0
    mine, other = mine_ref[...], other_ref[...]
    value = jnp.concatenate(
        [jnp.where(first, mine, other), jnp.where(first, other, mine)], axis=1
    )
    high = value.astype(jnp.bfloat16).astype(jnp.float32)
    middle = (value - high).astype(jnp.bfloat16).astype(jnp.float32)
    low = value - high - middle
    stacked = jnp.concatenate([high, middle, low, jnp.zeros((7, 2 * atoms), jnp.float32)], axis=0)
    filler = jnp.zeros((16, width - 2 * atoms), jnp.float32)
    out_ref[out_ref.shape[0] - 16 :, :] = jnp.concatenate([stacked, filler], axis=1).astype(
        jnp.bfloat16
    )


def prepare_kernel(copied, *refs):
    raw = refs[1:6]
    sources = refs[6 : 6 + copied]
    rows_ref, cols_ref, dist_ref, atom_part_ref = refs[6 + copied : 10 + copied]
    targets = refs[10 + copied : 10 + 2 * copied]
    w_left_ref, w_right_ref, w_dist_ref, atom_single_ref, atom_w_ref, arrived = refs[
        10 + 2 * copied :
    ]
    landing = (w_left_ref, w_right_ref, w_dist_ref, atom_single_ref, atom_w_ref)
    bring((*raw, *sources), (*landing, *targets), arrived)
    single = targets[0][...]
    rows_ref[...] = jnp.dot(single, w_left_ref[...], preferred_element_type=jnp.float32)
    cols_ref[...] = jnp.dot(single, w_right_ref[...], preferred_element_type=jnp.float32)
    dist_ref[...] = jnp.zeros_like(dist_ref)
    dist_ref[0 : w_dist_ref.shape[0], :] = w_dist_ref[...].astype(jnp.float32)
    atom_part_ref[...] = lax.dot_general(
        atom_w_ref[...],
        atom_single_ref[...],
        (((1,), (1,)), ((), ())),
        preferred_element_type=jnp.float32,
    )


def edge_kernel(slots, col_count, atoms, basis_count, *refs):
    packs = refs[: len(slots)]
    rows_ref, cols_ref, dist_ref, rep_ref, mask_ref, tri_in_ref = refs[len(slots) : len(slots) + 6]
    pair_ref, normed_ref, right_ref, distance_ref = refs[len(slots) + 6 :]
    _, tile_rows, _, tile_cols, width = normed_ref.shape
    tokens = rows_ref.shape[0]
    pairs = tile_rows * tile_cols
    chip, half, col = place_of()
    w_dist = dist_ref[...].astype(jnp.bfloat16)
    rep = rep_ref[...]
    order = lax.broadcasted_iota(jnp.int32, (width, tokens), 0)
    picked = jnp.zeros((tokens, 16), jnp.float32)
    across = jnp.zeros((16, tokens), jnp.float32)
    for pack, (chip_step, col_step) in zip(packs, slots):
        device = 2 * (chip ^ chip_step) * col_count + (col ^ col_step)
        number = jnp.where(
            order < atoms, order + device * atoms, order - atoms + (device + col_count) * atoms
        )
        chosen = (number == rep).astype(jnp.float32).astype(jnp.bfloat16)
        pieces = pack[pairs:, :]
        picked = picked + lax.dot_general(
            chosen, pieces, (((0,), (1,)), ((), ())), preferred_element_type=jnp.float32
        )
        across = across + jnp.dot(pieces, chosen, preferred_element_type=jnp.float32)
    square = jnp.zeros((tokens, width), jnp.float32)
    for axis in range(3):
        down = picked[:, axis : axis + 1] + picked[:, axis + 3 : axis + 4]
        down = down + picked[:, axis + 6 : axis + 7]
        along = across[axis : axis + 1] + across[axis + 3 : axis + 4] + across[axis + 6 : axis + 7]
        along = jnp.concatenate([along, jnp.zeros((1, width - tokens), jnp.float32)], axis=1)
        gap = down - along
        square = square + gap * gap
    distance = jnp.sqrt(square)
    for chip_step in range(pair_ref.shape[0]):
        first = (2 * (chip ^ chip_step) + half) * tile_rows
        distance_ref[chip_step] = pltpu.roll(distance, lax.rem(width - first, width), 1)
    step_size = 18.0 / (basis_count - 1)
    centers = 3.375 + step_size * lax.broadcasted_iota(jnp.int32, (1, 1, width), 2).astype(
        jnp.float32
    )
    limit = token_count(mask_ref).astype(jnp.int32)
    tile = (tile_rows, tile_cols, width)
    tri_in = tri_in_ref[:, 2 * width : 4 * width]
    for pack, (chip_step, col_step) in zip(packs, slots):
        at_chip = chip ^ chip_step
        at_col = col ^ col_step
        row_start = pl.multiple_of((2 * at_chip + half) * tile_rows, 8)
        col_start = pl.multiple_of(at_col * tile_cols, 8)
        row_slice = pl.ds(row_start, tile_rows)
        col_slice = pl.ds(col_start, tile_cols)
        near = distance_ref[chip_step, col_slice, :]
        spread = jnp.stack(
            [jnp.broadcast_to(near[:, i : i + 1], (tile_cols, width)) for i in range(tile_rows)]
        )
        scaled = (spread - centers) * (1.0 / step_size)
        basis = jnp.exp(-scaled * scaled).astype(jnp.bfloat16)
        pair = (
            pack[0:pairs, :].astype(jnp.float32).reshape(tile)
            + rows_ref[row_slice, :][:, None, :]
            + cols_ref[col_slice, :][None]
        )
        pair = pair.reshape(pairs, width) + jnp.dot(
            basis.reshape(pairs, width), w_dist, preferred_element_type=jnp.float32
        )
        spread_keys(pair_ref, at_chip, at_col, half, pair.reshape(tile))
        normed = layer_norm(pair).astype(jnp.bfloat16)
        normed_ref[at_chip, :, at_col] = normed.reshape(tile)
        projected = jnp.dot(normed, tri_in, preferred_element_type=jnp.float32)
        right = gated(
            projected[:, 0:width].reshape(tile),
            projected[:, width : 2 * width].reshape(tile),
            half_mask(limit, row_start, col_start, tile),
        )
        right_ref[at_chip, :, at_col] = right.astype(jnp.bfloat16)


def left_kernel(
    normed_ref, right_ref, tri_in_ref, mask_ref, turned_ref, keys_ref, gating_ref, left_ref
):
    chips, tile_rows, col_count, tile_cols, width = normed_ref.shape
    tokens = col_count * tile_cols
    _, half, _ = place_of()
    step = turned_ref.shape[0] // (chips * tile_rows)
    limit = token_count(mask_ref).astype(jnp.int32)
    pairs = tile_rows * tile_cols
    tile = (tile_rows, tile_cols, width)
    tri_in = jnp.concatenate([tri_in_ref[:, 0 : 2 * width], tri_in_ref[:, 4 * width :]], axis=1)
    for at_chip in range(chips):
        for at_col in range(col_count):
            normed = normed_ref[at_chip, :, at_col].reshape(pairs, width)
            projected = jnp.dot(normed, tri_in, preferred_element_type=jnp.float32)
            left_ref[:, at_col * tile_cols : (at_col + 1) * tile_cols, :] = gated(
                projected[:, 0:width].reshape(tile),
                projected[:, width : 2 * width].reshape(tile),
                half_mask(limit, (2 * at_chip + half) * tile_rows, at_col * tile_cols, tile),
            )
            spread_keys(
                gating_ref, at_chip, at_col, half, sigmoid(projected[:, 2 * width :]).reshape(tile)
            )
        for i in range(tile_rows):
            rows = pl.ds((at_chip * tile_rows + i) * step, width)
            turned_ref[rows, :] = left_ref[i].T
            key = right_ref[at_chip, i].reshape(tokens, width).astype(jnp.float32)
            keys_ref[rows, :] = key.T


def triangle_kernel(
    left_ref,
    mine_ref,
    other_ref,
    pair_ref,
    gating_ref,
    tri_out_ref,
    mask_ref,
    pooled_ref,
    own_ref,
    keys_ref,
    outer_ref,
    updated_ref,
):
    chips, tile_rows, _, _, _, width = pair_ref.shape
    tokens = 2 * chips * tile_rows
    queries = chips * tile_rows
    step = keys_ref.shape[0] // queries
    chip, half, _ = place_of()
    for at_chip in range(chips):
        for i in range(tile_rows):
            key = other_ref[at_chip, i].reshape(tokens, width).astype(jnp.float32)
            keys_ref[pl.ds((at_chip * tile_rows + i) * step, width), :] = key.T
    for channel in range(width):
        rows = pl.ds(channel, queries, stride=step)
        query = left_ref[rows, :].astype(jnp.bfloat16)
        key = jnp.concatenate([mine_ref[rows, :], keys_ref[rows, :]], axis=0)
        outer_ref[rows, :] = lax.dot_general(
            query,
            key.astype(jnp.bfloat16),
            (((1,), (1,)), ((), ())),
            preferred_element_type=jnp.float32,
        )
    place = lax.broadcasted_iota(jnp.int32, (tokens, width), 0)
    key_half = jnp.where(place < queries, half, 1 - half)
    place = jnp.where(place < queries, place, place - queries)
    token = 2 * place - lax.rem(place, tile_rows) + key_half * tile_rows
    real = jnp.where(token < token_count(mask_ref).astype(jnp.int32), 1.0, 0.0)
    tri_out = tri_out_ref[...]
    for at_chip in range(chips):
        outer = jnp.concatenate(
            [
                outer_ref[pl.ds((at_chip * tile_rows + i) * step, width), :].T
                for i in range(tile_rows)
            ],
            axis=0,
        )
        change = jnp.dot(
            layer_norm(outer).astype(jnp.bfloat16), tri_out, preferred_element_type=jnp.float32
        )
        for i in range(tile_rows):
            gating = gating_ref[at_chip, i].reshape(tokens, width)
            updated = pair_ref[at_chip, i].reshape(tokens, width) + gating * (
                change[i * tokens : (i + 1) * tokens]
            )
            updated_ref[at_chip, i] = updated.reshape(2, chips, tile_rows, width)
            row = at_chip * tile_rows + i
            pooled_ref[row : row + 1, :] = jnp.sum(updated * real, axis=0, keepdims=True)
    own_ref[:, :, half] = updated_ref[chip, :, 0]
    own_ref[:, :, 1 - half] = updated_ref[chip, :, 1]


def score_kernel(
    tm_scale, col_count, own_ref, pae_w_ref, mask_ref, chain_ref, aligned_ref, interface_ref
):
    tile_rows, tile_cols = aligned_ref.shape
    tokens = chain_ref.shape[1]
    chip, half, col = place_of()
    bins = pae_w_ref.shape[0]
    logits = lax.dot_general(
        pae_w_ref[...],
        own_ref[...].reshape(tile_rows * tokens, own_ref.shape[-1]).astype(jnp.bfloat16),
        (((1,), (1,)), ((), ())),
        preferred_element_type=jnp.float32,
    )
    centers = 0.5 * (lax.broadcasted_iota(jnp.int32, (bins, 1), 0).astype(jnp.float32) + 0.5)
    ratio = centers / tm_scale
    weight = jnp.exp(logits - jnp.max(logits, axis=0, keepdims=True))
    total = jnp.sum(weight, axis=0, keepdims=True)
    error = jnp.sum(weight * centers, axis=0, keepdims=True) / total
    tm_pair = jnp.sum(weight * (1.0 / (1.0 + ratio * ratio)), axis=0, keepdims=True) / total
    chains = chain_ref[...]
    keys = lax.broadcasted_iota(jnp.int32, (1, tokens), 1)
    limit = token_count(mask_ref).astype(jnp.int32)
    places = lax.broadcasted_iota(jnp.int32, (1, tile_rows), 1)
    scores = jnp.zeros((1, tile_rows), jnp.float32)
    query = (2 * chip + half) * tile_rows
    for i in range(tile_rows):
        span = error[:, i * tokens : (i + 1) * tokens]
        mine = span[:, 0:tile_cols]
        for other in range(1, col_count):
            mine = jnp.where(
                col == other, span[:, other * tile_cols : (other + 1) * tile_cols], mine
            )
        aligned_ref[i : i + 1, :] = mine
        own_chain = jnp.sum(
            jnp.where(keys == query + i, chains, 0).astype(jnp.float32), axis=1, keepdims=True
        ).astype(jnp.int32)
        face = (keys < limit) & (query + i < limit) & (chains != own_chain)
        face = jnp.where(face, 1.0, 0.0)
        number = jnp.sum(face, axis=1, keepdims=True)
        score = jnp.sum(face * tm_pair[:, i * tokens : (i + 1) * tokens], axis=1, keepdims=True)
        scores = jnp.where(places == i, score / jnp.maximum(number, 1.0), scores)
    interface_ref[...] = scores


def atom_kernel(
    mine_ref,
    other_ref,
    single_ref,
    mask_ref,
    pool_w_ref,
    plddt_w_ref,
    atom_token_ref,
    atom_part_ref,
    out_ref,
    pooled_ref,
):
    chips, _, tile_rows, width = pooled_ref.shape
    tokens = single_ref.shape[0]
    half = lax.rem(lax.axis_index("row"), 2)
    pooled_ref[:, half] = mine_ref[...].reshape(chips, tile_rows, width)
    pooled_ref[:, 1 - half] = other_ref[...].reshape(chips, tile_rows, width)
    pooled = pooled_ref[...].reshape(tokens, width) / token_count(mask_ref)
    atoms = atom_token_ref.shape[1]
    order = lax.broadcasted_iota(jnp.int32, (tokens, atoms), 0)
    chosen = (order == atom_token_ref[...]).astype(jnp.float32).astype(jnp.bfloat16)
    turned = (((0,), (0,)), ((), ()))
    pooled = lax.dot_general(
        chosen, pooled.astype(jnp.bfloat16), turned, preferred_element_type=jnp.float32
    )
    picked = lax.dot_general(chosen, single_ref[...], turned, preferred_element_type=jnp.float32)
    picked = layer_norm(
        picked
        + jnp.dot(
            pooled.astype(jnp.bfloat16), pool_w_ref[...], preferred_element_type=jnp.float32
        )
    ).astype(jnp.bfloat16)
    logits = (
        lax.dot_general(
            plddt_w_ref[...], picked, (((1,), (1,)), ((), ())), preferred_element_type=jnp.float32
        )
        + atom_part_ref[...]
    )
    bins = logits.shape[0]
    centers = (lax.broadcasted_iota(jnp.int32, (bins, 1), 0).astype(jnp.float32) + 0.5) / bins
    weight = jnp.exp(logits - jnp.max(logits, axis=0, keepdims=True))
    total = jnp.sum(weight, axis=0, keepdims=True)
    out_ref[...] = jnp.sum(weight * centers, axis=0, keepdims=True) / total


def direct(
    z_trunk,
    single,
    atom_coords,
    atom_single,
    rep_atom,
    atom_token,
    token_mask,
    chain_id,
    w_left,
    w_right,
    w_dist,
    tri_in,
    tri_out,
    pae_w,
    pool_w,
    plddt_w,
    atom_w,
):
    tile_rows, tile_cols, width = z_trunk.shape
    tokens = single.shape[0]
    atoms = atom_coords.shape[1]
    fits = 2 * atoms <= width and tile_cols % (2 * tile_rows) == 0 and tile_rows % 8 == 0
    if tokens * tokens * width * 4 > WHOLE_PAIR_BYTES or not fits:
        return per_device(
            z_trunk, single, atom_coords, atom_single, rep_atom, atom_token, token_mask, chain_id,
            w_left, w_right, w_dist, tri_in, tri_out, pae_w, pool_w, plddt_w, atom_w,
        )
    row_count = lax.axis_size("row")
    col_count = lax.axis_size("col")
    chips = row_count // 2
    float32, bfloat16 = jnp.float32, jnp.bfloat16

    def across(values, axis, count, step):
        return lax.ppermute(values, axis, [(i, i ^ step) for i in range(count)])

    def partner(values):
        return across(values, "row", row_count, 1)

    block = pltpu.VMEM((tile_rows * tile_cols + 16, width), bfloat16)
    fetched, coords = run(
        fetch_kernel,
        "fetch",
        (block, pltpu.VMEM((3, atoms), float32)),
        (z_trunk.reshape(tile_rows * tile_cols, width), atom_coords),
        0,
        scratch=(pltpu.SemaphoreType.DMA((2,)),),
    )
    packed = run(
        pack_kernel, "pack", block, (fetched, coords, partner(atom_coords)), aliases={0: 0}
    )
    slots = [(i, j) for i in range(chips) for j in range(col_count)]
    along = [packed] + [across(packed, "row", row_count, 2 * i) for i in range(1, chips)]
    beside = [packed] + [across(packed, "col", col_count, j) for j in range(1, col_count)]

    def pack_of(i, j):
        if i == 0 or j == 0:
            return beside[j] if i == 0 else along[i]
        if i < chips - 1:
            return across(beside[j], "row", row_count, 2 * i)
        return across(along[i], "col", col_count, j)

    packs = [pack_of(i, j) for i, j in slots]
    raw = (w_left, w_right, w_dist, atom_single, atom_w.T)
    kept = (
        single, tri_in, tri_out, pae_w.T, pool_w, plddt_w.T, rep_atom.reshape(1, tokens),
        token_mask.reshape(1, tokens), chain_id.reshape(1, tokens), atom_token.reshape(1, atoms),
    )
    rows, cols, dist, atom_part, *kept = run(
        lambda *refs: prepare_kernel(len(kept), *refs),
        "prepare",
        (
            pltpu.VMEM((tokens, width), float32),
            pltpu.VMEM((tokens, width), float32),
            pltpu.VMEM((width, width), float32),
            pltpu.VMEM((plddt_w.shape[1], atoms), float32),
            *[pltpu.VMEM(value.shape, value.dtype) for value in kept],
        ),
        (packed, *raw, *kept),
        1,
        scratch=(
            *[pltpu.VMEM(value.shape, value.dtype) for value in raw],
            pltpu.SemaphoreType.DMA((len(raw) + len(kept),)),
        ),
    )
    single, tri_in, tri_out, pae_w, pool_w, plddt_w, rep, mask, chain, atom_token = kept
    full = (chips, tile_rows, col_count, tile_cols, width)
    by_half = pltpu.VMEM((chips, tile_rows, 2, chips, tile_rows, width), float32)
    pair, normed, right = run(
        lambda *refs: edge_kernel(slots, col_count, atoms, w_dist.shape[0], *refs),
        "edges",
        (by_half, pltpu.VMEM(full, bfloat16), pltpu.VMEM(full, bfloat16)),
        (*packs, rows, cols, dist, rep, mask, tri_in),
        scratch=(pltpu.VMEM((chips, tokens, width), float32),),
    )
    turned = pltpu.VMEM((chips * tile_rows * (width + SPREAD), tokens), float32)
    left, keys, gating = run(
        left_kernel,
        "left",
        (turned, turned, by_half),
        (normed, right, tri_in, mask),
        scratch=(pltpu.VMEM((tile_rows, tokens, width), float32),),
    )
    pooled, own = run(
        triangle_kernel,
        "triangle",
        (
            pltpu.VMEM((chips * tile_rows, width), float32),
            pltpu.VMEM((tile_rows, chips, 2, tile_rows, width), float32),
        ),
        (left, keys, partner(right), pair, gating, tri_out, mask),
        scratch=(turned, turned, by_half),
    )
    tm_scale = 1.24 * (max(tokens, 19) - 15) ** (1.0 / 3.0) - 1.8
    aligned_error, interface_score = run(
        lambda *refs: score_kernel(tm_scale, col_count, *refs),
        "scores",
        (
            jax.ShapeDtypeStruct((tile_rows, tile_cols), float32),
            jax.ShapeDtypeStruct((1, tile_rows), float32),
        ),
        (own, pae_w, mask, chain),
    )
    atom_confidence = run(
        atom_kernel,
        "atoms",
        jax.ShapeDtypeStruct((1, atoms), float32),
        (pooled, partner(pooled), single, mask, pool_w, plddt_w, atom_token, atom_part),
        scratch=(pltpu.VMEM((chips, 2, tile_rows, width), float32),),
    )
    return (aligned_error, interface_score.reshape(tile_rows), atom_confidence.reshape(atoms))


def gathers_whole(mesh):
    row_count, col_count = mesh.shape["row"], mesh.shape["col"]
    power = all(count & (count - 1) == 0 for count in (row_count, col_count))
    return power and row_count > 1 and mesh.shape["ch"] == 1


def solution(mesh):
    placed = (
        P(("parts", "row"), ("col", "ch"), None),
        P("parts", None),
        P(None, ("parts", "row", "col", "ch")),
        P(("parts", "row", "col", "ch"), None),
        P("parts"),
        P(("parts", "row", "col", "ch")),
        P("parts"),
        P("parts"),
        P(),
        P(),
        P(),
        P(),
        P(),
        P(),
        P(),
        P(),
        P(),
    )
    return jax.shard_map(
        direct if gathers_whole(mesh) else per_device,
        mesh=mesh,
        in_specs=placed,
        out_specs=(
            P(("parts", "row"), ("col", "ch")),
            P(("parts", "row")),
            P(("parts", "row", "col", "ch")),
        ),
        check_vma=False,
    )
```

```python
import jax
import jax.numpy as jnp
from jax import lax
from jax.experimental import pallas as pl
from jax.experimental.pallas import tpu as pltpu
from jax.sharding import PartitionSpec as P

EPSILON = 1e-05


def layer_norm(values):
    center = values - jnp.mean(values, axis=-1, keepdims=True)
    spread = jnp.mean(center * center, axis=-1, keepdims=True)
    return center * lax.rsqrt(spread + EPSILON)


def distance_basis(distance, count):
    step_size = 18.0 / (count - 1)
    centers = 3.375 + step_size * jnp.arange(count, dtype=jnp.float32)
    scaled = (distance[..., None] - centers) / step_size
    return jnp.exp(-scaled * scaled)


def bin_average(logits, centers):
    probability = jax.nn.softmax(logits, axis=-1)
    return jnp.sum(probability * centers, axis=-1)


def per_device(
    z_trunk,
    single,
    atom_coords,
    atom_single,
    rep_atom,
    atom_token,
    token_mask,
    chain_id,
    w_left,
    w_right,
    w_dist,
    tri_in,
    tri_out,
    pae_w,
    pool_w,
    plddt_w,
    atom_w,
):
    tile_rows, tile_cols, pair_width = z_trunk.shape
    tokens = single.shape[0]
    col_index = lax.axis_index("col") * lax.axis_size("ch") + lax.axis_index("ch")
    row_start = lax.axis_index("row") * tile_rows
    col_start = col_index * tile_cols
    wanted = jnp.concatenate(
        [
            lax.dynamic_slice_in_dim(rep_atom, row_start, tile_rows),
            lax.dynamic_slice_in_dim(rep_atom, col_start, tile_cols),
        ]
    )
    shard_piece = lax.all_gather(atom_coords, ("row", "col", "ch"), axis=1, tiled=True)
    places = lax.iota(jnp.int32, shard_piece.shape[1])
    selector = (places[:, None] == wanted[None, :]).astype(jnp.float32)
    coords = jnp.dot(
        shard_piece, selector, precision=lax.Precision.HIGHEST, preferred_element_type=jnp.float32
    )
    offset = coords[:, :tile_rows, None] - coords[:, None, tile_rows:]
    distance = jnp.sqrt(jnp.sum(offset * offset, axis=0))
    basis_count = w_dist.shape[0]
    radial_basis = distance_basis(distance, basis_count).astype(jnp.bfloat16)
    embedded = jnp.dot(
        radial_basis.reshape(-1, basis_count), w_dist, preferred_element_type=jnp.float32
    ).reshape(tile_rows, tile_cols, pair_width)
    row_single = lax.dynamic_slice_in_dim(single, row_start, tile_rows)
    col_single = lax.dynamic_slice_in_dim(single, col_start, tile_cols)
    from_rows = jnp.dot(row_single, w_left, preferred_element_type=jnp.float32)
    from_cols = jnp.dot(col_single, w_right, preferred_element_type=jnp.float32)
    pair_rep = (
        z_trunk.astype(jnp.float32) + from_rows[:, None, :] + from_cols[None, :, :] + embedded
    )
    mask_float = token_mask.astype(jnp.float32)
    row_mask = lax.dynamic_slice_in_dim(mask_float, row_start, tile_rows)
    col_mask = lax.dynamic_slice_in_dim(mask_float, col_start, tile_cols)
    pair_mask = row_mask[:, None] * col_mask[None, :]
    normed = layer_norm(pair_rep).astype(jnp.bfloat16)
    projected = jnp.dot(
        normed.reshape(-1, pair_width), tri_in, preferred_element_type=jnp.float32
    ).reshape(tile_rows, tile_cols, 5 * pair_width)
    left_side = (
        jax.nn.sigmoid(projected[..., 0:pair_width])
        * projected[..., pair_width : 2 * pair_width]
        * pair_mask[..., None]
    ).astype(jnp.bfloat16)
    right_side = (
        jax.nn.sigmoid(projected[..., 2 * pair_width : 3 * pair_width])
        * projected[..., 3 * pair_width : 4 * pair_width]
        * pair_mask[..., None]
    ).astype(jnp.bfloat16)
    gating = jax.nn.sigmoid(projected[..., 4 * pair_width : 5 * pair_width])
    partial_terms = jnp.einsum(
        "ikc,jkc->ijc",
        left_side,
        lax.all_gather(right_side, "row", axis=0, tiled=True),
        preferred_element_type=jnp.float32,
    )
    product_sum = lax.psum_scatter(partial_terms, ("col", "ch"), scatter_dimension=1, tiled=True)
    normed_outer = layer_norm(product_sum).astype(jnp.bfloat16)
    updated = pair_rep + gating * jnp.dot(
        normed_outer.reshape(-1, pair_width), tri_out, preferred_element_type=jnp.float32
    ).reshape(tile_rows, tile_cols, pair_width)
    bins_pae = pae_w.shape[1]
    pae_logits = jnp.dot(
        updated.astype(jnp.bfloat16).reshape(-1, pair_width),
        pae_w,
        preferred_element_type=jnp.float32,
    ).reshape(tile_rows, tile_cols, bins_pae)
    pae_centers = 0.5 * (jnp.arange(bins_pae, dtype=jnp.float32) + 0.5)
    probability = jax.nn.softmax(pae_logits, axis=-1)
    aligned_error = jnp.sum(probability * pae_centers, axis=-1)
    tm_scale = 1.24 * (max(tokens, 19) - 15) ** (1.0 / 3.0) - 1.8
    tm_values = 1.0 / (1.0 + (pae_centers / tm_scale) ** 2)
    tm_pair = jnp.sum(probability * tm_values, axis=-1)
    row_chain = lax.dynamic_slice_in_dim(chain_id, row_start, tile_rows)
    col_chain = lax.dynamic_slice_in_dim(chain_id, col_start, tile_cols)
    interface = pair_mask * (row_chain[:, None] != col_chain[None, :]).astype(jnp.float32)
    numerator_part = jnp.sum(interface * tm_pair, axis=1)
    count_part = jnp.sum(interface, axis=1)
    pooled_part = jnp.sum(col_mask[None, :, None] * updated, axis=1)
    numerator, count_total, pooled = lax.psum(
        (numerator_part, count_part, pooled_part), ("col", "ch")
    )
    interface_score = numerator / jnp.maximum(count_total, 1.0)
    pooled = pooled / jnp.sum(mask_float)
    single_new = row_single.astype(jnp.float32) + jnp.dot(
        pooled.astype(jnp.bfloat16), pool_w, preferred_element_type=jnp.float32
    )
    single_norm = layer_norm(single_new).astype(jnp.bfloat16)
    bins_plddt = plddt_w.shape[1]
    shard_piece = lax.all_gather(single_norm, "row", axis=0, tiled=True)
    places = lax.iota(jnp.int32, shard_piece.shape[0])
    selector = (atom_token[:, None] == places[None, :]).astype(jnp.bfloat16)
    picked = jnp.dot(selector, shard_piece, preferred_element_type=jnp.float32)
    atom_logits = jnp.dot(picked.astype(jnp.bfloat16), plddt_w, preferred_element_type=jnp.float32)
    atom_logits = atom_logits + jnp.dot(atom_single, atom_w, preferred_element_type=jnp.float32)
    plddt_centers = (jnp.arange(bins_plddt, dtype=jnp.float32) + 0.5) / bins_plddt
    atom_confidence = bin_average(atom_logits, plddt_centers)
    return (aligned_error, interface_score, atom_confidence)


WHOLE_PAIR_BYTES = 4 * 1024 * 1024
SPREAD = 1
SCOPED_BYTES = 16 * 1024 * 1024
VMEM = pl.BlockSpec(memory_space=pltpu.VMEM)


HBM = pl.BlockSpec(memory_space=pltpu.HBM)


def run(kernel, name, out_shapes, arguments, held=None, scratch=(), aliases=None):
    held = len(arguments) if held is None else held
    spaces = [pltpu.VMEM] * held + [pltpu.HBM] * (len(arguments) - held)
    return pl.pallas_call(
        kernel,
        out_shape=out_shapes,
        in_specs=[VMEM] * held + [HBM] * (len(arguments) - held),
        out_specs=(VMEM,) * len(out_shapes) if isinstance(out_shapes, tuple) else VMEM,
        scratch_shapes=list(scratch),
        input_output_aliases=aliases or {},
        compiler_params=pltpu.CompilerParams(vmem_limit_bytes=SCOPED_BYTES),
        name=name,
    )(*map(pltpu.with_memory_space_constraint, arguments, spaces))


def bring(sources, targets, arrived):
    copies = [
        pltpu.make_async_copy(source, target, arrived.at[place])
        for place, (source, target) in enumerate(zip(sources, targets))
    ]
    for copy in copies:
        copy.start()
    for copy in copies:
        copy.wait()


def sigmoid(values):
    return 0.5 * jnp.tanh(0.5 * values) + 0.5


def gated(gates, values, half_mask):
    return (jnp.tanh(0.5 * gates) + 1.0) * values * half_mask


def place_of():
    row = lax.axis_index("row")
    return lax.div(row, 2), lax.rem(row, 2), lax.axis_index("col")


def token_count(mask_ref):
    return jnp.sum(mask_ref[...].astype(jnp.float32), axis=1, keepdims=True)


def half_mask(limit, row_start, col_start, shape):
    rows, cols, width = shape
    places = lax.broadcasted_iota(jnp.int32, (cols, width), 0) + col_start
    keys = jnp.where(places < limit, 0.5, 0.0)
    return jnp.stack([jnp.where(row_start + i < limit, keys, 0.0) for i in range(rows)])


def spread_keys(target, at_chip, at_col, half, tile):
    rows, cols, _ = tile.shape
    for group in range(cols // rows):
        chip = at_col * (cols // (2 * rows)) + group // 2
        target[at_chip, :, (group % 2) ^ half, chip] = tile[:, group * rows : (group + 1) * rows]


def fetch_kernel(z_ref, coords_ref, out_ref, coords_out_ref, arrived):
    pairs = z_ref.shape[0]
    bring((z_ref, coords_ref), (out_ref.at[0:pairs, :], coords_out_ref), arrived)
    out_ref[pairs:, :] = jnp.zeros_like(out_ref[pairs:, :])


def pack_kernel(packed_ref, mine_ref, other_ref, out_ref):
    del packed_ref
    width = out_ref.shape[1]
    atoms = mine_ref.shape[1]
    first = lax.rem(lax.axis_index("row"), 2) == 0
    mine, other = mine_ref[...], other_ref[...]
    value = jnp.concatenate(
        [jnp.where(first, mine, other), jnp.where(first, other, mine)], axis=1
    )
    high = value.astype(jnp.bfloat16).astype(jnp.float32)
    middle = (value - high).astype(jnp.bfloat16).astype(jnp.float32)
    low = value - high - middle
    stacked = jnp.concatenate([high, middle, low, jnp.zeros((7, 2 * atoms), jnp.float32)], axis=0)
    filler = jnp.zeros((16, width - 2 * atoms), jnp.float32)
    out_ref[out_ref.shape[0] - 16 :, :] = jnp.concatenate([stacked, filler], axis=1).astype(
        jnp.bfloat16
    )


def prepare_kernel(slots, col_count, atoms, copied, *refs):
    raw = refs[1:6]
    sources = refs[6 : 6 + copied]
    rows_ref, cols_ref, dist_ref, atom_part_ref, chosen_ref, turned_ref = refs[
        6 + copied : 12 + copied
    ]
    targets = refs[12 + copied : 12 + 2 * copied]
    w_left_ref, w_right_ref, w_dist_ref, atom_single_ref, atom_w_ref, arrived = refs[
        12 + 2 * copied :
    ]
    landing = (w_left_ref, w_right_ref, w_dist_ref, atom_single_ref, atom_w_ref)
    bring((*raw, *sources), (*landing, *targets), arrived)
    single, rep = targets[0][...], targets[-1][...]
    chip, _, col = place_of()
    order = lax.broadcasted_iota(jnp.int32, chosen_ref.shape[1:], 0)
    for place, (chip_step, col_step) in enumerate(slots):
        device = 2 * (chip ^ chip_step) * col_count + (col ^ col_step)
        number = jnp.where(
            order < atoms, order + device * atoms, order - atoms + (device + col_count) * atoms
        )
        chosen = (number == rep).astype(jnp.float32)
        chosen_ref[place] = chosen.astype(jnp.bfloat16)
        turned_ref[place] = chosen.T.astype(jnp.bfloat16)
    rows_ref[...] = jnp.dot(single, w_left_ref[...], preferred_element_type=jnp.float32)
    cols_ref[...] = jnp.dot(single, w_right_ref[...], preferred_element_type=jnp.float32)
    dist_ref[...] = jnp.zeros_like(dist_ref)
    dist_ref[0 : w_dist_ref.shape[0], :] = w_dist_ref[...].astype(jnp.float32)
    atom_part_ref[...] = lax.dot_general(
        atom_w_ref[...],
        atom_single_ref[...],
        (((1,), (1,)), ((), ())),
        preferred_element_type=jnp.float32,
    )


def edge_kernel(slots, basis_count, *refs):
    packs = refs[: len(slots)]
    rows_ref, cols_ref, dist_ref, chosen_ref, turned_ref, mask_ref, tri_in_ref = refs[
        len(slots) : len(slots) + 7
    ]
    pair_ref, normed_ref, right_ref, distance_ref = refs[len(slots) + 7 :]
    _, tile_rows, _, tile_cols, width = normed_ref.shape
    tokens = rows_ref.shape[0]
    pairs = tile_rows * tile_cols
    chip, half, col = place_of()
    w_dist = dist_ref[...].astype(jnp.bfloat16)
    across = jnp.zeros((16, tokens), jnp.float32)
    picked = jnp.zeros((tokens, 16), jnp.float32)
    for place, pack in enumerate(packs):
        pieces = pack[pairs:, :]
        across = across + jnp.dot(
            pieces, chosen_ref[place], preferred_element_type=jnp.float32
        )
        picked = picked + lax.dot_general(
            turned_ref[place], pieces, (((1,), (1,)), ((), ())), preferred_element_type=jnp.float32
        )
    square = jnp.zeros((tokens, width), jnp.float32)
    for axis in range(3):
        down = picked[:, axis : axis + 1] + picked[:, axis + 3 : axis + 4]
        down = down + picked[:, axis + 6 : axis + 7]
        along = across[axis : axis + 1] + across[axis + 3 : axis + 4] + across[axis + 6 : axis + 7]
        along = jnp.concatenate([along, jnp.zeros((1, width - tokens), jnp.float32)], axis=1)
        gap = down - along
        square = square + gap * gap
    distance = jnp.sqrt(square)
    for chip_step in range(pair_ref.shape[0]):
        first = (2 * (chip ^ chip_step) + half) * tile_rows
        distance_ref[chip_step] = pltpu.roll(distance, lax.rem(width - first, width), 1)
    step_size = 18.0 / (basis_count - 1)
    centers = 3.375 + step_size * lax.broadcasted_iota(jnp.int32, (1, 1, width), 2).astype(
        jnp.float32
    )
    limit = token_count(mask_ref).astype(jnp.int32)
    tile = (tile_rows, tile_cols, width)
    tri_in = tri_in_ref[:, 2 * width : 4 * width]
    for pack, (chip_step, col_step) in zip(packs, slots):
        at_chip = chip ^ chip_step
        at_col = col ^ col_step
        row_start = pl.multiple_of((2 * at_chip + half) * tile_rows, 8)
        col_start = pl.multiple_of(at_col * tile_cols, 8)
        row_slice = pl.ds(row_start, tile_rows)
        col_slice = pl.ds(col_start, tile_cols)
        near = distance_ref[chip_step, col_slice, :]
        spread = jnp.stack(
            [jnp.broadcast_to(near[:, i : i + 1], (tile_cols, width)) for i in range(tile_rows)]
        )
        scaled = (spread - centers) * (1.0 / step_size)
        basis = jnp.exp(-scaled * scaled).astype(jnp.bfloat16)
        pair = (
            pack[0:pairs, :].astype(jnp.float32).reshape(tile)
            + rows_ref[row_slice, :][:, None, :]
            + cols_ref[col_slice, :][None]
        )
        pair = pair.reshape(pairs, width) + jnp.dot(
            basis.reshape(pairs, width), w_dist, preferred_element_type=jnp.float32
        )
        spread_keys(pair_ref, at_chip, at_col, half, pair.reshape(tile))
        normed = layer_norm(pair).astype(jnp.bfloat16)
        normed_ref[at_chip, :, at_col] = normed.reshape(tile)
        projected = jnp.dot(normed, tri_in, preferred_element_type=jnp.float32)
        right = gated(
            projected[:, 0:width].reshape(tile),
            projected[:, width : 2 * width].reshape(tile),
            half_mask(limit, row_start, col_start, tile),
        )
        right_ref[at_chip, :, at_col] = right.astype(jnp.bfloat16)


def left_kernel(
    normed_ref, right_ref, tri_in_ref, mask_ref, turned_ref, keys_ref, gating_ref, left_ref
):
    chips, tile_rows, col_count, tile_cols, width = normed_ref.shape
    tokens = col_count * tile_cols
    _, half, _ = place_of()
    step = turned_ref.shape[0] // (chips * tile_rows)
    limit = token_count(mask_ref).astype(jnp.int32)
    pairs = tile_rows * tile_cols
    tile = (tile_rows, tile_cols, width)
    tri_in = jnp.concatenate([tri_in_ref[:, 0 : 2 * width], tri_in_ref[:, 4 * width :]], axis=1)
    for at_chip in range(chips):
        for at_col in range(col_count):
            normed = normed_ref[at_chip, :, at_col].reshape(pairs, width)
            projected = jnp.dot(normed, tri_in, preferred_element_type=jnp.float32)
            left_ref[:, at_col * tile_cols : (at_col + 1) * tile_cols, :] = gated(
                projected[:, 0:width].reshape(tile),
                projected[:, width : 2 * width].reshape(tile),
                half_mask(limit, (2 * at_chip + half) * tile_rows, at_col * tile_cols, tile),
            )
            spread_keys(
                gating_ref, at_chip, at_col, half, sigmoid(projected[:, 2 * width :]).reshape(tile)
            )
        for i in range(tile_rows):
            rows = pl.ds((at_chip * tile_rows + i) * step, width)
            turned_ref[rows, :] = left_ref[i].T
            key = right_ref[at_chip, i].reshape(tokens, width).astype(jnp.float32)
            keys_ref[rows, :] = key.T


def normed_columns(values):
    center = values - jnp.mean(values, axis=0, keepdims=True)
    spread = jnp.mean(center * center, axis=0, keepdims=True)
    return (center * lax.rsqrt(spread + EPSILON)).astype(jnp.bfloat16)


def triangle_kernel(
    left_ref,
    mine_ref,
    other_ref,
    pair_ref,
    gating_ref,
    tri_out_ref,
    mask_ref,
    pooled_ref,
    own_ref,
    keys_ref,
    outer_ref,
    updated_ref,
):
    chips, tile_rows, _, _, _, width = pair_ref.shape
    tokens = 2 * chips * tile_rows
    queries = chips * tile_rows
    step = keys_ref.shape[0] // queries
    chip, half, _ = place_of()
    for at_chip in range(chips):
        for i in range(tile_rows):
            key = other_ref[at_chip, i].reshape(tokens, width).astype(jnp.float32)
            keys_ref[pl.ds((at_chip * tile_rows + i) * step, width), :] = key.T
    for channel in range(width):
        rows = pl.ds(channel, queries, stride=step)
        query = left_ref[rows, :].astype(jnp.bfloat16)
        key = jnp.concatenate([mine_ref[rows, :], keys_ref[rows, :]], axis=0)
        outer_ref[rows, :] = lax.dot_general(
            query,
            key.astype(jnp.bfloat16),
            (((1,), (1,)), ((), ())),
            preferred_element_type=jnp.float32,
        )
    place = lax.broadcasted_iota(jnp.int32, (tokens, width), 0)
    key_half = jnp.where(place < queries, half, 1 - half)
    place = jnp.where(place < queries, place, place - queries)
    token = 2 * place - lax.rem(place, tile_rows) + key_half * tile_rows
    real = jnp.where(token < token_count(mask_ref).astype(jnp.int32), 1.0, 0.0)
    tri_out = tri_out_ref[...]
    for at_chip in range(chips):
        change = jnp.dot(
            jnp.concatenate(
                [
                    normed_columns(
                        outer_ref[pl.ds((at_chip * tile_rows + i) * step, width), :]
                    ).T
                    for i in range(tile_rows)
                ],
                axis=0,
            ),
            tri_out,
            preferred_element_type=jnp.float32,
        )
        for i in range(tile_rows):
            gating = gating_ref[at_chip, i].reshape(tokens, width)
            updated = pair_ref[at_chip, i].reshape(tokens, width) + gating * (
                change[i * tokens : (i + 1) * tokens]
            )
            updated_ref[at_chip, i] = updated.reshape(2, chips, tile_rows, width)
            row = at_chip * tile_rows + i
            pooled_ref[row : row + 1, :] = jnp.sum(updated * real, axis=0, keepdims=True)
    own_ref[:, :, half] = updated_ref[chip, :, 0]
    own_ref[:, :, 1 - half] = updated_ref[chip, :, 1]


def score_kernel(
    tm_scale, col_count, own_ref, pae_w_ref, mask_ref, chain_ref, aligned_ref, interface_ref
):
    tile_rows, tile_cols = aligned_ref.shape
    tokens = chain_ref.shape[1]
    chip, half, col = place_of()
    bins = pae_w_ref.shape[0]
    logits = lax.dot_general(
        pae_w_ref[...],
        own_ref[...].reshape(tile_rows * tokens, own_ref.shape[-1]).astype(jnp.bfloat16),
        (((1,), (1,)), ((), ())),
        preferred_element_type=jnp.float32,
    )
    centers = 0.5 * (lax.broadcasted_iota(jnp.int32, (bins, 1), 0).astype(jnp.float32) + 0.5)
    ratio = centers / tm_scale
    weight = jnp.exp(logits - jnp.max(logits, axis=0, keepdims=True))
    total = jnp.sum(weight, axis=0, keepdims=True)
    error = jnp.sum(weight * centers, axis=0, keepdims=True) / total
    tm_pair = jnp.sum(weight * (1.0 / (1.0 + ratio * ratio)), axis=0, keepdims=True) / total
    chains = chain_ref[...]
    keys = lax.broadcasted_iota(jnp.int32, (1, tokens), 1)
    limit = token_count(mask_ref).astype(jnp.int32)
    places = lax.broadcasted_iota(jnp.int32, (1, tile_rows), 1)
    scores = jnp.zeros((1, tile_rows), jnp.float32)
    query = (2 * chip + half) * tile_rows
    for i in range(tile_rows):
        span = error[:, i * tokens : (i + 1) * tokens]
        mine = span[:, 0:tile_cols]
        for other in range(1, col_count):
            mine = jnp.where(
                col == other, span[:, other * tile_cols : (other + 1) * tile_cols], mine
            )
        aligned_ref[i : i + 1, :] = mine
        own_chain = jnp.sum(
            jnp.where(keys == query + i, chains, 0).astype(jnp.float32), axis=1, keepdims=True
        ).astype(jnp.int32)
        face = (keys < limit) & (query + i < limit) & (chains != own_chain)
        face = jnp.where(face, 1.0, 0.0)
        number = jnp.sum(face, axis=1, keepdims=True)
        score = jnp.sum(face * tm_pair[:, i * tokens : (i + 1) * tokens], axis=1, keepdims=True)
        scores = jnp.where(places == i, score / jnp.maximum(number, 1.0), scores)
    interface_ref[...] = scores


def atom_kernel(
    mine_ref,
    other_ref,
    single_ref,
    mask_ref,
    pool_w_ref,
    plddt_w_ref,
    atom_token_ref,
    atom_part_ref,
    out_ref,
    pooled_ref,
):
    chips, _, tile_rows, width = pooled_ref.shape
    tokens = single_ref.shape[0]
    half = lax.rem(lax.axis_index("row"), 2)
    pooled_ref[:, half] = mine_ref[...].reshape(chips, tile_rows, width)
    pooled_ref[:, 1 - half] = other_ref[...].reshape(chips, tile_rows, width)
    pooled = pooled_ref[...].reshape(tokens, width) / token_count(mask_ref)
    atoms = atom_token_ref.shape[1]
    order = lax.broadcasted_iota(jnp.int32, (tokens, atoms), 0)
    chosen = (order == atom_token_ref[...]).astype(jnp.float32).astype(jnp.bfloat16)
    turned = (((0,), (0,)), ((), ()))
    pooled = lax.dot_general(
        chosen, pooled.astype(jnp.bfloat16), turned, preferred_element_type=jnp.float32
    )
    picked = lax.dot_general(chosen, single_ref[...], turned, preferred_element_type=jnp.float32)
    picked = layer_norm(
        picked
        + jnp.dot(
            pooled.astype(jnp.bfloat16), pool_w_ref[...], preferred_element_type=jnp.float32
        )
    ).astype(jnp.bfloat16)
    logits = (
        lax.dot_general(
            plddt_w_ref[...], picked, (((1,), (1,)), ((), ())), preferred_element_type=jnp.float32
        )
        + atom_part_ref[...]
    )
    bins = logits.shape[0]
    centers = (lax.broadcasted_iota(jnp.int32, (bins, 1), 0).astype(jnp.float32) + 0.5) / bins
    weight = jnp.exp(logits - jnp.max(logits, axis=0, keepdims=True))
    total = jnp.sum(weight, axis=0, keepdims=True)
    out_ref[...] = jnp.sum(weight * centers, axis=0, keepdims=True) / total


def direct(
    z_trunk,
    single,
    atom_coords,
    atom_single,
    rep_atom,
    atom_token,
    token_mask,
    chain_id,
    w_left,
    w_right,
    w_dist,
    tri_in,
    tri_out,
    pae_w,
    pool_w,
    plddt_w,
    atom_w,
):
    tile_rows, tile_cols, width = z_trunk.shape
    tokens = single.shape[0]
    atoms = atom_coords.shape[1]
    fits = 2 * atoms <= width and tile_cols % (2 * tile_rows) == 0 and tile_rows % 8 == 0
    if tokens * tokens * width * 4 > WHOLE_PAIR_BYTES or not fits:
        return per_device(
            z_trunk, single, atom_coords, atom_single, rep_atom, atom_token, token_mask, chain_id,
            w_left, w_right, w_dist, tri_in, tri_out, pae_w, pool_w, plddt_w, atom_w,
        )
    row_count = lax.axis_size("row")
    col_count = lax.axis_size("col")
    chips = row_count // 2
    float32, bfloat16 = jnp.float32, jnp.bfloat16

    def across(values, axis, count, step):
        return lax.ppermute(values, axis, [(i, i ^ step) for i in range(count)])

    def partner(values):
        return across(values, "row", row_count, 1)

    block = pltpu.VMEM((tile_rows * tile_cols + 16, width), bfloat16)
    fetched, coords = run(
        fetch_kernel,
        "fetch",
        (block, pltpu.VMEM((3, atoms), float32)),
        (z_trunk.reshape(tile_rows * tile_cols, width), atom_coords),
        0,
        scratch=(pltpu.SemaphoreType.DMA((2,)),),
    )
    packed = run(
        pack_kernel, "pack", block, (fetched, coords, partner(atom_coords)), aliases={0: 0}
    )
    slots = [(i, j) for i in range(chips) for j in range(col_count)]
    along = [packed] + [across(packed, "row", row_count, 2 * i) for i in range(1, chips)]
    beside = [packed] + [across(packed, "col", col_count, j) for j in range(1, col_count)]

    def pack_of(i, j):
        if i == 0 or j == 0:
            return beside[j] if i == 0 else along[i]
        if i == 1:
            step = 2 * i * col_count + j
            return across(packed, ("row", "col"), row_count * col_count, step)
        return across(along[i], "col", col_count, j)

    packs = [pack_of(i, j) for i, j in slots]
    raw = (w_left, w_right, w_dist, atom_single, atom_w.T)
    kept = (
        single, tri_in, tri_out, pae_w.T, pool_w, plddt_w.T, token_mask.reshape(1, tokens),
        chain_id.reshape(1, tokens), atom_token.reshape(1, atoms), rep_atom.reshape(1, tokens),
    )
    rows, cols, dist, atom_part, chosen, turned, *kept = run(
        lambda *refs: prepare_kernel(slots, col_count, atoms, len(kept), *refs),
        "prepare",
        (
            pltpu.VMEM((tokens, width), float32),
            pltpu.VMEM((tokens, width), float32),
            pltpu.VMEM((width, width), float32),
            pltpu.VMEM((plddt_w.shape[1], atoms), float32),
            pltpu.VMEM((len(slots), width, tokens), bfloat16),
            pltpu.VMEM((len(slots), tokens, width), bfloat16),
            *[pltpu.VMEM(value.shape, value.dtype) for value in kept],
        ),
        (packed, *raw, *kept),
        1,
        scratch=(
            *[pltpu.VMEM(value.shape, value.dtype) for value in raw],
            pltpu.SemaphoreType.DMA((len(raw) + len(kept),)),
        ),
    )
    single, tri_in, tri_out, pae_w, pool_w, plddt_w, mask, chain, atom_token, _ = kept
    full = (chips, tile_rows, col_count, tile_cols, width)
    by_half = pltpu.VMEM((chips, tile_rows, 2, chips, tile_rows, width), float32)
    pair, normed, right = run(
        lambda *refs: edge_kernel(slots, w_dist.shape[0], *refs),
        "edges",
        (by_half, pltpu.VMEM(full, bfloat16), pltpu.VMEM(full, bfloat16)),
        (*packs, rows, cols, dist, chosen, turned, mask, tri_in),
        scratch=(pltpu.VMEM((chips, tokens, width), float32),),
    )
    turned = pltpu.VMEM((chips * tile_rows * (width + SPREAD), tokens), float32)
    left, keys, gating = run(
        left_kernel,
        "left",
        (turned, turned, by_half),
        (normed, right, tri_in, mask),
        scratch=(pltpu.VMEM((tile_rows, tokens, width), float32),),
    )
    pooled, own = run(
        triangle_kernel,
        "triangle",
        (
            pltpu.VMEM((chips * tile_rows, width), float32),
            pltpu.VMEM((tile_rows, chips, 2, tile_rows, width), float32),
        ),
        (left, keys, partner(right), pair, gating, tri_out, mask),
        scratch=(turned, turned, by_half),
    )
    tm_scale = 1.24 * (max(tokens, 19) - 15) ** (1.0 / 3.0) - 1.8
    aligned_error, interface_score = run(
        lambda *refs: score_kernel(tm_scale, col_count, *refs),
        "scores",
        (
            jax.ShapeDtypeStruct((tile_rows, tile_cols), float32),
            jax.ShapeDtypeStruct((1, tile_rows), float32),
        ),
        (own, pae_w, mask, chain),
    )
    atom_confidence = run(
        atom_kernel,
        "atoms",
        jax.ShapeDtypeStruct((1, atoms), float32),
        (pooled, partner(pooled), single, mask, pool_w, plddt_w, atom_token, atom_part),
        scratch=(pltpu.VMEM((chips, 2, tile_rows, width), float32),),
    )
    return (aligned_error, interface_score.reshape(tile_rows), atom_confidence.reshape(atoms))


def gathers_whole(mesh):
    row_count, col_count = mesh.shape["row"], mesh.shape["col"]
    power = all(count & (count - 1) == 0 for count in (row_count, col_count))
    return power and row_count > 1 and mesh.shape["ch"] == 1


def solution(mesh):
    placed = (
        P(("parts", "row"), ("col", "ch"), None),
        P("parts", None),
        P(None, ("parts", "row", "col", "ch")),
        P(("parts", "row", "col", "ch"), None),
        P("parts"),
        P(("parts", "row", "col", "ch")),
        P("parts"),
        P("parts"),
        P(),
        P(),
        P(),
        P(),
        P(),
        P(),
        P(),
        P(),
        P(),
    )
    return jax.shard_map(
        direct if gathers_whole(mesh) else per_device,
        mesh=mesh,
        in_specs=placed,
        out_specs=(
            P(("parts", "row"), ("col", "ch")),
            P(("parts", "row")),
            P(("parts", "row", "col", "ch")),
        ),
        check_vma=False,
    )
```

```python
import jax
import jax.numpy as jnp
from jax import lax
from jax.experimental import pallas as pl
from jax.experimental.pallas import tpu as pltpu
from jax.sharding import PartitionSpec as P

EPSILON = 1e-05


def layer_norm(values):
    center = values - jnp.mean(values, axis=-1, keepdims=True)
    spread = jnp.mean(center * center, axis=-1, keepdims=True)
    return center * lax.rsqrt(spread + EPSILON)


def distance_basis(distance, count):
    step_size = 18.0 / (count - 1)
    centers = 3.375 + step_size * jnp.arange(count, dtype=jnp.float32)
    scaled = (distance[..., None] - centers) / step_size
    return jnp.exp(-scaled * scaled)


def bin_average(logits, centers):
    probability = jax.nn.softmax(logits, axis=-1)
    return jnp.sum(probability * centers, axis=-1)


def per_device(
    z_trunk,
    single,
    atom_coords,
    atom_single,
    rep_atom,
    atom_token,
    token_mask,
    chain_id,
    w_left,
    w_right,
    w_dist,
    tri_in,
    tri_out,
    pae_w,
    pool_w,
    plddt_w,
    atom_w,
):
    tile_rows, tile_cols, pair_width = z_trunk.shape
    tokens = single.shape[0]
    col_index = lax.axis_index("col") * lax.axis_size("ch") + lax.axis_index("ch")
    row_start = lax.axis_index("row") * tile_rows
    col_start = col_index * tile_cols
    wanted = jnp.concatenate(
        [
            lax.dynamic_slice_in_dim(rep_atom, row_start, tile_rows),
            lax.dynamic_slice_in_dim(rep_atom, col_start, tile_cols),
        ]
    )
    shard_piece = lax.all_gather(atom_coords, ("row", "col", "ch"), axis=1, tiled=True)
    places = lax.iota(jnp.int32, shard_piece.shape[1])
    selector = (places[:, None] == wanted[None, :]).astype(jnp.float32)
    coords = jnp.dot(
        shard_piece, selector, precision=lax.Precision.HIGHEST, preferred_element_type=jnp.float32
    )
    offset = coords[:, :tile_rows, None] - coords[:, None, tile_rows:]
    distance = jnp.sqrt(jnp.sum(offset * offset, axis=0))
    basis_count = w_dist.shape[0]
    radial_basis = distance_basis(distance, basis_count).astype(jnp.bfloat16)
    embedded = jnp.dot(
        radial_basis.reshape(-1, basis_count), w_dist, preferred_element_type=jnp.float32
    ).reshape(tile_rows, tile_cols, pair_width)
    row_single = lax.dynamic_slice_in_dim(single, row_start, tile_rows)
    col_single = lax.dynamic_slice_in_dim(single, col_start, tile_cols)
    from_rows = jnp.dot(row_single, w_left, preferred_element_type=jnp.float32)
    from_cols = jnp.dot(col_single, w_right, preferred_element_type=jnp.float32)
    pair_rep = (
        z_trunk.astype(jnp.float32) + from_rows[:, None, :] + from_cols[None, :, :] + embedded
    )
    mask_float = token_mask.astype(jnp.float32)
    row_mask = lax.dynamic_slice_in_dim(mask_float, row_start, tile_rows)
    col_mask = lax.dynamic_slice_in_dim(mask_float, col_start, tile_cols)
    pair_mask = row_mask[:, None] * col_mask[None, :]
    normed = layer_norm(pair_rep).astype(jnp.bfloat16)
    projected = jnp.dot(
        normed.reshape(-1, pair_width), tri_in, preferred_element_type=jnp.float32
    ).reshape(tile_rows, tile_cols, 5 * pair_width)
    left_side = (
        jax.nn.sigmoid(projected[..., 0:pair_width])
        * projected[..., pair_width : 2 * pair_width]
        * pair_mask[..., None]
    ).astype(jnp.bfloat16)
    right_side = (
        jax.nn.sigmoid(projected[..., 2 * pair_width : 3 * pair_width])
        * projected[..., 3 * pair_width : 4 * pair_width]
        * pair_mask[..., None]
    ).astype(jnp.bfloat16)
    gating = jax.nn.sigmoid(projected[..., 4 * pair_width : 5 * pair_width])
    partial_terms = jnp.einsum(
        "ikc,jkc->ijc",
        left_side,
        lax.all_gather(right_side, "row", axis=0, tiled=True),
        preferred_element_type=jnp.float32,
    )
    product_sum = lax.psum_scatter(partial_terms, ("col", "ch"), scatter_dimension=1, tiled=True)
    normed_outer = layer_norm(product_sum).astype(jnp.bfloat16)
    updated = pair_rep + gating * jnp.dot(
        normed_outer.reshape(-1, pair_width), tri_out, preferred_element_type=jnp.float32
    ).reshape(tile_rows, tile_cols, pair_width)
    bins_pae = pae_w.shape[1]
    pae_logits = jnp.dot(
        updated.astype(jnp.bfloat16).reshape(-1, pair_width),
        pae_w,
        preferred_element_type=jnp.float32,
    ).reshape(tile_rows, tile_cols, bins_pae)
    pae_centers = 0.5 * (jnp.arange(bins_pae, dtype=jnp.float32) + 0.5)
    probability = jax.nn.softmax(pae_logits, axis=-1)
    aligned_error = jnp.sum(probability * pae_centers, axis=-1)
    tm_scale = 1.24 * (max(tokens, 19) - 15) ** (1.0 / 3.0) - 1.8
    tm_values = 1.0 / (1.0 + (pae_centers / tm_scale) ** 2)
    tm_pair = jnp.sum(probability * tm_values, axis=-1)
    row_chain = lax.dynamic_slice_in_dim(chain_id, row_start, tile_rows)
    col_chain = lax.dynamic_slice_in_dim(chain_id, col_start, tile_cols)
    interface = pair_mask * (row_chain[:, None] != col_chain[None, :]).astype(jnp.float32)
    numerator_part = jnp.sum(interface * tm_pair, axis=1)
    count_part = jnp.sum(interface, axis=1)
    pooled_part = jnp.sum(col_mask[None, :, None] * updated, axis=1)
    numerator, count_total, pooled = lax.psum(
        (numerator_part, count_part, pooled_part), ("col", "ch")
    )
    interface_score = numerator / jnp.maximum(count_total, 1.0)
    pooled = pooled / jnp.sum(mask_float)
    single_new = row_single.astype(jnp.float32) + jnp.dot(
        pooled.astype(jnp.bfloat16), pool_w, preferred_element_type=jnp.float32
    )
    single_norm = layer_norm(single_new).astype(jnp.bfloat16)
    bins_plddt = plddt_w.shape[1]
    shard_piece = lax.all_gather(single_norm, "row", axis=0, tiled=True)
    places = lax.iota(jnp.int32, shard_piece.shape[0])
    selector = (atom_token[:, None] == places[None, :]).astype(jnp.bfloat16)
    picked = jnp.dot(selector, shard_piece, preferred_element_type=jnp.float32)
    atom_logits = jnp.dot(picked.astype(jnp.bfloat16), plddt_w, preferred_element_type=jnp.float32)
    atom_logits = atom_logits + jnp.dot(atom_single, atom_w, preferred_element_type=jnp.float32)
    plddt_centers = (jnp.arange(bins_plddt, dtype=jnp.float32) + 0.5) / bins_plddt
    atom_confidence = bin_average(atom_logits, plddt_centers)
    return (aligned_error, interface_score, atom_confidence)


WHOLE_PAIR_BYTES = 4 * 1024 * 1024
SPREAD = 1
SCOPED_BYTES = 16 * 1024 * 1024
VMEM = pl.BlockSpec(memory_space=pltpu.VMEM)


HBM = pl.BlockSpec(memory_space=pltpu.HBM)


def run(kernel, name, out_shapes, arguments, held=None, scratch=(), aliases=None):
    held = len(arguments) if held is None else held
    spaces = [pltpu.VMEM] * held + [pltpu.HBM] * (len(arguments) - held)
    return pl.pallas_call(
        kernel,
        out_shape=out_shapes,
        in_specs=[VMEM] * held + [HBM] * (len(arguments) - held),
        out_specs=(VMEM,) * len(out_shapes) if isinstance(out_shapes, tuple) else VMEM,
        scratch_shapes=list(scratch),
        input_output_aliases=aliases or {},
        compiler_params=pltpu.CompilerParams(vmem_limit_bytes=SCOPED_BYTES),
        name=name,
    )(*map(pltpu.with_memory_space_constraint, arguments, spaces))


def bring(sources, targets, arrived):
    copies = [
        pltpu.make_async_copy(source, target, arrived.at[place])
        for place, (source, target) in enumerate(zip(sources, targets))
    ]
    for copy in copies:
        copy.start()
    for copy in copies:
        copy.wait()


def sigmoid(values):
    return 0.5 * jnp.tanh(0.5 * values) + 0.5


def gated(gates, values, half_mask):
    return (jnp.tanh(0.5 * gates) + 1.0) * values * half_mask


def place_of():
    row = lax.axis_index("row")
    return lax.div(row, 2), lax.rem(row, 2), lax.axis_index("col")


def token_count(mask_ref):
    return jnp.sum(mask_ref[...].astype(jnp.float32), axis=1, keepdims=True)


def half_mask(limit, row_start, col_start, shape):
    rows, cols, width = shape
    places = lax.broadcasted_iota(jnp.int32, (cols, width), 0) + col_start
    keys = jnp.where(places < limit, 0.5, 0.0)
    return jnp.stack([jnp.where(row_start + i < limit, keys, 0.0) for i in range(rows)])


def spread_keys(target, at_chip, at_col, half, tile):
    rows, cols, _ = tile.shape
    for group in range(cols // rows):
        chip = at_col * (cols // (2 * rows)) + group // 2
        target[at_chip, :, (group % 2) ^ half, chip] = tile[:, group * rows : (group + 1) * rows]


def fetch_kernel(z_ref, coords_ref, out_ref, coords_out_ref, arrived):
    pairs = z_ref.shape[0]
    bring((z_ref, coords_ref), (out_ref.at[0:pairs, :], coords_out_ref), arrived)
    out_ref[pairs:, :] = jnp.zeros_like(out_ref[pairs:, :])


def pack_kernel(packed_ref, mine_ref, other_ref, out_ref):
    del packed_ref
    width = out_ref.shape[1]
    atoms = mine_ref.shape[1]
    first = lax.rem(lax.axis_index("row"), 2) == 0
    mine, other = mine_ref[...], other_ref[...]
    value = jnp.concatenate(
        [jnp.where(first, mine, other), jnp.where(first, other, mine)], axis=1
    )
    high = value.astype(jnp.bfloat16).astype(jnp.float32)
    middle = (value - high).astype(jnp.bfloat16).astype(jnp.float32)
    low = value - high - middle
    stacked = jnp.concatenate([high, middle, low, jnp.zeros((7, 2 * atoms), jnp.float32)], axis=0)
    filler = jnp.zeros((16, width - 2 * atoms), jnp.float32)
    out_ref[out_ref.shape[0] - 16 :, :] = jnp.concatenate([stacked, filler], axis=1).astype(
        jnp.bfloat16
    )


def prepare_kernel(slots, col_count, atoms, copied, *refs):
    raw = refs[1:6]
    sources = refs[6 : 6 + copied]
    rows_ref, cols_ref, dist_ref, atom_part_ref, chosen_ref, turned_ref = refs[
        6 + copied : 12 + copied
    ]
    targets = refs[12 + copied : 12 + 2 * copied]
    w_left_ref, w_right_ref, w_dist_ref, atom_single_ref, atom_w_ref, arrived = refs[
        12 + 2 * copied :
    ]
    landing = (w_left_ref, w_right_ref, w_dist_ref, atom_single_ref, atom_w_ref)
    bring((*raw, *sources), (*landing, *targets), arrived)
    single, rep = targets[0][...], targets[-1][...]
    chip, _, col = place_of()
    order = lax.broadcasted_iota(jnp.int32, chosen_ref.shape[1:], 0)
    for place, (chip_step, col_step) in enumerate(slots):
        device = 2 * (chip ^ chip_step) * col_count + (col ^ col_step)
        number = jnp.where(
            order < atoms, order + device * atoms, order - atoms + (device + col_count) * atoms
        )
        chosen = (number == rep).astype(jnp.float32)
        chosen_ref[place] = chosen.astype(jnp.bfloat16)
        turned_ref[place] = chosen.T.astype(jnp.bfloat16)
    rows_ref[...] = jnp.dot(single, w_left_ref[...], preferred_element_type=jnp.float32)
    cols_ref[...] = jnp.dot(single, w_right_ref[...], preferred_element_type=jnp.float32)
    dist_ref[...] = jnp.zeros_like(dist_ref)
    dist_ref[0 : w_dist_ref.shape[0], :] = w_dist_ref[...].astype(jnp.float32)
    atom_part_ref[...] = lax.dot_general(
        atom_w_ref[...],
        atom_single_ref[...],
        (((1,), (1,)), ((), ())),
        preferred_element_type=jnp.float32,
    )


def edge_kernel(slots, basis_count, *refs):
    packs = refs[: len(slots)]
    rows_ref, cols_ref, dist_ref, chosen_ref, turned_ref, mask_ref, tri_in_ref = refs[
        len(slots) : len(slots) + 7
    ]
    pair_ref, normed_ref, right_ref, distance_ref = refs[len(slots) + 7 :]
    _, tile_rows, _, tile_cols, width = normed_ref.shape
    tokens = rows_ref.shape[0]
    pairs = tile_rows * tile_cols
    chip, half, col = place_of()
    w_dist = dist_ref[...].astype(jnp.bfloat16)
    across = jnp.zeros((16, tokens), jnp.float32)
    picked = jnp.zeros((tokens, 16), jnp.float32)
    for place, pack in enumerate(packs):
        pieces = pack[pairs:, :]
        across = across + jnp.dot(
            pieces, chosen_ref[place], preferred_element_type=jnp.float32
        )
        picked = picked + lax.dot_general(
            turned_ref[place], pieces, (((1,), (1,)), ((), ())), preferred_element_type=jnp.float32
        )
    square = jnp.zeros((tokens, width), jnp.float32)
    for axis in range(3):
        down = picked[:, axis : axis + 1] + picked[:, axis + 3 : axis + 4]
        down = down + picked[:, axis + 6 : axis + 7]
        along = across[axis : axis + 1] + across[axis + 3 : axis + 4] + across[axis + 6 : axis + 7]
        along = jnp.concatenate([along, jnp.zeros((1, width - tokens), jnp.float32)], axis=1)
        gap = down - along
        square = square + gap * gap
    distance = jnp.sqrt(square)
    for chip_step in range(pair_ref.shape[0]):
        first = (2 * (chip ^ chip_step) + half) * tile_rows
        distance_ref[chip_step] = pltpu.roll(distance, lax.rem(width - first, width), 1)
    step_size = 18.0 / (basis_count - 1)
    centers = 3.375 + step_size * lax.broadcasted_iota(jnp.int32, (1, 1, width), 2).astype(
        jnp.float32
    )
    limit = token_count(mask_ref).astype(jnp.int32)
    tile = (tile_rows, tile_cols, width)
    tri_in = tri_in_ref[:, 2 * width : 4 * width]
    for pack, (chip_step, col_step) in zip(packs, slots):
        at_chip = chip ^ chip_step
        at_col = col ^ col_step
        row_start = pl.multiple_of((2 * at_chip + half) * tile_rows, 8)
        col_start = pl.multiple_of(at_col * tile_cols, 8)
        row_slice = pl.ds(row_start, tile_rows)
        col_slice = pl.ds(col_start, tile_cols)
        near = distance_ref[chip_step, col_slice, :]
        spread = jnp.stack(
            [jnp.broadcast_to(near[:, i : i + 1], (tile_cols, width)) for i in range(tile_rows)]
        )
        scaled = (spread - centers) * (1.0 / step_size)
        basis = jnp.exp(-scaled * scaled).astype(jnp.bfloat16)
        pair = (
            pack[0:pairs, :].astype(jnp.float32).reshape(tile)
            + rows_ref[row_slice, :][:, None, :]
            + cols_ref[col_slice, :][None]
        )
        pair = pair.reshape(pairs, width) + jnp.dot(
            basis.reshape(pairs, width), w_dist, preferred_element_type=jnp.float32
        )
        spread_keys(pair_ref, at_chip, at_col, half, pair.reshape(tile))
        normed = layer_norm(pair).astype(jnp.bfloat16)
        normed_ref[at_chip, :, at_col] = normed.reshape(tile)
        projected = jnp.dot(normed, tri_in, preferred_element_type=jnp.float32)
        right = gated(
            projected[:, 0:width].reshape(tile),
            projected[:, width : 2 * width].reshape(tile),
            half_mask(limit, row_start, col_start, tile),
        )
        right_ref[at_chip, :, at_col] = right.astype(jnp.bfloat16)


def over_keys(query, key):
    return lax.dot_general(
        query.astype(jnp.bfloat16),
        key.astype(jnp.bfloat16),
        (((1,), (1,)), ((), ())),
        preferred_element_type=jnp.float32,
    )


def left_kernel(
    normed_ref, right_ref, tri_in_ref, mask_ref, turned_ref, keys_ref, mine_ref, gating_ref, left_ref
):
    chips, tile_rows, col_count, tile_cols, width = normed_ref.shape
    tokens = col_count * tile_cols
    _, half, _ = place_of()
    step = turned_ref.shape[0] // (chips * tile_rows)
    limit = token_count(mask_ref).astype(jnp.int32)
    pairs = tile_rows * tile_cols
    tile = (tile_rows, tile_cols, width)
    tri_in = jnp.concatenate([tri_in_ref[:, 0 : 2 * width], tri_in_ref[:, 4 * width :]], axis=1)
    for at_chip in range(chips):
        for at_col in range(col_count):
            normed = normed_ref[at_chip, :, at_col].reshape(pairs, width)
            projected = jnp.dot(normed, tri_in, preferred_element_type=jnp.float32)
            left_ref[:, at_col * tile_cols : (at_col + 1) * tile_cols, :] = gated(
                projected[:, 0:width].reshape(tile),
                projected[:, width : 2 * width].reshape(tile),
                half_mask(limit, (2 * at_chip + half) * tile_rows, at_col * tile_cols, tile),
            )
            spread_keys(
                gating_ref, at_chip, at_col, half, sigmoid(projected[:, 2 * width :]).reshape(tile)
            )
        for i in range(tile_rows):
            rows = pl.ds((at_chip * tile_rows + i) * step, width)
            turned_ref[rows, :] = left_ref[i].T
            key = right_ref[at_chip, i].reshape(tokens, width).astype(jnp.float32)
            keys_ref[rows, :] = key.T
    for channel in range(width // 2):
        rows = pl.ds(channel, chips * tile_rows, stride=step)
        mine_ref[rows, :] = over_keys(turned_ref[rows, :], keys_ref[rows, :])


def normed_columns(values):
    center = values - jnp.mean(values, axis=0, keepdims=True)
    spread = jnp.mean(center * center, axis=0, keepdims=True)
    return (center * lax.rsqrt(spread + EPSILON)).astype(jnp.bfloat16)


def triangle_kernel(
    left_ref,
    mine_keys_ref,
    mine_ref,
    other_ref,
    pair_ref,
    gating_ref,
    tri_out_ref,
    mask_ref,
    pooled_ref,
    own_ref,
    keys_ref,
    outer_ref,
    updated_ref,
):
    chips, tile_rows, _, _, _, width = pair_ref.shape
    tokens = 2 * chips * tile_rows
    queries = chips * tile_rows
    step = keys_ref.shape[0] // queries
    chip, half, _ = place_of()
    for at_chip in range(chips):
        for i in range(tile_rows):
            key = other_ref[at_chip, i].reshape(tokens, width).astype(jnp.float32)
            keys_ref[pl.ds((at_chip * tile_rows + i) * step, width), :] = key.T
    for channel in range(width):
        rows = pl.ds(channel, queries, stride=step)
        query, other = left_ref[rows, :], keys_ref[rows, :]
        if channel < width // 2:
            outer = jnp.concatenate([mine_ref[rows, :], over_keys(query, other)], axis=1)
        else:
            outer = over_keys(query, jnp.concatenate([mine_keys_ref[rows, :], other], axis=0))
        outer_ref[rows, :] = outer
    place = lax.broadcasted_iota(jnp.int32, (tokens, width), 0)
    key_half = jnp.where(place < queries, half, 1 - half)
    place = jnp.where(place < queries, place, place - queries)
    token = 2 * place - lax.rem(place, tile_rows) + key_half * tile_rows
    real = jnp.where(token < token_count(mask_ref).astype(jnp.int32), 1.0, 0.0)
    tri_out = tri_out_ref[...]
    for at_chip in range(chips):
        change = jnp.dot(
            jnp.concatenate(
                [
                    normed_columns(
                        outer_ref[pl.ds((at_chip * tile_rows + i) * step, width), :]
                    ).T
                    for i in range(tile_rows)
                ],
                axis=0,
            ),
            tri_out,
            preferred_element_type=jnp.float32,
        )
        for i in range(tile_rows):
            gating = gating_ref[at_chip, i].reshape(tokens, width)
            updated = pair_ref[at_chip, i].reshape(tokens, width) + gating * (
                change[i * tokens : (i + 1) * tokens]
            )
            updated_ref[at_chip, i] = updated.reshape(2, chips, tile_rows, width)
            row = at_chip * tile_rows + i
            pooled_ref[row : row + 1, :] = jnp.sum(updated * real, axis=0, keepdims=True)
    own_ref[:, :, half] = updated_ref[chip, :, 0]
    own_ref[:, :, 1 - half] = updated_ref[chip, :, 1]


def score_kernel(
    tm_scale, col_count, own_ref, pae_w_ref, mask_ref, chain_ref, aligned_ref, interface_ref
):
    tile_rows, tile_cols = aligned_ref.shape
    tokens = chain_ref.shape[1]
    chip, half, col = place_of()
    bins = pae_w_ref.shape[0]
    logits = lax.dot_general(
        pae_w_ref[...],
        own_ref[...].reshape(tile_rows * tokens, own_ref.shape[-1]).astype(jnp.bfloat16),
        (((1,), (1,)), ((), ())),
        preferred_element_type=jnp.float32,
    )
    centers = 0.5 * (lax.broadcasted_iota(jnp.int32, (bins, 1), 0).astype(jnp.float32) + 0.5)
    ratio = centers / tm_scale
    weight = jnp.exp(logits - jnp.max(logits, axis=0, keepdims=True))
    total = jnp.sum(weight, axis=0, keepdims=True)
    error = jnp.sum(weight * centers, axis=0, keepdims=True) / total
    tm_pair = jnp.sum(weight * (1.0 / (1.0 + ratio * ratio)), axis=0, keepdims=True) / total
    chains = chain_ref[...]
    keys = lax.broadcasted_iota(jnp.int32, (1, tokens), 1)
    limit = token_count(mask_ref).astype(jnp.int32)
    places = lax.broadcasted_iota(jnp.int32, (1, tile_rows), 1)
    scores = jnp.zeros((1, tile_rows), jnp.float32)
    query = (2 * chip + half) * tile_rows
    for i in range(tile_rows):
        span = error[:, i * tokens : (i + 1) * tokens]
        mine = span[:, 0:tile_cols]
        for other in range(1, col_count):
            mine = jnp.where(
                col == other, span[:, other * tile_cols : (other + 1) * tile_cols], mine
            )
        aligned_ref[i : i + 1, :] = mine
        own_chain = jnp.sum(
            jnp.where(keys == query + i, chains, 0).astype(jnp.float32), axis=1, keepdims=True
        ).astype(jnp.int32)
        face = (keys < limit) & (query + i < limit) & (chains != own_chain)
        face = jnp.where(face, 1.0, 0.0)
        number = jnp.sum(face, axis=1, keepdims=True)
        score = jnp.sum(face * tm_pair[:, i * tokens : (i + 1) * tokens], axis=1, keepdims=True)
        scores = jnp.where(places == i, score / jnp.maximum(number, 1.0), scores)
    interface_ref[...] = scores


def atom_kernel(
    mine_ref,
    other_ref,
    single_ref,
    mask_ref,
    pool_w_ref,
    plddt_w_ref,
    atom_token_ref,
    atom_part_ref,
    out_ref,
    pooled_ref,
):
    chips, _, tile_rows, width = pooled_ref.shape
    tokens = single_ref.shape[0]
    half = lax.rem(lax.axis_index("row"), 2)
    pooled_ref[:, half] = mine_ref[...].reshape(chips, tile_rows, width)
    pooled_ref[:, 1 - half] = other_ref[...].reshape(chips, tile_rows, width)
    pooled = pooled_ref[...].reshape(tokens, width) / token_count(mask_ref)
    atoms = atom_token_ref.shape[1]
    order = lax.broadcasted_iota(jnp.int32, (tokens, atoms), 0)
    chosen = (order == atom_token_ref[...]).astype(jnp.float32).astype(jnp.bfloat16)
    turned = (((0,), (0,)), ((), ()))
    pooled = lax.dot_general(
        chosen, pooled.astype(jnp.bfloat16), turned, preferred_element_type=jnp.float32
    )
    picked = lax.dot_general(chosen, single_ref[...], turned, preferred_element_type=jnp.float32)
    picked = layer_norm(
        picked
        + jnp.dot(
            pooled.astype(jnp.bfloat16), pool_w_ref[...], preferred_element_type=jnp.float32
        )
    ).astype(jnp.bfloat16)
    logits = (
        lax.dot_general(
            plddt_w_ref[...], picked, (((1,), (1,)), ((), ())), preferred_element_type=jnp.float32
        )
        + atom_part_ref[...]
    )
    bins = logits.shape[0]
    centers = (lax.broadcasted_iota(jnp.int32, (bins, 1), 0).astype(jnp.float32) + 0.5) / bins
    weight = jnp.exp(logits - jnp.max(logits, axis=0, keepdims=True))
    total = jnp.sum(weight, axis=0, keepdims=True)
    out_ref[...] = jnp.sum(weight * centers, axis=0, keepdims=True) / total


def direct(
    z_trunk,
    single,
    atom_coords,
    atom_single,
    rep_atom,
    atom_token,
    token_mask,
    chain_id,
    w_left,
    w_right,
    w_dist,
    tri_in,
    tri_out,
    pae_w,
    pool_w,
    plddt_w,
    atom_w,
):
    tile_rows, tile_cols, width = z_trunk.shape
    tokens = single.shape[0]
    atoms = atom_coords.shape[1]
    fits = 2 * atoms <= width and tile_cols % (2 * tile_rows) == 0 and tile_rows % 8 == 0
    if tokens * tokens * width * 4 > WHOLE_PAIR_BYTES or not fits:
        return per_device(
            z_trunk, single, atom_coords, atom_single, rep_atom, atom_token, token_mask, chain_id,
            w_left, w_right, w_dist, tri_in, tri_out, pae_w, pool_w, plddt_w, atom_w,
        )
    row_count = lax.axis_size("row")
    col_count = lax.axis_size("col")
    chips = row_count // 2
    float32, bfloat16 = jnp.float32, jnp.bfloat16

    def across(values, axis, count, step):
        return lax.ppermute(values, axis, [(i, i ^ step) for i in range(count)])

    def partner(values):
        return across(values, "row", row_count, 1)

    block = pltpu.VMEM((tile_rows * tile_cols + 16, width), bfloat16)
    fetched, coords = run(
        fetch_kernel,
        "fetch",
        (block, pltpu.VMEM((3, atoms), float32)),
        (z_trunk.reshape(tile_rows * tile_cols, width), atom_coords),
        0,
        scratch=(pltpu.SemaphoreType.DMA((2,)),),
    )
    packed = run(
        pack_kernel, "pack", block, (fetched, coords, partner(atom_coords)), aliases={0: 0}
    )
    slots = [(i, j) for i in range(chips) for j in range(col_count)]
    along = [packed] + [across(packed, "row", row_count, 2 * i) for i in range(1, chips)]
    beside = [packed] + [across(packed, "col", col_count, j) for j in range(1, col_count)]

    def pack_of(i, j):
        if i == 0 or j == 0:
            return beside[j] if i == 0 else along[i]
        if i == 1:
            step = 2 * i * col_count + j
            return across(packed, ("row", "col"), row_count * col_count, step)
        return across(along[i], "col", col_count, j)

    packs = [pack_of(i, j) for i, j in slots]
    raw = (w_left, w_right, w_dist, atom_single, atom_w.T)
    kept = (
        single, tri_in, tri_out, pae_w.T, pool_w, plddt_w.T, token_mask.reshape(1, tokens),
        chain_id.reshape(1, tokens), atom_token.reshape(1, atoms), rep_atom.reshape(1, tokens),
    )
    rows, cols, dist, atom_part, chosen, turned, *kept = run(
        lambda *refs: prepare_kernel(slots, col_count, atoms, len(kept), *refs),
        "prepare",
        (
            pltpu.VMEM((tokens, width), float32),
            pltpu.VMEM((tokens, width), float32),
            pltpu.VMEM((width, width), float32),
            pltpu.VMEM((plddt_w.shape[1], atoms), float32),
            pltpu.VMEM((len(slots), width, tokens), bfloat16),
            pltpu.VMEM((len(slots), tokens, width), bfloat16),
            *[pltpu.VMEM(value.shape, value.dtype) for value in kept],
        ),
        (packed, *raw, *kept),
        1,
        scratch=(
            *[pltpu.VMEM(value.shape, value.dtype) for value in raw],
            pltpu.SemaphoreType.DMA((len(raw) + len(kept),)),
        ),
    )
    single, tri_in, tri_out, pae_w, pool_w, plddt_w, mask, chain, atom_token, _ = kept
    full = (chips, tile_rows, col_count, tile_cols, width)
    by_half = pltpu.VMEM((chips, tile_rows, 2, chips, tile_rows, width), float32)
    pair, normed, right = run(
        lambda *refs: edge_kernel(slots, w_dist.shape[0], *refs),
        "edges",
        (by_half, pltpu.VMEM(full, bfloat16), pltpu.VMEM(full, bfloat16)),
        (*packs, rows, cols, dist, chosen, turned, mask, tri_in),
        scratch=(pltpu.VMEM((chips, tokens, width), float32),),
    )
    turned = pltpu.VMEM((chips * tile_rows * (width + SPREAD), tokens), float32)
    mine = pltpu.VMEM((chips * tile_rows * (width + SPREAD), chips * tile_rows), float32)
    left, keys, mine, gating = run(
        left_kernel,
        "left",
        (turned, turned, mine, by_half),
        (normed, right, tri_in, mask),
        scratch=(pltpu.VMEM((tile_rows, tokens, width), float32),),
    )
    pooled, own = run(
        triangle_kernel,
        "triangle",
        (
            pltpu.VMEM((chips * tile_rows, width), float32),
            pltpu.VMEM((tile_rows, chips, 2, tile_rows, width), float32),
        ),
        (left, keys, mine, partner(right), pair, gating, tri_out, mask),
        scratch=(turned, turned, by_half),
    )
    tm_scale = 1.24 * (max(tokens, 19) - 15) ** (1.0 / 3.0) - 1.8
    aligned_error, interface_score = run(
        lambda *refs: score_kernel(tm_scale, col_count, *refs),
        "scores",
        (
            jax.ShapeDtypeStruct((tile_rows, tile_cols), float32),
            jax.ShapeDtypeStruct((1, tile_rows), float32),
        ),
        (own, pae_w, mask, chain),
    )
    atom_confidence = run(
        atom_kernel,
        "atoms",
        jax.ShapeDtypeStruct((1, atoms), float32),
        (pooled, partner(pooled), single, mask, pool_w, plddt_w, atom_token, atom_part),
        scratch=(pltpu.VMEM((chips, 2, tile_rows, width), float32),),
    )
    return (aligned_error, interface_score.reshape(tile_rows), atom_confidence.reshape(atoms))


def gathers_whole(mesh):
    row_count, col_count = mesh.shape["row"], mesh.shape["col"]
    power = all(count & (count - 1) == 0 for count in (row_count, col_count))
    return power and row_count > 1 and mesh.shape["ch"] == 1


def solution(mesh):
    placed = (
        P(("parts", "row"), ("col", "ch"), None),
        P("parts", None),
        P(None, ("parts", "row", "col", "ch")),
        P(("parts", "row", "col", "ch"), None),
        P("parts"),
        P(("parts", "row", "col", "ch")),
        P("parts"),
        P("parts"),
        P(),
        P(),
        P(),
        P(),
        P(),
        P(),
        P(),
        P(),
        P(),
    )
    return jax.shard_map(
        direct if gathers_whole(mesh) else per_device,
        mesh=mesh,
        in_specs=placed,
        out_specs=(
            P(("parts", "row"), ("col", "ch")),
            P(("parts", "row")),
            P(("parts", "row", "col", "ch")),
        ),
        check_vma=False,
    )
```

```python
import jax
import jax.numpy as jnp
from jax import lax
from jax.experimental import pallas as pl
from jax.experimental.pallas import tpu as pltpu
from jax.sharding import PartitionSpec as P

EPSILON = 1e-05


def layer_norm(values):
    center = values - jnp.mean(values, axis=-1, keepdims=True)
    spread = jnp.mean(center * center, axis=-1, keepdims=True)
    return center * lax.rsqrt(spread + EPSILON)


def distance_basis(distance, count):
    step_size = 18.0 / (count - 1)
    centers = 3.375 + step_size * jnp.arange(count, dtype=jnp.float32)
    scaled = (distance[..., None] - centers) / step_size
    return jnp.exp(-scaled * scaled)


def bin_average(logits, centers):
    probability = jax.nn.softmax(logits, axis=-1)
    return jnp.sum(probability * centers, axis=-1)


def per_device(
    z_trunk,
    single,
    atom_coords,
    atom_single,
    rep_atom,
    atom_token,
    token_mask,
    chain_id,
    w_left,
    w_right,
    w_dist,
    tri_in,
    tri_out,
    pae_w,
    pool_w,
    plddt_w,
    atom_w,
):
    tile_rows, tile_cols, pair_width = z_trunk.shape
    tokens = single.shape[0]
    col_index = lax.axis_index("col") * lax.axis_size("ch") + lax.axis_index("ch")
    row_start = lax.axis_index("row") * tile_rows
    col_start = col_index * tile_cols
    wanted = jnp.concatenate(
        [
            lax.dynamic_slice_in_dim(rep_atom, row_start, tile_rows),
            lax.dynamic_slice_in_dim(rep_atom, col_start, tile_cols),
        ]
    )
    shard_piece = lax.all_gather(atom_coords, ("row", "col", "ch"), axis=1, tiled=True)
    places = lax.iota(jnp.int32, shard_piece.shape[1])
    selector = (places[:, None] == wanted[None, :]).astype(jnp.float32)
    coords = jnp.dot(
        shard_piece, selector, precision=lax.Precision.HIGHEST, preferred_element_type=jnp.float32
    )
    offset = coords[:, :tile_rows, None] - coords[:, None, tile_rows:]
    distance = jnp.sqrt(jnp.sum(offset * offset, axis=0))
    basis_count = w_dist.shape[0]
    radial_basis = distance_basis(distance, basis_count).astype(jnp.bfloat16)
    embedded = jnp.dot(
        radial_basis.reshape(-1, basis_count), w_dist, preferred_element_type=jnp.float32
    ).reshape(tile_rows, tile_cols, pair_width)
    row_single = lax.dynamic_slice_in_dim(single, row_start, tile_rows)
    col_single = lax.dynamic_slice_in_dim(single, col_start, tile_cols)
    from_rows = jnp.dot(row_single, w_left, preferred_element_type=jnp.float32)
    from_cols = jnp.dot(col_single, w_right, preferred_element_type=jnp.float32)
    pair_rep = (
        z_trunk.astype(jnp.float32) + from_rows[:, None, :] + from_cols[None, :, :] + embedded
    )
    mask_float = token_mask.astype(jnp.float32)
    row_mask = lax.dynamic_slice_in_dim(mask_float, row_start, tile_rows)
    col_mask = lax.dynamic_slice_in_dim(mask_float, col_start, tile_cols)
    pair_mask = row_mask[:, None] * col_mask[None, :]
    normed = layer_norm(pair_rep).astype(jnp.bfloat16)
    projected = jnp.dot(
        normed.reshape(-1, pair_width), tri_in, preferred_element_type=jnp.float32
    ).reshape(tile_rows, tile_cols, 5 * pair_width)
    left_side = (
        jax.nn.sigmoid(projected[..., 0:pair_width])
        * projected[..., pair_width : 2 * pair_width]
        * pair_mask[..., None]
    ).astype(jnp.bfloat16)
    right_side = (
        jax.nn.sigmoid(projected[..., 2 * pair_width : 3 * pair_width])
        * projected[..., 3 * pair_width : 4 * pair_width]
        * pair_mask[..., None]
    ).astype(jnp.bfloat16)
    gating = jax.nn.sigmoid(projected[..., 4 * pair_width : 5 * pair_width])
    partial_terms = jnp.einsum(
        "ikc,jkc->ijc",
        left_side,
        lax.all_gather(right_side, "row", axis=0, tiled=True),
        preferred_element_type=jnp.float32,
    )
    product_sum = lax.psum_scatter(partial_terms, ("col", "ch"), scatter_dimension=1, tiled=True)
    normed_outer = layer_norm(product_sum).astype(jnp.bfloat16)
    updated = pair_rep + gating * jnp.dot(
        normed_outer.reshape(-1, pair_width), tri_out, preferred_element_type=jnp.float32
    ).reshape(tile_rows, tile_cols, pair_width)
    bins_pae = pae_w.shape[1]
    pae_logits = jnp.dot(
        updated.astype(jnp.bfloat16).reshape(-1, pair_width),
        pae_w,
        preferred_element_type=jnp.float32,
    ).reshape(tile_rows, tile_cols, bins_pae)
    pae_centers = 0.5 * (jnp.arange(bins_pae, dtype=jnp.float32) + 0.5)
    probability = jax.nn.softmax(pae_logits, axis=-1)
    aligned_error = jnp.sum(probability * pae_centers, axis=-1)
    tm_scale = 1.24 * (max(tokens, 19) - 15) ** (1.0 / 3.0) - 1.8
    tm_values = 1.0 / (1.0 + (pae_centers / tm_scale) ** 2)
    tm_pair = jnp.sum(probability * tm_values, axis=-1)
    row_chain = lax.dynamic_slice_in_dim(chain_id, row_start, tile_rows)
    col_chain = lax.dynamic_slice_in_dim(chain_id, col_start, tile_cols)
    interface = pair_mask * (row_chain[:, None] != col_chain[None, :]).astype(jnp.float32)
    numerator_part = jnp.sum(interface * tm_pair, axis=1)
    count_part = jnp.sum(interface, axis=1)
    pooled_part = jnp.sum(col_mask[None, :, None] * updated, axis=1)
    numerator, count_total, pooled = lax.psum(
        (numerator_part, count_part, pooled_part), ("col", "ch")
    )
    interface_score = numerator / jnp.maximum(count_total, 1.0)
    pooled = pooled / jnp.sum(mask_float)
    single_new = row_single.astype(jnp.float32) + jnp.dot(
        pooled.astype(jnp.bfloat16), pool_w, preferred_element_type=jnp.float32
    )
    single_norm = layer_norm(single_new).astype(jnp.bfloat16)
    bins_plddt = plddt_w.shape[1]
    shard_piece = lax.all_gather(single_norm, "row", axis=0, tiled=True)
    places = lax.iota(jnp.int32, shard_piece.shape[0])
    selector = (atom_token[:, None] == places[None, :]).astype(jnp.bfloat16)
    picked = jnp.dot(selector, shard_piece, preferred_element_type=jnp.float32)
    atom_logits = jnp.dot(picked.astype(jnp.bfloat16), plddt_w, preferred_element_type=jnp.float32)
    atom_logits = atom_logits + jnp.dot(atom_single, atom_w, preferred_element_type=jnp.float32)
    plddt_centers = (jnp.arange(bins_plddt, dtype=jnp.float32) + 0.5) / bins_plddt
    atom_confidence = bin_average(atom_logits, plddt_centers)
    return (aligned_error, interface_score, atom_confidence)


WHOLE_PAIR_BYTES = 4 * 1024 * 1024
SPREAD = 1
GROUP = 4
SCOPED_BYTES = 16 * 1024 * 1024
VMEM = pl.BlockSpec(memory_space=pltpu.VMEM)


HBM = pl.BlockSpec(memory_space=pltpu.HBM)


def run(kernel, name, out_shapes, arguments, held=None, scratch=(), aliases=None):
    held = len(arguments) if held is None else held
    spaces = [pltpu.VMEM] * held + [pltpu.HBM] * (len(arguments) - held)
    return pl.pallas_call(
        kernel,
        out_shape=out_shapes,
        in_specs=[VMEM] * held + [HBM] * (len(arguments) - held),
        out_specs=(VMEM,) * len(out_shapes) if isinstance(out_shapes, tuple) else VMEM,
        scratch_shapes=list(scratch),
        input_output_aliases=aliases or {},
        compiler_params=pltpu.CompilerParams(vmem_limit_bytes=SCOPED_BYTES),
        name=name,
    )(*map(pltpu.with_memory_space_constraint, arguments, spaces))


def bring(sources, targets, arrived):
    copies = [
        pltpu.make_async_copy(source, target, arrived.at[place])
        for place, (source, target) in enumerate(zip(sources, targets))
    ]
    for copy in copies:
        copy.start()
    for copy in copies:
        copy.wait()


def sigmoid(values):
    return 0.5 * jnp.tanh(0.5 * values) + 0.5


def gated(gates, values, half_mask):
    return (jnp.tanh(0.5 * gates) + 1.0) * values * half_mask


def place_of():
    row = lax.axis_index("row")
    return lax.div(row, 2), lax.rem(row, 2), lax.axis_index("col")


def token_count(mask_ref):
    return jnp.sum(mask_ref[...].astype(jnp.float32), axis=1, keepdims=True)


def half_mask(limit, row_start, col_start, shape):
    rows, cols, width = shape
    places = lax.broadcasted_iota(jnp.int32, (cols, width), 0) + col_start
    keys = jnp.where(places < limit, 0.5, 0.0)
    return jnp.stack([jnp.where(row_start + i < limit, keys, 0.0) for i in range(rows)])


def spread_keys(target, at_chip, at_col, half, tile):
    rows, cols, _ = tile.shape
    for group in range(cols // rows):
        chip = at_col * (cols // (2 * rows)) + group // 2
        target[at_chip, :, (group % 2) ^ half, chip] = tile[:, group * rows : (group + 1) * rows]


def fetch_kernel(z_ref, coords_ref, out_ref, coords_out_ref, arrived):
    pairs = z_ref.shape[0]
    bring((z_ref, coords_ref), (out_ref.at[0:pairs, :], coords_out_ref), arrived)
    out_ref[pairs:, :] = jnp.zeros_like(out_ref[pairs:, :])


def pack_kernel(packed_ref, mine_ref, other_ref, out_ref):
    del packed_ref
    width = out_ref.shape[1]
    atoms = mine_ref.shape[1]
    first = lax.rem(lax.axis_index("row"), 2) == 0
    mine, other = mine_ref[...], other_ref[...]
    value = jnp.concatenate(
        [jnp.where(first, mine, other), jnp.where(first, other, mine)], axis=1
    )
    high = value.astype(jnp.bfloat16).astype(jnp.float32)
    middle = (value - high).astype(jnp.bfloat16).astype(jnp.float32)
    low = value - high - middle
    stacked = jnp.concatenate([high, middle, low, jnp.zeros((7, 2 * atoms), jnp.float32)], axis=0)
    filler = jnp.zeros((16, width - 2 * atoms), jnp.float32)
    out_ref[out_ref.shape[0] - 16 :, :] = jnp.concatenate([stacked, filler], axis=1).astype(
        jnp.bfloat16
    )


def prepare_kernel(slots, col_count, atoms, copied, *refs):
    raw = refs[1:6]
    sources = refs[6 : 6 + copied]
    rows_ref, cols_ref, dist_ref, atom_part_ref, chosen_ref, turned_ref = refs[
        6 + copied : 12 + copied
    ]
    targets = refs[12 + copied : 12 + 2 * copied]
    w_left_ref, w_right_ref, w_dist_ref, atom_single_ref, atom_w_ref, arrived = refs[
        12 + 2 * copied :
    ]
    landing = (w_left_ref, w_right_ref, w_dist_ref, atom_single_ref, atom_w_ref)
    bring((*raw, *sources), (*landing, *targets), arrived)
    single, rep = targets[0][...], targets[-1][...]
    chip, _, col = place_of()
    order = lax.broadcasted_iota(jnp.int32, chosen_ref.shape[1:], 0)
    for place, (chip_step, col_step) in enumerate(slots):
        device = 2 * (chip ^ chip_step) * col_count + (col ^ col_step)
        number = jnp.where(
            order < atoms, order + device * atoms, order - atoms + (device + col_count) * atoms
        )
        chosen = (number == rep).astype(jnp.float32)
        chosen_ref[place] = chosen.astype(jnp.bfloat16)
        turned_ref[place] = chosen.T.astype(jnp.bfloat16)
    rows_ref[...] = jnp.dot(single, w_left_ref[...], preferred_element_type=jnp.float32)
    cols_ref[...] = jnp.dot(single, w_right_ref[...], preferred_element_type=jnp.float32)
    dist_ref[...] = jnp.zeros_like(dist_ref)
    dist_ref[0 : w_dist_ref.shape[0], :] = w_dist_ref[...].astype(jnp.float32)
    atom_part_ref[...] = lax.dot_general(
        atom_w_ref[...],
        atom_single_ref[...],
        (((1,), (1,)), ((), ())),
        preferred_element_type=jnp.float32,
    )


def edge_kernel(slots, basis_count, *refs):
    packs = refs[: len(slots)]
    rows_ref, cols_ref, dist_ref, chosen_ref, turned_ref, mask_ref, tri_in_ref = refs[
        len(slots) : len(slots) + 7
    ]
    pair_ref, normed_ref, right_ref, distance_ref = refs[len(slots) + 7 :]
    _, tile_rows, _, tile_cols, width = normed_ref.shape
    tokens = rows_ref.shape[0]
    pairs = tile_rows * tile_cols
    chip, half, col = place_of()
    w_dist = dist_ref[...].astype(jnp.bfloat16)
    across = jnp.zeros((16, tokens), jnp.float32)
    picked = jnp.zeros((tokens, 16), jnp.float32)
    for place, pack in enumerate(packs):
        pieces = pack[pairs:, :]
        across = across + jnp.dot(
            pieces, chosen_ref[place], preferred_element_type=jnp.float32
        )
        picked = picked + lax.dot_general(
            turned_ref[place], pieces, (((1,), (1,)), ((), ())), preferred_element_type=jnp.float32
        )
    square = jnp.zeros((tokens, width), jnp.float32)
    for axis in range(3):
        down = picked[:, axis : axis + 1] + picked[:, axis + 3 : axis + 4]
        down = down + picked[:, axis + 6 : axis + 7]
        along = across[axis : axis + 1] + across[axis + 3 : axis + 4] + across[axis + 6 : axis + 7]
        along = jnp.concatenate([along, jnp.zeros((1, width - tokens), jnp.float32)], axis=1)
        gap = down - along
        square = square + gap * gap
    distance = jnp.sqrt(square)
    for chip_step in range(pair_ref.shape[0]):
        first = (2 * (chip ^ chip_step) + half) * tile_rows
        distance_ref[chip_step] = pltpu.roll(distance, lax.rem(width - first, width), 1)
    step_size = 18.0 / (basis_count - 1)
    centers = 3.375 + step_size * lax.broadcasted_iota(jnp.int32, (1, 1, width), 2).astype(
        jnp.float32
    )
    limit = token_count(mask_ref).astype(jnp.int32)
    tile = (tile_rows, tile_cols, width)
    tri_in = tri_in_ref[:, 2 * width : 4 * width]
    for pack, (chip_step, col_step) in zip(packs, slots):
        at_chip = chip ^ chip_step
        at_col = col ^ col_step
        row_start = pl.multiple_of((2 * at_chip + half) * tile_rows, 8)
        col_start = pl.multiple_of(at_col * tile_cols, 8)
        row_slice = pl.ds(row_start, tile_rows)
        col_slice = pl.ds(col_start, tile_cols)
        near = distance_ref[chip_step, col_slice, :]
        spread = jnp.stack(
            [jnp.broadcast_to(near[:, i : i + 1], (tile_cols, width)) for i in range(tile_rows)]
        )
        scaled = (spread - centers) * (1.0 / step_size)
        basis = jnp.exp(-scaled * scaled).astype(jnp.bfloat16)
        pair = (
            pack[0:pairs, :].astype(jnp.float32).reshape(tile)
            + rows_ref[row_slice, :][:, None, :]
            + cols_ref[col_slice, :][None]
        )
        pair = pair.reshape(pairs, width) + jnp.dot(
            basis.reshape(pairs, width), w_dist, preferred_element_type=jnp.float32
        )
        spread_keys(pair_ref, at_chip, at_col, half, pair.reshape(tile))
        normed = layer_norm(pair).astype(jnp.bfloat16)
        normed_ref[at_chip, :, at_col] = normed.reshape(tile)
        projected = jnp.dot(normed, tri_in, preferred_element_type=jnp.float32)
        right = gated(
            projected[:, 0:width].reshape(tile),
            projected[:, width : 2 * width].reshape(tile),
            half_mask(limit, row_start, col_start, tile),
        )
        right_ref[at_chip, :, at_col] = right.astype(jnp.bfloat16)


def over_keys(query, key):
    return lax.dot_general(
        query.astype(jnp.bfloat16),
        key.astype(jnp.bfloat16),
        (((1,), (1,)), ((), ())),
        preferred_element_type=jnp.float32,
    )


def left_kernel(
    normed_ref, right_ref, tri_in_ref, mask_ref, turned_ref, keys_ref, mine_ref, gating_ref, left_ref
):
    chips, tile_rows, col_count, tile_cols, width = normed_ref.shape
    tokens = col_count * tile_cols
    _, half, _ = place_of()
    step = turned_ref.shape[0] // (chips * tile_rows)
    limit = token_count(mask_ref).astype(jnp.int32)
    pairs = tile_rows * tile_cols
    tile = (tile_rows, tile_cols, width)
    tri_in = jnp.concatenate([tri_in_ref[:, 0 : 2 * width], tri_in_ref[:, 4 * width :]], axis=1)
    for at_chip in range(chips):
        for at_col in range(col_count):
            normed = normed_ref[at_chip, :, at_col].reshape(pairs, width)
            projected = jnp.dot(normed, tri_in, preferred_element_type=jnp.float32)
            left_ref[:, at_col * tile_cols : (at_col + 1) * tile_cols, :] = gated(
                projected[:, 0:width].reshape(tile),
                projected[:, width : 2 * width].reshape(tile),
                half_mask(limit, (2 * at_chip + half) * tile_rows, at_col * tile_cols, tile),
            )
            spread_keys(
                gating_ref, at_chip, at_col, half, sigmoid(projected[:, 2 * width :]).reshape(tile)
            )
        for i in range(tile_rows):
            rows = pl.ds((at_chip * tile_rows + i) * step, width)
            turned_ref[rows, :] = left_ref[i].T
            key = right_ref[at_chip, i].reshape(tokens, width).astype(jnp.float32)
            keys_ref[rows, :] = key.T
    for channel in range(width // 2):
        rows = pl.ds(channel, chips * tile_rows, stride=step)
        mine_ref[rows, :] = over_keys(turned_ref[rows, :], keys_ref[rows, :])


def normed_columns(values):
    center = values - jnp.mean(values, axis=0, keepdims=True)
    spread = jnp.mean(center * center, axis=0, keepdims=True)
    return (center * lax.rsqrt(spread + EPSILON)).astype(jnp.bfloat16)


def triangle_kernel(
    left_ref,
    mine_keys_ref,
    mine_ref,
    other_ref,
    pair_ref,
    gating_ref,
    tri_out_ref,
    mask_ref,
    pooled_ref,
    own_ref,
    keys_ref,
    outer_ref,
    updated_ref,
):
    chips, tile_rows, _, _, _, width = pair_ref.shape
    tokens = 2 * chips * tile_rows
    queries = chips * tile_rows
    step = keys_ref.shape[0] // queries
    chip, half, _ = place_of()
    for at_chip in range(chips):
        for i in range(tile_rows):
            key = other_ref[at_chip, i].reshape(tokens, width).astype(jnp.float32)
            keys_ref[pl.ds((at_chip * tile_rows + i) * step, width), :] = key.T
    for channel in range(width):
        rows = pl.ds(channel, queries, stride=step)
        query, other = left_ref[rows, :], keys_ref[rows, :]
        if channel < width // 2:
            outer = jnp.concatenate([mine_ref[rows, :], over_keys(query, other)], axis=1)
        else:
            outer = over_keys(query, jnp.concatenate([mine_keys_ref[rows, :], other], axis=0))
        outer_ref[rows, :] = outer
    place = lax.broadcasted_iota(jnp.int32, (tokens, width), 0)
    key_half = jnp.where(place < queries, half, 1 - half)
    place = jnp.where(place < queries, place, place - queries)
    token = 2 * place - lax.rem(place, tile_rows) + key_half * tile_rows
    real = jnp.where(token < token_count(mask_ref).astype(jnp.int32), 1.0, 0.0)
    tri_out = tri_out_ref[...]
    for first in range(0, queries, GROUP):
        change = jnp.dot(
            jnp.concatenate(
                [
                    normed_columns(outer_ref[pl.ds(row * step, width), :]).T
                    for row in range(first, first + GROUP)
                ],
                axis=0,
            ),
            tri_out,
            preferred_element_type=jnp.float32,
        )
        for i in range(GROUP):
            at_chip, at_row = divmod(first + i, tile_rows)
            gating = gating_ref[at_chip, at_row].reshape(tokens, width)
            updated = pair_ref[at_chip, at_row].reshape(tokens, width) + gating * (
                change[i * tokens : (i + 1) * tokens]
            )
            updated_ref[at_chip, at_row] = updated.reshape(2, chips, tile_rows, width)
            pooled_ref[first + i : first + i + 1, :] = jnp.sum(
                updated * real, axis=0, keepdims=True
            )
    own_ref[:, :, half] = updated_ref[chip, :, 0]
    own_ref[:, :, 1 - half] = updated_ref[chip, :, 1]


def score_kernel(
    tm_scale, col_count, own_ref, pae_w_ref, mask_ref, chain_ref, aligned_ref, interface_ref
):
    tile_rows, tile_cols = aligned_ref.shape
    tokens = chain_ref.shape[1]
    chip, half, col = place_of()
    bins = pae_w_ref.shape[0]
    logits = lax.dot_general(
        pae_w_ref[...],
        own_ref[...].reshape(tile_rows * tokens, own_ref.shape[-1]).astype(jnp.bfloat16),
        (((1,), (1,)), ((), ())),
        preferred_element_type=jnp.float32,
    )
    centers = 0.5 * (lax.broadcasted_iota(jnp.int32, (bins, 1), 0).astype(jnp.float32) + 0.5)
    ratio = centers / tm_scale
    weight = jnp.exp(logits - jnp.max(logits, axis=0, keepdims=True))
    total = jnp.sum(weight, axis=0, keepdims=True)
    error = jnp.sum(weight * centers, axis=0, keepdims=True) / total
    tm_pair = jnp.sum(weight * (1.0 / (1.0 + ratio * ratio)), axis=0, keepdims=True) / total
    chains = chain_ref[...]
    keys = lax.broadcasted_iota(jnp.int32, (1, tokens), 1)
    limit = token_count(mask_ref).astype(jnp.int32)
    places = lax.broadcasted_iota(jnp.int32, (1, tile_rows), 1)
    scores = jnp.zeros((1, tile_rows), jnp.float32)
    query = (2 * chip + half) * tile_rows
    for i in range(tile_rows):
        span = error[:, i * tokens : (i + 1) * tokens]
        mine = span[:, 0:tile_cols]
        for other in range(1, col_count):
            mine = jnp.where(
                col == other, span[:, other * tile_cols : (other + 1) * tile_cols], mine
            )
        aligned_ref[i : i + 1, :] = mine
        own_chain = jnp.sum(
            jnp.where(keys == query + i, chains, 0).astype(jnp.float32), axis=1, keepdims=True
        ).astype(jnp.int32)
        face = (keys < limit) & (query + i < limit) & (chains != own_chain)
        face = jnp.where(face, 1.0, 0.0)
        number = jnp.sum(face, axis=1, keepdims=True)
        score = jnp.sum(face * tm_pair[:, i * tokens : (i + 1) * tokens], axis=1, keepdims=True)
        scores = jnp.where(places == i, score / jnp.maximum(number, 1.0), scores)
    interface_ref[...] = scores


def atom_kernel(
    mine_ref,
    other_ref,
    single_ref,
    mask_ref,
    pool_w_ref,
    plddt_w_ref,
    atom_token_ref,
    atom_part_ref,
    out_ref,
    pooled_ref,
):
    chips, _, tile_rows, width = pooled_ref.shape
    tokens = single_ref.shape[0]
    half = lax.rem(lax.axis_index("row"), 2)
    pooled_ref[:, half] = mine_ref[...].reshape(chips, tile_rows, width)
    pooled_ref[:, 1 - half] = other_ref[...].reshape(chips, tile_rows, width)
    pooled = pooled_ref[...].reshape(tokens, width) / token_count(mask_ref)
    atoms = atom_token_ref.shape[1]
    order = lax.broadcasted_iota(jnp.int32, (tokens, atoms), 0)
    chosen = (order == atom_token_ref[...]).astype(jnp.float32).astype(jnp.bfloat16)
    turned = (((0,), (0,)), ((), ()))
    pooled = lax.dot_general(
        chosen, pooled.astype(jnp.bfloat16), turned, preferred_element_type=jnp.float32
    )
    picked = lax.dot_general(chosen, single_ref[...], turned, preferred_element_type=jnp.float32)
    picked = layer_norm(
        picked
        + jnp.dot(
            pooled.astype(jnp.bfloat16), pool_w_ref[...], preferred_element_type=jnp.float32
        )
    ).astype(jnp.bfloat16)
    logits = (
        lax.dot_general(
            plddt_w_ref[...], picked, (((1,), (1,)), ((), ())), preferred_element_type=jnp.float32
        )
        + atom_part_ref[...]
    )
    bins = logits.shape[0]
    centers = (lax.broadcasted_iota(jnp.int32, (bins, 1), 0).astype(jnp.float32) + 0.5) / bins
    weight = jnp.exp(logits - jnp.max(logits, axis=0, keepdims=True))
    total = jnp.sum(weight, axis=0, keepdims=True)
    out_ref[...] = jnp.sum(weight * centers, axis=0, keepdims=True) / total


def direct(
    z_trunk,
    single,
    atom_coords,
    atom_single,
    rep_atom,
    atom_token,
    token_mask,
    chain_id,
    w_left,
    w_right,
    w_dist,
    tri_in,
    tri_out,
    pae_w,
    pool_w,
    plddt_w,
    atom_w,
):
    tile_rows, tile_cols, width = z_trunk.shape
    tokens = single.shape[0]
    atoms = atom_coords.shape[1]
    fits = 2 * atoms <= width and tile_cols % (2 * tile_rows) == 0 and tile_rows % 8 == 0
    if tokens * tokens * width * 4 > WHOLE_PAIR_BYTES or not fits:
        return per_device(
            z_trunk, single, atom_coords, atom_single, rep_atom, atom_token, token_mask, chain_id,
            w_left, w_right, w_dist, tri_in, tri_out, pae_w, pool_w, plddt_w, atom_w,
        )
    row_count = lax.axis_size("row")
    col_count = lax.axis_size("col")
    chips = row_count // 2
    float32, bfloat16 = jnp.float32, jnp.bfloat16

    def across(values, axis, count, step):
        return lax.ppermute(values, axis, [(i, i ^ step) for i in range(count)])

    def partner(values):
        return across(values, "row", row_count, 1)

    block = pltpu.VMEM((tile_rows * tile_cols + 16, width), bfloat16)
    fetched, coords = run(
        fetch_kernel,
        "fetch",
        (block, pltpu.VMEM((3, atoms), float32)),
        (z_trunk.reshape(tile_rows * tile_cols, width), atom_coords),
        0,
        scratch=(pltpu.SemaphoreType.DMA((2,)),),
    )
    packed = run(
        pack_kernel, "pack", block, (fetched, coords, partner(atom_coords)), aliases={0: 0}
    )
    slots = [(i, j) for i in range(chips) for j in range(col_count)]
    along = [packed] + [across(packed, "row", row_count, 2 * i) for i in range(1, chips)]
    beside = [packed] + [across(packed, "col", col_count, j) for j in range(1, col_count)]

    def pack_of(i, j):
        if i == 0 or j == 0:
            return beside[j] if i == 0 else along[i]
        if i == 1:
            step = 2 * i * col_count + j
            return across(packed, ("row", "col"), row_count * col_count, step)
        return across(along[i], "col", col_count, j)

    packs = [pack_of(i, j) for i, j in slots]
    raw = (w_left, w_right, w_dist, atom_single, atom_w.T)
    kept = (
        single, tri_in, tri_out, pae_w.T, pool_w, plddt_w.T, token_mask.reshape(1, tokens),
        chain_id.reshape(1, tokens), atom_token.reshape(1, atoms), rep_atom.reshape(1, tokens),
    )
    rows, cols, dist, atom_part, chosen, turned, *kept = run(
        lambda *refs: prepare_kernel(slots, col_count, atoms, len(kept), *refs),
        "prepare",
        (
            pltpu.VMEM((tokens, width), float32),
            pltpu.VMEM((tokens, width), float32),
            pltpu.VMEM((width, width), float32),
            pltpu.VMEM((plddt_w.shape[1], atoms), float32),
            pltpu.VMEM((len(slots), width, tokens), bfloat16),
            pltpu.VMEM((len(slots), tokens, width), bfloat16),
            *[pltpu.VMEM(value.shape, value.dtype) for value in kept],
        ),
        (packed, *raw, *kept),
        1,
        scratch=(
            *[pltpu.VMEM(value.shape, value.dtype) for value in raw],
            pltpu.SemaphoreType.DMA((len(raw) + len(kept),)),
        ),
    )
    single, tri_in, tri_out, pae_w, pool_w, plddt_w, mask, chain, atom_token, _ = kept
    full = (chips, tile_rows, col_count, tile_cols, width)
    by_half = pltpu.VMEM((chips, tile_rows, 2, chips, tile_rows, width), float32)
    pair, normed, right = run(
        lambda *refs: edge_kernel(slots, w_dist.shape[0], *refs),
        "edges",
        (by_half, pltpu.VMEM(full, bfloat16), pltpu.VMEM(full, bfloat16)),
        (*packs, rows, cols, dist, chosen, turned, mask, tri_in),
        scratch=(pltpu.VMEM((chips, tokens, width), float32),),
    )
    turned = pltpu.VMEM((chips * tile_rows * (width + SPREAD), tokens), float32)
    mine = pltpu.VMEM((chips * tile_rows * (width + SPREAD), chips * tile_rows), float32)
    left, keys, mine, gating = run(
        left_kernel,
        "left",
        (turned, turned, mine, by_half),
        (normed, right, tri_in, mask),
        scratch=(pltpu.VMEM((tile_rows, tokens, width), float32),),
    )
    pooled, own = run(
        triangle_kernel,
        "triangle",
        (
            pltpu.VMEM((chips * tile_rows, width), float32),
            pltpu.VMEM((tile_rows, chips, 2, tile_rows, width), float32),
        ),
        (left, keys, mine, partner(right), pair, gating, tri_out, mask),
        scratch=(turned, turned, by_half),
    )
    tm_scale = 1.24 * (max(tokens, 19) - 15) ** (1.0 / 3.0) - 1.8
    aligned_error, interface_score = run(
        lambda *refs: score_kernel(tm_scale, col_count, *refs),
        "scores",
        (
            jax.ShapeDtypeStruct((tile_rows, tile_cols), float32),
            jax.ShapeDtypeStruct((1, tile_rows), float32),
        ),
        (own, pae_w, mask, chain),
    )
    atom_confidence = run(
        atom_kernel,
        "atoms",
        jax.ShapeDtypeStruct((1, atoms), float32),
        (pooled, partner(pooled), single, mask, pool_w, plddt_w, atom_token, atom_part),
        scratch=(pltpu.VMEM((chips, 2, tile_rows, width), float32),),
    )
    return (aligned_error, interface_score.reshape(tile_rows), atom_confidence.reshape(atoms))


def gathers_whole(mesh):
    row_count, col_count = mesh.shape["row"], mesh.shape["col"]
    power = all(count & (count - 1) == 0 for count in (row_count, col_count))
    return power and row_count > 1 and mesh.shape["ch"] == 1


def solution(mesh):
    placed = (
        P(("parts", "row"), ("col", "ch"), None),
        P("parts", None),
        P(None, ("parts", "row", "col", "ch")),
        P(("parts", "row", "col", "ch"), None),
        P("parts"),
        P(("parts", "row", "col", "ch")),
        P("parts"),
        P("parts"),
        P(),
        P(),
        P(),
        P(),
        P(),
        P(),
        P(),
        P(),
        P(),
    )
    return jax.shard_map(
        direct if gathers_whole(mesh) else per_device,
        mesh=mesh,
        in_specs=placed,
        out_specs=(
            P(("parts", "row"), ("col", "ch")),
            P(("parts", "row")),
            P(("parts", "row", "col", "ch")),
        ),
        check_vma=False,
    )
```
